512 devices in a mesh: fsdp: 32 (over x, z_hi, core), ctx: 16 (over y, z_lo).
Axes of the slice: x: 4, y: 4, z: 16 (z_hi: 4, z_lo: 4; z = z_hi * 4 + z_lo), core: 2. Of those that a mesh axis runs over, the one named last changes fastest.
Arguments:
- features: bfloat16 [3, 16384, 8192], P(None, 'ctx', 'fsdp'), may hold values from -6 to 6
- short_taps: float32 [3, 3, 8192], P(None, None, 'fsdp'), may hold values from -3.5 to 3.5
- decay_rates: float32 [512, 16], P('fsdp'), may hold values from 1.5258789e-05 to 0.1
- mode_gains: float32 [512, 16], P('fsdp'), may hold values from -2.5 to 2.5
- cotangent: bfloat16 [16384, 8192], P('ctx', 'fsdp'), may hold values from -6 to 6
Outputs:
- mixer_output: bfloat16 [16384, 8192], P('ctx', 'fsdp')
- feature_grads: bfloat16 [3, 16384, 8192], P(None, 'ctx', 'fsdp')
- gain_grads: float32 [512, 16], P('fsdp')
- rate_grads: float32 [512, 16], P('fsdp')
The draws below stay inside these ranges and needn't reach their ends.
All inputs are finite; a program needn't handle non-finite values.
Results may differ from the reference program's by a relative error of at most 0.0048.
Values may be sent and summed in bfloat16 or wider, within the bound.
A program may use at most 64 MiB of HBM per device.

```python
import jax
import jax.numpy as jnp
from jax import lax

D = 8192
GROUP = 16
ORDER = 16
SHORT = 3
SEQ = 16384
GROUPS = 512


def draw_decay_rates(key, part):
    base = jax.random.fold_in(key, 11)
    choose_key, slow_key, other_key = jax.random.split(base, 3)
    slow_share = 0.5
    lowest = 0.25 / SEQ
    slow_top = 2.0 / SEQ
    slow_pick = jax.random.uniform(choose_key, (GROUPS, ORDER), jnp.float32) < slow_share
    slow_log = jax.random.uniform(slow_key, (GROUPS, ORDER), jnp.float32, jnp.log(lowest), jnp.log(slow_top))
    other_log = jax.random.uniform(other_key, (GROUPS, ORDER), jnp.float32, jnp.log(slow_top), jnp.log(0.1))
    rates = jnp.exp(jnp.where(slow_pick, slow_log, other_log))
    return jnp.clip(rates, lowest, 0.1).astype(jnp.float32)


def levels(key, shape, shards, least, largest):
    def one(axis_at, blocks):
        heights = jax.random.uniform(jax.random.fold_in(jax.random.fold_in(key, 6), axis_at), (blocks,), jnp.float32, least / len(shards), largest / len(shards))
        return jnp.repeat(jnp.exp(heights), shape[axis_at] // blocks).reshape((-1,) + (1,) * (len(shape) - axis_at - 1))

    loudness = one(*shards[0])
    for cut in shards[1:]:
        loudness = loudness * one(*cut)
    return loudness


def noise(own_key, shape, scale, limit, cuts=(), kind=jnp.bfloat16):
    entries = jax.random.normal(own_key, shape, jnp.float32) * scale
    if len(cuts) > 0:
        entries = levels(own_key, shape, cuts, -0.22, 0.18) * entries
    return jnp.clip(entries, min=-limit, max=limit).astype(kind)


def setup_inputs(seed: int = 0) -> dict:
    streams_of = jax.random.split(jax.random.key(seed), 6)
    features = noise(streams_of[0], (3, SEQ, D), 1.0, 6.0, ((1, 16), (2, 32)))
    short_taps = noise(streams_of[1], (3, SHORT, D), SHORT ** -0.5, 3.5, ((2, 32),), jnp.float32)
    decay_rates = draw_decay_rates(jax.random.fold_in(streams_of[5], 71), 0)
    mode_gains = noise(streams_of[3], (GROUPS, ORDER), 0.5, 2.5, ((0, 32),), jnp.float32)
    cotangent = noise(streams_of[4], (SEQ, D), 1.0, 6.0, ((0, 16), (1, 32)))
    return dict(features=features, short_taps=short_taps, decay_rates=decay_rates, mode_gains=mode_gains, cotangent=cotangent)


def spread(gn_table):
    return jnp.repeat(gn_table.T, GROUP, axis=1)

def reference(features, short_taps, decay_rates, mode_gains, cotangent):
    seq_len = features.shape[1]
    total_width = features.shape[2]
    slab_width = min(total_width, 32 * GROUP)
    slab_count = total_width // slab_width
    slab_groups = slab_width // GROUP
    rim_rows = SHORT - 1

    def slab_pass(slab_index):
        slab_start = (slab_index * slab_width).astype(jnp.int32)
        group_start = (slab_index * slab_groups).astype(jnp.int32)
        feature_slab = lax.dynamic_slice_in_dim(features, slab_start, slab_width, 2)
        taps_slab = lax.dynamic_slice_in_dim(short_taps, slab_start, slab_width, 2)
        rate_slab = lax.dynamic_slice_in_dim(decay_rates, group_start, slab_groups, 0)
        gain_slab = lax.dynamic_slice_in_dim(mode_gains, group_start, slab_groups, 0)
        upstream = lax.dynamic_slice_in_dim(cotangent, slab_start, slab_width, 1)
        padded = jnp.pad(feature_slab, ((0, 0), (rim_rows, 0), (0, 0)))
        shaped = jnp.zeros((3, seq_len, slab_width), jnp.float32)
        for offset in range(SHORT):
            shaped = shaped + taps_slab[:, offset, None, :] * padded[:, rim_rows - offset:rim_rows - offset + seq_len, :]
        product = lax.optimization_barrier((shaped[1] * shaped[2]).astype(jnp.bfloat16)).astype(jnp.float32)
        adjoint = upstream * shaped[0]
        mode_coefs = gain_slab * jnp.sqrt(2.0 * rate_slab)
        decay_cols = spread(jnp.exp(-rate_slab))
        weight_cols = spread(mode_coefs)
        zero_state = jnp.zeros((ORDER, slab_width), jnp.float32)

        def forward_step(carried_in, inputs):
            mode_state, lagged, first_acc, lag_acc = carried_in
            z_row, e_row = inputs
            lagged = decay_cols * (lagged - mode_state)
            mode_state = decay_cols * mode_state + z_row[None, :]
            first_acc = first_acc + e_row[None, :] * mode_state
            lag_acc = lag_acc + e_row[None, :] * lagged
            return ((mode_state, lagged, first_acc, lag_acc), lax.optimization_barrier(jnp.sum(weight_cols * mode_state, axis=0)))
        final_carry, inner_sum = lax.scan(forward_step, (zero_state, zero_state, zero_state, zero_state), (product, adjoint))
        first_acc, lag_acc = (final_carry[2], final_carry[3])

        def backward_step(later_state, e_row):
            mode_state = decay_cols * later_state + e_row[None, :]
            return (mode_state, lax.optimization_barrier(jnp.sum(weight_cols * mode_state, axis=0)))
        first_state, product_grad = lax.scan(backward_step, zero_state, adjoint, reverse=True)
        mixed_slab = (shaped[0] * inner_sum).astype(jnp.bfloat16)
        adjoints = jnp.stack([upstream * inner_sum, product_grad * shaped[2], product_grad * shaped[1]])
        appended = jnp.pad(adjoints, ((0, 0), (0, rim_rows), (0, 0)))
        grad_acc = jnp.zeros((3, seq_len, slab_width), jnp.float32)
        for offset in range(SHORT):
            grad_acc = grad_acc + taps_slab[:, offset, None, :] * appended[:, offset:offset + seq_len, :]
        first_total = first_acc.reshape(ORDER, slab_groups, GROUP).sum(axis=2).T
        lag_total = lag_acc.reshape(ORDER, slab_groups, GROUP).sum(axis=2).T
        gain_part = jnp.sqrt(2.0 * rate_slab) * first_total
        rate_part = mode_coefs * (0.5 * first_total + rate_slab * lag_total)
        return (mixed_slab, grad_acc.astype(jnp.bfloat16), gain_part, rate_part)
    indices = jnp.arange(slab_count, dtype=jnp.int32)
    mixed_slabs, grad_slabs, gain_slabs, rate_slabs = lax.map(slab_pass, indices)
    mixer_output = jnp.moveaxis(mixed_slabs, 0, 1).reshape(seq_len, total_width)
    feature_grads = jnp.moveaxis(grad_slabs, 0, 2).reshape(3, seq_len, total_width)
    gain_raw = gain_slabs.reshape(GROUPS, ORDER)
    rate_raw = rate_slabs.reshape(GROUPS, ORDER)
    mean_square = (jnp.sum(gain_raw * gain_raw) + jnp.sum(rate_raw * rate_raw)) / (2 * GROUPS * ORDER)
    factor = jnp.minimum(1.0, lax.rsqrt(mean_square + 1e-06))
    return (mixer_output, feature_grads, factor * gain_raw, factor * rate_raw)
```

```python
import jax
import jax.numpy as jnp
from jax import lax
from jax.sharding import PartitionSpec as P

precise = lax.Precision.HIGHEST
threepass = lax.Precision.HIGH


def passed_along(value, axis, steps):
    count = lax.axis_size(axis)
    leading, last = (max(0, -steps), min(count, count - steps))
    return lax.ppermute(value, axis, [(source, source + steps) for source in range(leading, last)])


def diagonal_sums(gram_acc):
    group_count, block_len, width_same = gram_acc.shape
    flipped = jnp.flip(gram_acc, axis=2)
    padded = jnp.concatenate([flipped, jnp.zeros_like(flipped)], axis=2)
    flattened = padded.reshape(group_count, 2 * block_len * block_len)[
        :, : block_len * (2 * block_len - 1)
    ]
    sheared = flattened.reshape(group_count, block_len, 2 * block_len - 1)
    return jnp.sum(sheared, axis=1)[:, block_len - 1 :]


def short_conv(taps_table, row_data, tokens, rim_rows, forward):
    summed = jnp.zeros((3, tokens, row_data.shape[2]), jnp.float32)
    for offset in range(taps_table.shape[1]):
        start_row = rim_rows - offset if forward else offset
        summed = (
            summed + taps_table[:, offset, None, :] * row_data[:, start_row : start_row + tokens, :]
        )
    return summed


def per_device(features, short_taps, decay_rates, mode_gains, cotangent):
    tokens = features.shape[1]
    channels = features.shape[2]
    group_count = decay_rates.shape[0]
    order_count = decay_rates.shape[1]
    members = channels // group_count
    rim_rows = short_taps.shape[1] - 1
    block_len = 128
    block_count = tokens // block_len
    ctx_count = lax.axis_size("ctx")
    ctx_index = lax.axis_index("ctx")
    earlier_rows = passed_along(features[:, tokens - rim_rows :, :], "ctx", 1)
    extended = jnp.concatenate([earlier_rows, features], axis=1)
    shaped = short_conv(short_taps, extended, tokens, rim_rows, True)
    query_part, key_part, value_part = (shaped[0], shaped[1], shaped[2])
    product = (key_part * value_part).astype(jnp.bfloat16)
    adjoint = cotangent * query_part
    grouped_z = product.reshape(tokens, group_count, members)
    grouped_e = adjoint.reshape(tokens, group_count, members)
    mode_coefs = mode_gains * jnp.sqrt(2.0 * decay_rates)
    rate_axis = decay_rates[:, :, None]
    positions = jnp.arange(tokens, dtype=jnp.float32)[None, None, :]
    decay_from = jnp.exp(-rate_axis * positions)
    end_tables = jnp.stack([jnp.flip(decay_from, 2), -jnp.flip(positions * decay_from, 2)])
    end_states = jnp.einsum(
        "kgns,sgm->kngm", end_tables, grouped_z.astype(jnp.float32), precision=threepass
    )
    start_state = jnp.einsum("gnt,tgm->ngm", decay_from, grouped_e, precision=precise)
    local_states = jnp.stack([end_states[0], end_states[1], start_state]).reshape(
        3, order_count, channels
    )
    lag_axis = jnp.arange(block_len, dtype=jnp.float32)[None, None, :]
    block_pow = jnp.exp(-rate_axis * lag_axis)
    block_after = block_pow * jnp.exp(-rate_axis)
    block_moments = jnp.stack([block_after, (lag_axis + 1.0) * block_after])
    coef_after = mode_coefs[:, :, None] * block_after
    block_ends = jnp.stack([jnp.flip(block_pow, 2), -jnp.flip(lag_axis * block_pow, 2)])
    coef_tail = mode_coefs[:, :, None] * jnp.flip(block_after, 2)
    block_span = jnp.exp(-decay_rates * block_len).T[:, :, None]
    lag_index = (
        jnp.arange(block_len, dtype=jnp.int32)[:, None]
        - jnp.arange(block_len, dtype=jnp.int32)[None, :]
    )
    lag_value = jnp.maximum(lag_index, 0).astype(jnp.float32)
    pair_pow = jnp.exp(-decay_rates[:, :, None, None] * lag_value[None, None])
    toeplitz = jnp.where(
        lag_index[None] >= 0, jnp.sum(mode_coefs[:, :, None, None] * pair_pow, axis=1), 0.0
    )
    z_blocks = grouped_z.reshape(block_count, block_len, group_count, members)
    e_blocks = grouped_e.reshape(block_count, block_len, group_count, members)

    def forward_block(carried_in, inputs):
        mode_state, lagged, first_acc, lag_acc, gram_acc = carried_in
        z_block, e_block = inputs
        z_wide = z_block.astype(jnp.float32)
        inside_part = jnp.einsum("gts,sgm->tgm", toeplitz, z_wide, precision=threepass)
        carried = jnp.einsum("gnt,ngm->tgm", coef_after, mode_state, precision=precise)
        moments = jnp.einsum("kgnt,tgm->kngm", block_moments, e_block, precision=precise)
        first_acc = first_acc + jnp.sum(moments[0] * mode_state, axis=2)
        lag_acc = lag_acc + jnp.sum(moments[0] * lagged - moments[1] * mode_state, axis=2)
        gram_acc = gram_acc + jnp.einsum("tgm,sgm->gts", e_block, z_wide, precision=precise)
        fresh_part = jnp.einsum("kgns,sgm->kngm", block_ends, z_wide, precision=threepass)
        new_lagged = block_span * lagged - block_len * block_span * mode_state + fresh_part[1]
        new_state = block_span * mode_state + fresh_part[0]
        return ((new_state, new_lagged, first_acc, lag_acc, gram_acc), inside_part + carried)

    zero_state = jnp.zeros((order_count, group_count, members), jnp.float32)
    zero_pairs = jnp.zeros((order_count, group_count), jnp.float32)
    zero_gram = jnp.zeros((group_count, block_len, block_len), jnp.float32)
    final_carry, inner_blocks = lax.scan(
        forward_block,
        (zero_state, zero_state, zero_pairs, zero_pairs, zero_gram),
        (z_blocks, e_blocks),
    )
    first_acc, lag_acc, gram_acc = (final_carry[2], final_carry[3], final_carry[4])
    lag_totals = diagonal_sums(gram_acc)
    first_local = first_acc.T + jnp.sum(lag_totals[:, None, :] * block_pow, axis=2)
    lag_local = lag_acc.T - jnp.sum(lag_totals[:, None, :] * lag_axis * block_pow, axis=2)
    device_after = decay_from * jnp.exp(-rate_axis)
    second_moment = jnp.einsum(
        "gnt,tgm->ngm", (positions + 1.0) * device_after, grouped_e, precision=precise
    )
    partial_rows = jnp.stack([first_local, lag_local]).reshape(-1, channels)
    partial_slot = jnp.zeros((order_count, channels), jnp.float32)
    partial_slot = partial_slot.at[: partial_rows.shape[0]].set(partial_rows)
    local_states = jnp.concatenate(
        [local_states, second_moment.reshape(1, order_count, channels), partial_slot[None]]
    )
    rate_cols = jnp.repeat(decay_rates.T, members, axis=1)
    everyone = lax.all_gather(local_states[None], "ctx", axis=0, tiled=True)
    device_ids = jnp.arange(ctx_count, dtype=jnp.int32)
    ahead_steps = (ctx_index - 1 - device_ids).astype(jnp.float32)[:, None, None]
    behind_steps = (device_ids - ctx_index - 1).astype(jnp.float32)[:, None, None]
    ahead_weight = jnp.where(
        ahead_steps >= 0, jnp.exp(-rate_cols[None] * (tokens * jnp.maximum(ahead_steps, 0.0))), 0.0
    )
    behind_weight = jnp.where(
        behind_steps >= 0,
        jnp.exp(-rate_cols[None] * (tokens * jnp.maximum(behind_steps, 0.0))),
        0.0,
    )
    prev_state = jnp.sum(ahead_weight * everyone[:, 0], axis=0)
    next_state = jnp.sum(behind_weight * everyone[:, 2], axis=0)
    all_ids = device_ids.astype(jnp.float32)
    pair_steps = (all_ids[:, None] - 1.0 - all_ids[None, :])[:, :, None, None]
    pair_weight = jnp.where(
        pair_steps >= 0, jnp.exp(-rate_cols[None, None] * (tokens * jnp.maximum(pair_steps, 0.0))), 0.0
    )
    all_prev = jnp.sum(pair_weight * everyone[None, :, 0], axis=1)
    all_lagged = jnp.sum(
        pair_weight * (everyone[None, :, 1] - tokens * pair_steps * everyone[None, :, 0]), axis=1
    )
    all_first = jnp.exp(-rate_cols)[None] * everyone[:, 2]
    cross_first = jnp.sum(all_first * all_prev, axis=0)
    cross_lag = jnp.sum(all_first * all_lagged - everyone[:, 3] * all_prev, axis=0)
    cross_first = cross_first.reshape(order_count, group_count, members).sum(axis=2).T
    cross_lag = cross_lag.reshape(order_count, group_count, members).sum(axis=2).T
    gathered_parts = everyone[:, 4, : partial_rows.shape[0]].reshape(
        ctx_count, 2, group_count, order_count
    )
    local_totals = jnp.sum(gathered_parts, axis=0)
    first_total = local_totals[0] + cross_first
    lag_total = local_totals[1] + cross_lag

    def backward_block(later_state, e_block):
        inside_part = jnp.einsum("gts,tgm->sgm", toeplitz, e_block, precision=precise)
        carried = jnp.einsum("gns,ngm->sgm", coef_tail, later_state, precision=precise)
        fresh_part = jnp.einsum("gnt,tgm->ngm", block_pow, e_block, precision=precise)
        return (block_span * later_state + fresh_part, inside_part + carried)

    top_state, grad_blocks = lax.scan(backward_block, zero_state, e_blocks, reverse=True)
    prev_grouped = prev_state.reshape(order_count, group_count, members)
    next_grouped = next_state.reshape(order_count, group_count, members)
    inner_sum = inner_blocks.reshape(tokens, group_count, members) + jnp.einsum(
        "gnt,ngm->tgm", mode_coefs[:, :, None] * device_after, prev_grouped, precision=precise
    )
    device_tail = mode_coefs[:, :, None] * jnp.flip(device_after, 2)
    product_grad = grad_blocks.reshape(tokens, group_count, members) + jnp.einsum(
        "gns,ngm->sgm", device_tail, next_grouped, precision=precise
    )
    gain_part = jnp.sqrt(2.0 * decay_rates) * first_total
    rate_part = mode_coefs * (0.5 * first_total + decay_rates * lag_total)
    inner_flat = inner_sum.reshape(tokens, channels)
    mixer_output = (query_part * inner_flat).astype(jnp.bfloat16)
    grad_flat = product_grad.reshape(tokens, channels)
    feature_adj = jnp.stack([cotangent * inner_flat, grad_flat * value_part, grad_flat * key_part])
    later_rows = passed_along(feature_adj[:, :rim_rows, :], "ctx", -1)
    appended = jnp.concatenate([feature_adj, later_rows], axis=1)
    feature_grads = short_conv(short_taps, appended, tokens, rim_rows, False).astype(jnp.bfloat16)
    filter_local = jnp.stack([gain_part, rate_part])
    entry_count = 2 * group_count * order_count * lax.axis_size("fsdp")
    summed = filter_local
    squares = lax.psum(jnp.sum(summed * summed), "fsdp")
    factor = jnp.minimum(1.0, lax.rsqrt(squares / entry_count + 1e-06))
    clipped = summed * factor
    return (mixer_output, feature_grads, clipped[0], clipped[1])


def solution(mesh):
    return jax.shard_map(
        per_device,
        mesh=mesh,
        in_specs=(
            P(None, "ctx", "fsdp"),
            P(None, None, "fsdp"),
            P("fsdp", None),
            P("fsdp", None),
            P("ctx", "fsdp"),
        ),
        out_specs=(P("ctx", "fsdp"), P(None, "ctx", "fsdp"), P("fsdp", None), P("fsdp", None)),
        check_vma=False,
    )
```

```python
import jax
import jax.numpy as jnp
from jax import lax
from jax.experimental import pallas as pl
from jax.experimental.pallas import tpu as pltpu
from jax.sharding import PartitionSpec as P
import functools

MESH = pl.DeviceIdType.MESH

precise = lax.Precision.HIGHEST
threepass = lax.Precision.HIGH


def gather_kernel(axis, count, x_ref, o_ref, held, send_sem, recv_sem):
    me = lax.axis_index(axis)

    def device(peer):
        if axis == "ctx":
            return (lax.axis_index("fsdp"), peer)
        return (peer, lax.axis_index("ctx"))

    barrier = pltpu.get_barrier_semaphore()
    for step in range(1, count):
        pl.semaphore_signal(
            barrier, inc=1, device_id=device(lax.rem(me + step, count)), device_id_type=MESH
        )
    pl.semaphore_wait(barrier, count - 1)
    copies = []
    for step in range(1, count):
        copy = pltpu.make_async_remote_copy(
            src_ref=x_ref,
            dst_ref=held.at[me],
            send_sem=send_sem.at[step - 1],
            recv_sem=recv_sem.at[step - 1],
            device_id=device(lax.rem(me + step, count)),
            device_id_type=MESH,
        )
        copy.start()
        copies.append(copy)
    for copy in copies:
        copy.wait()
    held[me] = x_ref[...]
    o_ref[...] = held[...]


def gather_along(value, axis, collective_id):
    count = lax.axis_size(axis)
    return pl.pallas_call(
        functools.partial(gather_kernel, axis, count),
        out_shape=jax.ShapeDtypeStruct((count,) + value.shape, value.dtype),
        in_specs=[pl.BlockSpec(memory_space=pltpu.VMEM)],
        out_specs=pl.BlockSpec(memory_space=pltpu.VMEM),
        scratch_shapes=[
            pltpu.VMEM((count,) + value.shape, value.dtype),
            pltpu.SemaphoreType.DMA((count - 1,)),
            pltpu.SemaphoreType.DMA((count - 1,)),
        ],
        compiler_params=pltpu.CompilerParams(collective_id=collective_id, has_side_effects=True),
    )(value)


def passed_along(value, axis, steps):
    count = lax.axis_size(axis)
    leading, last = (max(0, -steps), min(count, count - steps))
    return lax.ppermute(value, axis, [(source, source + steps) for source in range(leading, last)])


def diagonal_sums(gram_acc):
    group_count, block_len, width_same = gram_acc.shape
    flipped = jnp.flip(gram_acc, axis=2)
    padded = jnp.concatenate([flipped, jnp.zeros_like(flipped)], axis=2)
    flattened = padded.reshape(group_count, 2 * block_len * block_len)[
        :, : block_len * (2 * block_len - 1)
    ]
    sheared = flattened.reshape(group_count, block_len, 2 * block_len - 1)
    return jnp.sum(sheared, axis=1)[:, block_len - 1 :]


def short_conv(taps_table, row_data, tokens, rim_rows, forward):
    summed = jnp.zeros((3, tokens, row_data.shape[2]), jnp.float32)
    for offset in range(taps_table.shape[1]):
        start_row = rim_rows - offset if forward else offset
        summed = (
            summed + taps_table[:, offset, None, :] * row_data[:, start_row : start_row + tokens, :]
        )
    return summed


def per_device(features, short_taps, decay_rates, mode_gains, cotangent):
    tokens = features.shape[1]
    channels = features.shape[2]
    group_count = decay_rates.shape[0]
    order_count = decay_rates.shape[1]
    members = channels // group_count
    rim_rows = short_taps.shape[1] - 1
    block_len = 128
    block_count = tokens // block_len
    ctx_count = lax.axis_size("ctx")
    ctx_index = lax.axis_index("ctx")
    earlier_rows = passed_along(features[:, tokens - rim_rows :, :], "ctx", 1)
    extended = jnp.concatenate([earlier_rows, features], axis=1)
    shaped = short_conv(short_taps, extended, tokens, rim_rows, True)
    query_part, key_part, value_part = (shaped[0], shaped[1], shaped[2])
    product = (key_part * value_part).astype(jnp.bfloat16)
    adjoint = cotangent * query_part
    grouped_z = product.reshape(tokens, group_count, members)
    grouped_e = adjoint.reshape(tokens, group_count, members)
    mode_coefs = mode_gains * jnp.sqrt(2.0 * decay_rates)
    rate_axis = decay_rates[:, :, None]
    positions = jnp.arange(tokens, dtype=jnp.float32)[None, None, :]
    decay_from = jnp.exp(-rate_axis * positions)
    end_tables = jnp.stack([jnp.flip(decay_from, 2), -jnp.flip(positions * decay_from, 2)])
    end_states = jnp.einsum(
        "kgns,sgm->kngm", end_tables, grouped_z.astype(jnp.float32), precision=threepass
    )
    start_state = jnp.einsum("gnt,tgm->ngm", decay_from, grouped_e, precision=precise)
    local_states = jnp.stack([end_states[0], end_states[1], start_state]).reshape(
        3, order_count, channels
    )
    lag_axis = jnp.arange(block_len, dtype=jnp.float32)[None, None, :]
    block_pow = jnp.exp(-rate_axis * lag_axis)
    block_after = block_pow * jnp.exp(-rate_axis)
    block_moments = jnp.stack([block_after, (lag_axis + 1.0) * block_after])
    coef_after = mode_coefs[:, :, None] * block_after
    block_ends = jnp.stack([jnp.flip(block_pow, 2), -jnp.flip(lag_axis * block_pow, 2)])
    coef_tail = mode_coefs[:, :, None] * jnp.flip(block_after, 2)
    block_span = jnp.exp(-decay_rates * block_len).T[:, :, None]
    lag_index = (
        jnp.arange(block_len, dtype=jnp.int32)[:, None]
        - jnp.arange(block_len, dtype=jnp.int32)[None, :]
    )
    lag_value = jnp.maximum(lag_index, 0).astype(jnp.float32)
    pair_pow = jnp.exp(-decay_rates[:, :, None, None] * lag_value[None, None])
    toeplitz = jnp.where(
        lag_index[None] >= 0, jnp.sum(mode_coefs[:, :, None, None] * pair_pow, axis=1), 0.0
    )
    z_blocks = grouped_z.reshape(block_count, block_len, group_count, members)
    e_blocks = grouped_e.reshape(block_count, block_len, group_count, members)

    def forward_block(carried_in, inputs):
        mode_state, lagged, first_acc, lag_acc, gram_acc = carried_in
        z_block, e_block = inputs
        z_wide = z_block.astype(jnp.float32)
        inside_part = jnp.einsum("gts,sgm->tgm", toeplitz, z_wide, precision=threepass)
        carried = jnp.einsum("gnt,ngm->tgm", coef_after, mode_state, precision=precise)
        moments = jnp.einsum("kgnt,tgm->kngm", block_moments, e_block, precision=precise)
        first_acc = first_acc + jnp.sum(moments[0] * mode_state, axis=2)
        lag_acc = lag_acc + jnp.sum(moments[0] * lagged - moments[1] * mode_state, axis=2)
        gram_acc = gram_acc + jnp.einsum("tgm,sgm->gts", e_block, z_wide, precision=precise)
        fresh_part = jnp.einsum("kgns,sgm->kngm", block_ends, z_wide, precision=threepass)
        new_lagged = block_span * lagged - block_len * block_span * mode_state + fresh_part[1]
        new_state = block_span * mode_state + fresh_part[0]
        return ((new_state, new_lagged, first_acc, lag_acc, gram_acc), inside_part + carried)

    zero_state = jnp.zeros((order_count, group_count, members), jnp.float32)
    zero_pairs = jnp.zeros((order_count, group_count), jnp.float32)
    zero_gram = jnp.zeros((group_count, block_len, block_len), jnp.float32)
    final_carry, inner_blocks = lax.scan(
        forward_block,
        (zero_state, zero_state, zero_pairs, zero_pairs, zero_gram),
        (z_blocks, e_blocks),
    )
    first_acc, lag_acc, gram_acc = (final_carry[2], final_carry[3], final_carry[4])
    lag_totals = diagonal_sums(gram_acc)
    first_local = first_acc.T + jnp.sum(lag_totals[:, None, :] * block_pow, axis=2)
    lag_local = lag_acc.T - jnp.sum(lag_totals[:, None, :] * lag_axis * block_pow, axis=2)
    device_after = decay_from * jnp.exp(-rate_axis)
    second_moment = jnp.einsum(
        "gnt,tgm->ngm", (positions + 1.0) * device_after, grouped_e, precision=precise
    )
    partial_rows = jnp.stack([first_local, lag_local]).reshape(-1, channels)
    partial_slot = jnp.zeros((order_count, channels), jnp.float32)
    partial_slot = partial_slot.at[: partial_rows.shape[0]].set(partial_rows)
    local_states = jnp.concatenate(
        [local_states, second_moment.reshape(1, order_count, channels), partial_slot[None]]
    )
    rate_cols = jnp.repeat(decay_rates.T, members, axis=1)
    everyone = gather_along(local_states, "ctx", 0)
    device_ids = jnp.arange(ctx_count, dtype=jnp.int32)
    ahead_steps = (ctx_index - 1 - device_ids).astype(jnp.float32)[:, None, None]
    behind_steps = (device_ids - ctx_index - 1).astype(jnp.float32)[:, None, None]
    ahead_weight = jnp.where(
        ahead_steps >= 0, jnp.exp(-rate_cols[None] * (tokens * jnp.maximum(ahead_steps, 0.0))), 0.0
    )
    behind_weight = jnp.where(
        behind_steps >= 0,
        jnp.exp(-rate_cols[None] * (tokens * jnp.maximum(behind_steps, 0.0))),
        0.0,
    )
    prev_state = jnp.sum(ahead_weight * everyone[:, 0], axis=0)
    next_state = jnp.sum(behind_weight * everyone[:, 2], axis=0)
    all_ids = device_ids.astype(jnp.float32)
    pair_steps = (all_ids[:, None] - 1.0 - all_ids[None, :])[:, :, None, None]
    pair_weight = jnp.where(
        pair_steps >= 0, jnp.exp(-rate_cols[None, None] * (tokens * jnp.maximum(pair_steps, 0.0))), 0.0
    )
    all_prev = jnp.sum(pair_weight * everyone[None, :, 0], axis=1)
    all_lagged = jnp.sum(
        pair_weight * (everyone[None, :, 1] - tokens * pair_steps * everyone[None, :, 0]), axis=1
    )
    all_first = jnp.exp(-rate_cols)[None] * everyone[:, 2]
    cross_first = jnp.sum(all_first * all_prev, axis=0)
    cross_lag = jnp.sum(all_first * all_lagged - everyone[:, 3] * all_prev, axis=0)
    cross_first = cross_first.reshape(order_count, group_count, members).sum(axis=2).T
    cross_lag = cross_lag.reshape(order_count, group_count, members).sum(axis=2).T
    gathered_parts = everyone[:, 4, : partial_rows.shape[0]].reshape(
        ctx_count, 2, group_count, order_count
    )
    local_totals = jnp.sum(gathered_parts, axis=0)
    first_total = local_totals[0] + cross_first
    lag_total = local_totals[1] + cross_lag

    def backward_block(later_state, e_block):
        inside_part = jnp.einsum("gts,tgm->sgm", toeplitz, e_block, precision=precise)
        carried = jnp.einsum("gns,ngm->sgm", coef_tail, later_state, precision=precise)
        fresh_part = jnp.einsum("gnt,tgm->ngm", block_pow, e_block, precision=precise)
        return (block_span * later_state + fresh_part, inside_part + carried)

    top_state, grad_blocks = lax.scan(backward_block, zero_state, e_blocks, reverse=True)
    prev_grouped = prev_state.reshape(order_count, group_count, members)
    next_grouped = next_state.reshape(order_count, group_count, members)
    inner_sum = inner_blocks.reshape(tokens, group_count, members) + jnp.einsum(
        "gnt,ngm->tgm", mode_coefs[:, :, None] * device_after, prev_grouped, precision=precise
    )
    device_tail = mode_coefs[:, :, None] * jnp.flip(device_after, 2)
    product_grad = grad_blocks.reshape(tokens, group_count, members) + jnp.einsum(
        "gns,ngm->sgm", device_tail, next_grouped, precision=precise
    )
    gain_part = jnp.sqrt(2.0 * decay_rates) * first_total
    rate_part = mode_coefs * (0.5 * first_total + decay_rates * lag_total)
    inner_flat = inner_sum.reshape(tokens, channels)
    mixer_output = (query_part * inner_flat).astype(jnp.bfloat16)
    grad_flat = product_grad.reshape(tokens, channels)
    feature_adj = jnp.stack([cotangent * inner_flat, grad_flat * value_part, grad_flat * key_part])
    later_rows = passed_along(feature_adj[:, :rim_rows, :], "ctx", -1)
    appended = jnp.concatenate([feature_adj, later_rows], axis=1)
    feature_grads = short_conv(short_taps, appended, tokens, rim_rows, False).astype(jnp.bfloat16)
    filter_local = jnp.stack([gain_part, rate_part])
    entry_count = 2 * group_count * order_count * lax.axis_size("fsdp")
    summed = filter_local
    square_tile = jnp.full((8, 128), jnp.sum(summed * summed), jnp.float32)
    squares = jnp.sum(gather_along(square_tile, "fsdp", 1)[:, 0, 0])
    factor = jnp.minimum(1.0, lax.rsqrt(squares / entry_count + 1e-06))
    clipped = summed * factor
    return (mixer_output, feature_grads, clipped[0], clipped[1])


def solution(mesh):
    return jax.shard_map(
        per_device,
        mesh=mesh,
        in_specs=(
            P(None, "ctx", "fsdp"),
            P(None, None, "fsdp"),
            P("fsdp", None),
            P("fsdp", None),
            P("ctx", "fsdp"),
        ),
        out_specs=(P("ctx", "fsdp"), P(None, "ctx", "fsdp"), P("fsdp", None), P("fsdp", None)),
        check_vma=False,
    )
```

```python
import jax
import jax.numpy as jnp
from jax import lax
from jax.experimental import pallas as pl
from jax.experimental.pallas import tpu as pltpu
from jax.sharding import PartitionSpec as P
import functools

MESH = pl.DeviceIdType.MESH

precise = lax.Precision.HIGHEST
threepass = lax.Precision.HIGH


def gather_kernel(axis, count, x_ref, o_ref, held, send_sem, recv_sem):
    me = lax.axis_index(axis)

    def device(peer):
        if axis == "ctx":
            return (lax.axis_index("fsdp"), peer)
        return (peer, lax.axis_index("ctx"))

    barrier = pltpu.get_barrier_semaphore()
    for step in range(1, count):
        pl.semaphore_signal(
            barrier, inc=1, device_id=device(lax.rem(me + step, count)), device_id_type=MESH
        )
    pl.semaphore_wait(barrier, count - 1)
    copies = []
    for step in range(1, count):
        copy = pltpu.make_async_remote_copy(
            src_ref=x_ref,
            dst_ref=held.at[me],
            send_sem=send_sem.at[step - 1],
            recv_sem=recv_sem.at[step - 1],
            device_id=device(lax.rem(me + step, count)),
            device_id_type=MESH,
        )
        copy.start()
        copies.append(copy)
    for copy in copies:
        copy.wait()
    held[me] = x_ref[...]
    o_ref[...] = held[...]


def gather_along(value, axis, collective_id):
    count = lax.axis_size(axis)
    return pl.pallas_call(
        functools.partial(gather_kernel, axis, count),
        out_shape=jax.ShapeDtypeStruct((count,) + value.shape, value.dtype),
        in_specs=[pl.BlockSpec(memory_space=pltpu.VMEM)],
        out_specs=pl.BlockSpec(memory_space=pltpu.VMEM),
        scratch_shapes=[
            pltpu.VMEM((count,) + value.shape, value.dtype),
            pltpu.SemaphoreType.DMA((count - 1,)),
            pltpu.SemaphoreType.DMA((count - 1,)),
        ],
        compiler_params=pltpu.CompilerParams(collective_id=collective_id, has_side_effects=True),
    )(value)


def passed_along(value, axis, steps):
    count = lax.axis_size(axis)
    leading, last = (max(0, -steps), min(count, count - steps))
    return lax.ppermute(value, axis, [(source, source + steps) for source in range(leading, last)])


def diagonal_sums(gram_acc):
    group_count, block_len, width_same = gram_acc.shape
    flipped = jnp.flip(gram_acc, axis=2)
    padded = jnp.concatenate([flipped, jnp.zeros_like(flipped)], axis=2)
    flattened = padded.reshape(group_count, 2 * block_len * block_len)[
        :, : block_len * (2 * block_len - 1)
    ]
    sheared = flattened.reshape(group_count, block_len, 2 * block_len - 1)
    return jnp.sum(sheared, axis=1)[:, block_len - 1 :]


def short_conv(taps_table, row_data, tokens, rim_rows, forward):
    summed = jnp.zeros((3, tokens, row_data.shape[2]), jnp.float32)
    for offset in range(taps_table.shape[1]):
        start_row = rim_rows - offset if forward else offset
        summed = (
            summed + taps_table[:, offset, None, :] * row_data[:, start_row : start_row + tokens, :]
        )
    return summed


def per_device(features, short_taps, decay_rates, mode_gains, cotangent):
    tokens = features.shape[1]
    channels = features.shape[2]
    group_count = decay_rates.shape[0]
    order_count = decay_rates.shape[1]
    members = channels // group_count
    rim_rows = short_taps.shape[1] - 1
    block_len = 128
    block_count = tokens // block_len
    ctx_count = lax.axis_size("ctx")
    ctx_index = lax.axis_index("ctx")
    earlier_rows = passed_along(features[:, tokens - rim_rows :, :], "ctx", 1)
    extended = jnp.concatenate([earlier_rows, features], axis=1)
    shaped = short_conv(short_taps, extended, tokens, rim_rows, True)
    query_part, key_part, value_part = (shaped[0], shaped[1], shaped[2])
    product = (key_part * value_part).astype(jnp.bfloat16)
    adjoint = cotangent * query_part
    grouped_z = product.reshape(tokens, group_count, members)
    grouped_e = adjoint.reshape(tokens, group_count, members)
    mode_coefs = mode_gains * jnp.sqrt(2.0 * decay_rates)
    rate_axis = decay_rates[:, :, None]
    positions = jnp.arange(tokens, dtype=jnp.float32)[None, None, :]
    decay_from = jnp.exp(-rate_axis * positions)
    end_tables = jnp.stack([jnp.flip(decay_from, 2), -jnp.flip(positions * decay_from, 2)])
    end_states = jnp.einsum(
        "kgns,sgm->kngm", end_tables, grouped_z.astype(jnp.float32), precision=threepass
    )
    start_state = jnp.einsum("gnt,tgm->ngm", decay_from, grouped_e, precision=precise)
    local_states = jnp.stack([end_states[0], end_states[1], start_state]).reshape(
        3, order_count, channels
    )
    lag_axis = jnp.arange(block_len, dtype=jnp.float32)[None, None, :]
    block_pow = jnp.exp(-rate_axis * lag_axis)
    block_after = block_pow * jnp.exp(-rate_axis)
    block_moments = jnp.stack([block_after, (lag_axis + 1.0) * block_after])
    coef_after = mode_coefs[:, :, None] * block_after
    block_ends = jnp.stack([jnp.flip(block_pow, 2), -jnp.flip(lag_axis * block_pow, 2)])
    coef_tail = mode_coefs[:, :, None] * jnp.flip(block_after, 2)
    lag_index = (
        jnp.arange(block_len, dtype=jnp.int32)[:, None]
        - jnp.arange(block_len, dtype=jnp.int32)[None, :]
    )
    lag_value = jnp.maximum(lag_index, 0).astype(jnp.float32)
    pair_pow = jnp.exp(-decay_rates[:, :, None, None] * lag_value[None, None])
    toeplitz = jnp.where(
        lag_index[None] >= 0, jnp.sum(mode_coefs[:, :, None, None] * pair_pow, axis=1), 0.0
    )
    z_blocks = grouped_z.reshape(block_count, block_len, group_count, members)
    e_blocks = grouped_e.reshape(block_count, block_len, group_count, members)

    z_wide = z_blocks.astype(jnp.float32)
    block_ids = jnp.arange(block_count, dtype=jnp.float32)
    block_steps = (block_ids[:, None] - 1.0 - block_ids[None, :])[:, :, None, None, None]
    span_weight = jnp.where(
        block_steps >= 0,
        jnp.exp(-decay_rates.T[None, None, :, :, None] * (block_len * jnp.maximum(block_steps, 0.0))),
        0.0,
    )
    inside_fwd = jnp.einsum("gts,bsgm->btgm", toeplitz, z_wide, precision=threepass)
    fresh_fwd = jnp.einsum("kgns,bsgm->kbngm", block_ends, z_wide, precision=threepass)
    start_states = jnp.sum(span_weight * fresh_fwd[0][None], axis=1)
    start_lagged = jnp.sum(
        span_weight * (fresh_fwd[1][None] - block_len * block_steps * fresh_fwd[0][None]), axis=1
    )
    carried_fwd = jnp.einsum("gnt,bngm->btgm", coef_after, start_states, precision=precise)
    inner_blocks = inside_fwd + carried_fwd
    moments = jnp.einsum("kgnt,btgm->kbngm", block_moments, e_blocks, precision=precise)
    first_acc = jnp.sum(moments[0] * start_states, axis=(0, 3))
    lag_acc = jnp.sum(moments[0] * start_lagged - moments[1] * start_states, axis=(0, 3))
    gram_acc = jnp.einsum("btgm,bsgm->gts", e_blocks, z_wide, precision=precise)
    lag_totals = diagonal_sums(gram_acc)
    first_local = first_acc.T + jnp.sum(lag_totals[:, None, :] * block_pow, axis=2)
    lag_local = lag_acc.T - jnp.sum(lag_totals[:, None, :] * lag_axis * block_pow, axis=2)
    device_after = decay_from * jnp.exp(-rate_axis)
    second_moment = jnp.einsum(
        "gnt,tgm->ngm", (positions + 1.0) * device_after, grouped_e, precision=precise
    )
    partial_rows = jnp.stack([first_local, lag_local]).reshape(-1, channels)
    partial_slot = jnp.zeros((order_count, channels), jnp.float32)
    partial_slot = partial_slot.at[: partial_rows.shape[0]].set(partial_rows)
    local_states = jnp.concatenate(
        [local_states, second_moment.reshape(1, order_count, channels), partial_slot[None]]
    )
    rate_cols = jnp.repeat(decay_rates.T, members, axis=1)
    everyone = gather_along(local_states, "ctx", 0)
    device_ids = jnp.arange(ctx_count, dtype=jnp.int32)
    ahead_steps = (ctx_index - 1 - device_ids).astype(jnp.float32)[:, None, None]
    behind_steps = (device_ids - ctx_index - 1).astype(jnp.float32)[:, None, None]
    ahead_weight = jnp.where(
        ahead_steps >= 0, jnp.exp(-rate_cols[None] * (tokens * jnp.maximum(ahead_steps, 0.0))), 0.0
    )
    behind_weight = jnp.where(
        behind_steps >= 0,
        jnp.exp(-rate_cols[None] * (tokens * jnp.maximum(behind_steps, 0.0))),
        0.0,
    )
    prev_state = jnp.sum(ahead_weight * everyone[:, 0], axis=0)
    next_state = jnp.sum(behind_weight * everyone[:, 2], axis=0)
    all_ids = device_ids.astype(jnp.float32)
    pair_steps = (all_ids[:, None] - 1.0 - all_ids[None, :])[:, :, None, None]
    pair_weight = jnp.where(
        pair_steps >= 0, jnp.exp(-rate_cols[None, None] * (tokens * jnp.maximum(pair_steps, 0.0))), 0.0
    )
    all_prev = jnp.sum(pair_weight * everyone[None, :, 0], axis=1)
    all_lagged = jnp.sum(
        pair_weight * (everyone[None, :, 1] - tokens * pair_steps * everyone[None, :, 0]), axis=1
    )
    all_first = jnp.exp(-rate_cols)[None] * everyone[:, 2]
    cross_first = jnp.sum(all_first * all_prev, axis=0)
    cross_lag = jnp.sum(all_first * all_lagged - everyone[:, 3] * all_prev, axis=0)
    cross_first = cross_first.reshape(order_count, group_count, members).sum(axis=2).T
    cross_lag = cross_lag.reshape(order_count, group_count, members).sum(axis=2).T
    gathered_parts = everyone[:, 4, : partial_rows.shape[0]].reshape(
        ctx_count, 2, group_count, order_count
    )
    local_totals = jnp.sum(gathered_parts, axis=0)
    first_total = local_totals[0] + cross_first
    lag_total = local_totals[1] + cross_lag

    inside_bwd = jnp.einsum("gts,btgm->bsgm", toeplitz, e_blocks, precision=precise)
    fresh_bwd = jnp.einsum("gnt,btgm->bngm", block_pow, e_blocks, precision=precise)
    later_states = jnp.sum(jnp.swapaxes(span_weight, 0, 1) * fresh_bwd[None], axis=1)
    carried_bwd = jnp.einsum("gns,bngm->bsgm", coef_tail, later_states, precision=precise)
    grad_blocks = inside_bwd + carried_bwd
    prev_grouped = prev_state.reshape(order_count, group_count, members)
    next_grouped = next_state.reshape(order_count, group_count, members)
    inner_sum = inner_blocks.reshape(tokens, group_count, members) + jnp.einsum(
        "gnt,ngm->tgm", mode_coefs[:, :, None] * device_after, prev_grouped, precision=precise
    )
    device_tail = mode_coefs[:, :, None] * jnp.flip(device_after, 2)
    product_grad = grad_blocks.reshape(tokens, group_count, members) + jnp.einsum(
        "gns,ngm->sgm", device_tail, next_grouped, precision=precise
    )
    gain_part = jnp.sqrt(2.0 * decay_rates) * first_total
    rate_part = mode_coefs * (0.5 * first_total + decay_rates * lag_total)
    inner_flat = inner_sum.reshape(tokens, channels)
    mixer_output = (query_part * inner_flat).astype(jnp.bfloat16)
    grad_flat = product_grad.reshape(tokens, channels)
    feature_adj = jnp.stack([cotangent * inner_flat, grad_flat * value_part, grad_flat * key_part])
    later_rows = passed_along(feature_adj[:, :rim_rows, :], "ctx", -1)
    appended = jnp.concatenate([feature_adj, later_rows], axis=1)
    feature_grads = short_conv(short_taps, appended, tokens, rim_rows, False).astype(jnp.bfloat16)
    filter_local = jnp.stack([gain_part, rate_part])
    entry_count = 2 * group_count * order_count * lax.axis_size("fsdp")
    summed = filter_local
    square_tile = jnp.full((8, 128), jnp.sum(summed * summed), jnp.float32)
    squares = jnp.sum(gather_along(square_tile, "fsdp", 1)[:, 0, 0])
    factor = jnp.minimum(1.0, lax.rsqrt(squares / entry_count + 1e-06))
    clipped = summed * factor
    return (mixer_output, feature_grads, clipped[0], clipped[1])


def solution(mesh):
    return jax.shard_map(
        per_device,
        mesh=mesh,
        in_specs=(
            P(None, "ctx", "fsdp"),
            P(None, None, "fsdp"),
            P("fsdp", None),
            P("fsdp", None),
            P("ctx", "fsdp"),
        ),
        out_specs=(P("ctx", "fsdp"), P(None, "ctx", "fsdp"), P("fsdp", None), P("fsdp", None)),
        check_vma=False,
    )
```

```python
import jax
import jax.numpy as jnp
from jax import lax
from jax.experimental import pallas as pl
from jax.experimental.pallas import tpu as pltpu
from jax.sharding import PartitionSpec as P
import functools

MESH = pl.DeviceIdType.MESH

precise = lax.Precision.HIGHEST
threepass = lax.Precision.HIGH


def gather_kernel(axis, count, x_ref, o_ref, held, send_sem, recv_sem):
    me = lax.axis_index(axis)

    def device(peer):
        if axis == "ctx":
            return (lax.axis_index("fsdp"), peer)
        return (peer, lax.axis_index("ctx"))

    barrier = pltpu.get_barrier_semaphore()
    for step in range(1, count):
        pl.semaphore_signal(
            barrier, inc=1, device_id=device(lax.rem(me + step, count)), device_id_type=MESH
        )
    pl.semaphore_wait(barrier, count - 1)
    copies = []
    for step in range(1, count):
        copy = pltpu.make_async_remote_copy(
            src_ref=x_ref,
            dst_ref=held.at[me],
            send_sem=send_sem.at[step - 1],
            recv_sem=recv_sem.at[step - 1],
            device_id=device(lax.rem(me + step, count)),
            device_id_type=MESH,
        )
        copy.start()
        copies.append(copy)
    for copy in copies:
        copy.wait()
    held[me] = x_ref[...]
    o_ref[...] = held[...]


def gather_along(value, axis, collective_id):
    count = lax.axis_size(axis)
    return pl.pallas_call(
        functools.partial(gather_kernel, axis, count),
        out_shape=jax.ShapeDtypeStruct((count,) + value.shape, value.dtype),
        in_specs=[pl.BlockSpec(memory_space=pltpu.VMEM)],
        out_specs=pl.BlockSpec(memory_space=pltpu.VMEM),
        scratch_shapes=[
            pltpu.VMEM((count,) + value.shape, value.dtype),
            pltpu.SemaphoreType.DMA((count - 1,)),
            pltpu.SemaphoreType.DMA((count - 1,)),
        ],
        compiler_params=pltpu.CompilerParams(collective_id=collective_id, has_side_effects=True),
    )(value)


def passed_along(value, axis, steps):
    count = lax.axis_size(axis)
    leading, last = (max(0, -steps), min(count, count - steps))
    return lax.ppermute(value, axis, [(source, source + steps) for source in range(leading, last)])


def short_conv(taps_table, row_data, tokens, rim_rows, forward):
    summed = jnp.zeros((3, tokens, row_data.shape[2]), jnp.float32)
    for offset in range(taps_table.shape[1]):
        start_row = rim_rows - offset if forward else offset
        summed = (
            summed + taps_table[:, offset, None, :] * row_data[:, start_row : start_row + tokens, :]
        )
    return summed


def per_device(features, short_taps, decay_rates, mode_gains, cotangent):
    tokens = features.shape[1]
    channels = features.shape[2]
    group_count = decay_rates.shape[0]
    order_count = decay_rates.shape[1]
    members = channels // group_count
    rim_rows = short_taps.shape[1] - 1
    block_len = 128
    block_count = tokens // block_len
    ctx_count = lax.axis_size("ctx")
    ctx_index = lax.axis_index("ctx")
    earlier_rows = passed_along(features[:, tokens - rim_rows :, :], "ctx", 1)
    extended = jnp.concatenate([earlier_rows, features], axis=1)
    shaped = short_conv(short_taps, extended, tokens, rim_rows, True)
    query_part, key_part, value_part = (shaped[0], shaped[1], shaped[2])
    product = (key_part * value_part).astype(jnp.bfloat16)
    adjoint = cotangent * query_part
    grouped_z = product.reshape(tokens, group_count, members)
    grouped_e = adjoint.reshape(tokens, group_count, members)
    mode_coefs = mode_gains * jnp.sqrt(2.0 * decay_rates)
    rate_axis = decay_rates[:, :, None]
    lag_axis = jnp.arange(block_len, dtype=jnp.float32)[None, None, :]
    block_pow = jnp.exp(-rate_axis * lag_axis)
    block_after = block_pow * jnp.exp(-rate_axis)
    block_moments = jnp.stack([block_after, (lag_axis + 1.0) * block_after])
    coef_after = mode_coefs[:, :, None] * block_after
    tail_axis = block_len - 1.0 - lag_axis
    tail_pow = jnp.exp(-rate_axis * tail_axis)
    block_ends = jnp.stack([tail_pow, -tail_axis * tail_pow])
    coef_tail = mode_coefs[:, :, None] * jnp.exp(-rate_axis * (tail_axis + 1.0))
    lag_index = (
        jnp.arange(block_len, dtype=jnp.int32)[:, None]
        - jnp.arange(block_len, dtype=jnp.int32)[None, :]
    )
    lag_value = jnp.maximum(lag_index, 0).astype(jnp.float32)
    pair_pow = jnp.exp(-decay_rates[:, :, None, None] * lag_value[None, None])
    toeplitz = jnp.where(
        lag_index[None] >= 0, jnp.sum(mode_coefs[:, :, None, None] * pair_pow, axis=1), 0.0
    )
    z_blocks = grouped_z.reshape(block_count, block_len, group_count, members)
    e_blocks = grouped_e.reshape(block_count, block_len, group_count, members)

    z_wide = z_blocks.astype(jnp.float32)
    block_ids = jnp.arange(block_count, dtype=jnp.float32)
    block_steps = (block_ids[:, None] - 1.0 - block_ids[None, :])[:, :, None, None, None]
    span_weight = jnp.where(
        block_steps >= 0,
        jnp.exp(-decay_rates.T[None, None, :, :, None] * (block_len * jnp.maximum(block_steps, 0.0))),
        0.0,
    )
    inside_fwd = jnp.einsum("gts,bsgm->btgm", toeplitz, z_wide, precision=threepass)
    fresh_fwd = jnp.einsum("kgns,bsgm->kbngm", block_ends, z_wide, precision=threepass)
    start_states = jnp.sum(span_weight * fresh_fwd[0][None], axis=1)
    start_lagged = jnp.sum(
        span_weight * (fresh_fwd[1][None] - block_len * block_steps * fresh_fwd[0][None]), axis=1
    )
    moments = jnp.einsum("kgnt,btgm->kbngm", block_moments, e_blocks, precision=precise)
    first_acc = jnp.sum(moments[0] * start_states, axis=(0, 3))
    lag_acc = jnp.sum(moments[0] * start_lagged - moments[1] * start_states, axis=(0, 3))
    gram_acc = jnp.einsum("btgm,bsgm->gts", e_blocks, z_wide, precision=precise)
    pair_mask = jnp.where(lag_index[None, None] >= 0, pair_pow, 0.0)
    first_in = jnp.sum(pair_mask * gram_acc[:, None], axis=(2, 3))
    lag_in = jnp.sum((pair_mask * lag_value[None, None]) * gram_acc[:, None], axis=(2, 3))
    first_local = first_acc.T + first_in
    lag_local = lag_acc.T - lag_in
    inside_bwd = jnp.einsum("gts,btgm->bsgm", toeplitz, e_blocks, precision=precise)
    fresh_bwd = jnp.einsum("gnt,btgm->bngm", block_pow, e_blocks, precision=precise)
    later_states = jnp.sum(jnp.swapaxes(span_weight, 0, 1) * fresh_bwd[None], axis=1)
    rates_ng = decay_rates.T[None, :, :, None]
    from_first = jnp.exp(-rates_ng * (block_len * block_ids[:, None, None, None]))
    from_last = jnp.exp(-rates_ng * (block_len * (block_count - 1.0 - block_ids[:, None, None, None])))
    end_state = jnp.sum(from_last * fresh_fwd[0], axis=0)
    end_lagged = jnp.sum(
        from_last
        * (fresh_fwd[1] - block_len * (block_count - 1.0 - block_ids[:, None, None, None]) * fresh_fwd[0]),
        axis=0,
    )
    start_state = jnp.sum(from_first * fresh_bwd, axis=0)
    second_moment = jnp.sum(
        from_first * (moments[1] + block_len * block_ids[:, None, None, None] * moments[0]), axis=0
    )
    local_states = jnp.stack([end_state, end_lagged, start_state]).reshape(3, order_count, channels)
    partial_rows = jnp.stack([first_local, lag_local]).reshape(-1, channels)
    partial_slot = jnp.zeros((order_count, channels), jnp.float32)
    partial_slot = partial_slot.at[: partial_rows.shape[0]].set(partial_rows)
    local_states = jnp.concatenate(
        [local_states, second_moment.reshape(1, order_count, channels), partial_slot[None]]
    )
    rate_cols = jnp.repeat(decay_rates.T, members, axis=1)
    everyone = gather_along(local_states, "ctx", 0)
    device_ids = jnp.arange(ctx_count, dtype=jnp.int32)
    ahead_steps = (ctx_index - 1 - device_ids).astype(jnp.float32)[:, None, None]
    behind_steps = (device_ids - ctx_index - 1).astype(jnp.float32)[:, None, None]
    ahead_weight = jnp.where(
        ahead_steps >= 0, jnp.exp(-rate_cols[None] * (tokens * jnp.maximum(ahead_steps, 0.0))), 0.0
    )
    behind_weight = jnp.where(
        behind_steps >= 0,
        jnp.exp(-rate_cols[None] * (tokens * jnp.maximum(behind_steps, 0.0))),
        0.0,
    )
    prev_state = jnp.sum(ahead_weight * everyone[:, 0], axis=0)
    next_state = jnp.sum(behind_weight * everyone[:, 2], axis=0)
    all_ids = device_ids.astype(jnp.float32)
    pair_steps = (all_ids[:, None] - 1.0 - all_ids[None, :])[:, :, None, None]
    pair_weight = jnp.where(
        pair_steps >= 0, jnp.exp(-rate_cols[None, None] * (tokens * jnp.maximum(pair_steps, 0.0))), 0.0
    )
    all_prev = jnp.sum(pair_weight * everyone[None, :, 0], axis=1)
    all_lagged = jnp.sum(
        pair_weight * (everyone[None, :, 1] - tokens * pair_steps * everyone[None, :, 0]), axis=1
    )
    all_first = jnp.exp(-rate_cols)[None] * everyone[:, 2]
    cross_first = jnp.sum(all_first * all_prev, axis=0)
    cross_lag = jnp.sum(all_first * all_lagged - everyone[:, 3] * all_prev, axis=0)
    cross_first = cross_first.reshape(order_count, group_count, members).sum(axis=2).T
    cross_lag = cross_lag.reshape(order_count, group_count, members).sum(axis=2).T
    gathered_parts = everyone[:, 4, : partial_rows.shape[0]].reshape(
        ctx_count, 2, group_count, order_count
    )
    local_totals = jnp.sum(gathered_parts, axis=0)
    first_total = local_totals[0] + cross_first
    lag_total = local_totals[1] + cross_lag

    prev_grouped = prev_state.reshape(order_count, group_count, members)
    next_grouped = next_state.reshape(order_count, group_count, members)
    start_total = start_states + from_first * prev_grouped[None]
    later_total = later_states + from_last * next_grouped[None]
    carried_fwd = jnp.einsum("gnt,bngm->btgm", coef_after, start_total, precision=precise)
    inner_sum = (inside_fwd + carried_fwd).reshape(tokens, group_count, members)
    carried_bwd = jnp.einsum("gns,bngm->bsgm", coef_tail, later_total, precision=precise)
    product_grad = (inside_bwd + carried_bwd).reshape(tokens, group_count, members)
    gain_part = jnp.sqrt(2.0 * decay_rates) * first_total
    rate_part = mode_coefs * (0.5 * first_total + decay_rates * lag_total)
    inner_flat = inner_sum.reshape(tokens, channels)
    mixer_output = (query_part * inner_flat).astype(jnp.bfloat16)
    grad_flat = product_grad.reshape(tokens, channels)
    feature_adj = jnp.stack([cotangent * inner_flat, grad_flat * value_part, grad_flat * key_part])
    later_rows = passed_along(feature_adj[:, :rim_rows, :], "ctx", -1)
    appended = jnp.concatenate([feature_adj, later_rows], axis=1)
    feature_grads = short_conv(short_taps, appended, tokens, rim_rows, False).astype(jnp.bfloat16)
    filter_local = jnp.stack([gain_part, rate_part])
    entry_count = 2 * group_count * order_count * lax.axis_size("fsdp")
    summed = filter_local
    square_tile = jnp.full((8, 128), jnp.sum(summed * summed), jnp.float32)
    squares = jnp.sum(gather_along(square_tile, "fsdp", 1)[:, 0, 0])
    factor = jnp.minimum(1.0, lax.rsqrt(squares / entry_count + 1e-06))
    clipped = summed * factor
    return (mixer_output, feature_grads, clipped[0], clipped[1])


def solution(mesh):
    return jax.shard_map(
        per_device,
        mesh=mesh,
        in_specs=(
            P(None, "ctx", "fsdp"),
            P(None, None, "fsdp"),
            P("fsdp", None),
            P("fsdp", None),
            P("ctx", "fsdp"),
        ),
        out_specs=(P("ctx", "fsdp"), P(None, "ctx", "fsdp"), P("fsdp", None), P("fsdp", None)),
        check_vma=False,
    )
```

```python
import jax
import jax.numpy as jnp
from jax import lax
from jax.experimental import pallas as pl
from jax.experimental.pallas import tpu as pltpu
from jax.sharding import PartitionSpec as P
import functools

MESH = pl.DeviceIdType.MESH

precise = lax.Precision.HIGHEST
threepass = lax.Precision.HIGH


def gather_kernel(axis, count, x_ref, o_ref, held, send_sem, recv_sem):
    me = lax.axis_index(axis)

    def device(peer):
        if axis == "ctx":
            return (lax.axis_index("fsdp"), peer)
        return (peer, lax.axis_index("ctx"))

    barrier = pltpu.get_barrier_semaphore()
    for step in range(1, count):
        pl.semaphore_signal(
            barrier, inc=1, device_id=device(lax.rem(me + step, count)), device_id_type=MESH
        )
    pl.semaphore_wait(barrier, count - 1)
    copies = []
    for step in range(1, count):
        copy = pltpu.make_async_remote_copy(
            src_ref=x_ref,
            dst_ref=held.at[me],
            send_sem=send_sem.at[step - 1],
            recv_sem=recv_sem.at[step - 1],
            device_id=device(lax.rem(me + step, count)),
            device_id_type=MESH,
        )
        copy.start()
        copies.append(copy)
    for copy in copies:
        copy.wait()
    held[me] = x_ref[...]
    o_ref[...] = held[...]


def gather_along(value, axis, collective_id):
    count = lax.axis_size(axis)
    return pl.pallas_call(
        functools.partial(gather_kernel, axis, count),
        out_shape=jax.ShapeDtypeStruct((count,) + value.shape, value.dtype),
        in_specs=[pl.BlockSpec(memory_space=pltpu.VMEM)],
        out_specs=pl.BlockSpec(memory_space=pltpu.VMEM),
        scratch_shapes=[
            pltpu.VMEM((count,) + value.shape, value.dtype),
            pltpu.SemaphoreType.DMA((count - 1,)),
            pltpu.SemaphoreType.DMA((count - 1,)),
        ],
        compiler_params=pltpu.CompilerParams(collective_id=collective_id, has_side_effects=True),
    )(value)


def finish_kernel(
    fsdp_count, ctx_count, tile_ref, rim_ref, tiles_out, rim_out, tiles_held, rim_held,
    send_sem, recv_sem, rim_send_sem, rim_recv_sem,
):
    f_me = lax.axis_index("fsdp")
    c_me = lax.axis_index("ctx")
    left = lax.rem(c_me + ctx_count - 1, ctx_count)
    right = lax.rem(c_me + 1, ctx_count)
    barrier = pltpu.get_barrier_semaphore()
    for step in range(1, fsdp_count):
        peer = (lax.rem(f_me + step, fsdp_count), c_me)
        pl.semaphore_signal(barrier, inc=1, device_id=peer, device_id_type=MESH)
    for side in (left, right):
        pl.semaphore_signal(barrier, inc=1, device_id=(f_me, side), device_id_type=MESH)
    pl.semaphore_wait(barrier, fsdp_count + 1)
    rim_copy = pltpu.make_async_remote_copy(
        src_ref=rim_ref,
        dst_ref=rim_held,
        send_sem=rim_send_sem,
        recv_sem=rim_recv_sem,
        device_id=(f_me, left),
        device_id_type=MESH,
    )
    rim_copy.start()
    copies = []
    for step in range(1, fsdp_count):
        copy = pltpu.make_async_remote_copy(
            src_ref=tile_ref,
            dst_ref=tiles_held.at[f_me],
            send_sem=send_sem.at[step - 1],
            recv_sem=recv_sem.at[step - 1],
            device_id=(lax.rem(f_me + step, fsdp_count), c_me),
            device_id_type=MESH,
        )
        copy.start()
        copies.append(copy)
    for copy in copies:
        copy.wait()
    rim_copy.wait()
    tiles_held[f_me] = tile_ref[...]
    tiles_out[...] = tiles_held[...]
    rim_out[...] = rim_held[...]


def finish_exchange(tile, rim):
    fsdp_count = lax.axis_size("fsdp")
    ctx_count = lax.axis_size("ctx")
    return pl.pallas_call(
        functools.partial(finish_kernel, fsdp_count, ctx_count),
        out_shape=(
            jax.ShapeDtypeStruct((fsdp_count,) + tile.shape, tile.dtype),
            jax.ShapeDtypeStruct(rim.shape, rim.dtype),
        ),
        in_specs=[pl.BlockSpec(memory_space=pltpu.VMEM)] * 2,
        out_specs=(pl.BlockSpec(memory_space=pltpu.VMEM), pl.BlockSpec(memory_space=pltpu.VMEM)),
        scratch_shapes=[
            pltpu.VMEM((fsdp_count,) + tile.shape, tile.dtype),
            pltpu.VMEM(rim.shape, rim.dtype),
            pltpu.SemaphoreType.DMA((fsdp_count - 1,)),
            pltpu.SemaphoreType.DMA((fsdp_count - 1,)),
            pltpu.SemaphoreType.DMA(()),
            pltpu.SemaphoreType.DMA(()),
        ],
        compiler_params=pltpu.CompilerParams(collective_id=1, has_side_effects=True),
    )(tile, rim)


def passed_along(value, axis, steps):
    count = lax.axis_size(axis)
    leading, last = (max(0, -steps), min(count, count - steps))
    return lax.ppermute(value, axis, [(source, source + steps) for source in range(leading, last)])


def short_conv(taps_table, row_data, tokens, rim_rows, forward):
    summed = jnp.zeros((3, tokens, row_data.shape[2]), jnp.float32)
    for offset in range(taps_table.shape[1]):
        start_row = rim_rows - offset if forward else offset
        summed = (
            summed + taps_table[:, offset, None, :] * row_data[:, start_row : start_row + tokens, :]
        )
    return summed


def per_device(features, short_taps, decay_rates, mode_gains, cotangent):
    tokens = features.shape[1]
    channels = features.shape[2]
    group_count = decay_rates.shape[0]
    order_count = decay_rates.shape[1]
    members = channels // group_count
    rim_rows = short_taps.shape[1] - 1
    block_len = 128
    block_count = tokens // block_len
    ctx_count = lax.axis_size("ctx")
    ctx_index = lax.axis_index("ctx")
    earlier_rows = passed_along(features[:, tokens - rim_rows :, :], "ctx", 1)
    extended = jnp.concatenate([earlier_rows, features], axis=1)
    shaped = short_conv(short_taps, extended, tokens, rim_rows, True)
    query_part, key_part, value_part = (shaped[0], shaped[1], shaped[2])
    product = (key_part * value_part).astype(jnp.bfloat16)
    adjoint = cotangent * query_part
    grouped_z = product.reshape(tokens, group_count, members)
    grouped_e = adjoint.reshape(tokens, group_count, members)
    mode_coefs = mode_gains * jnp.sqrt(2.0 * decay_rates)
    rate_axis = decay_rates[:, :, None]
    lag_axis = jnp.arange(block_len, dtype=jnp.float32)[None, None, :]
    block_pow = jnp.exp(-rate_axis * lag_axis)
    block_after = block_pow * jnp.exp(-rate_axis)
    block_moments = jnp.stack([block_after, (lag_axis + 1.0) * block_after])
    coef_after = mode_coefs[:, :, None] * block_after
    tail_axis = block_len - 1.0 - lag_axis
    tail_pow = jnp.exp(-rate_axis * tail_axis)
    block_ends = jnp.stack([tail_pow, -tail_axis * tail_pow])
    coef_tail = mode_coefs[:, :, None] * jnp.exp(-rate_axis * (tail_axis + 1.0))
    lag_index = (
        jnp.arange(block_len, dtype=jnp.int32)[:, None]
        - jnp.arange(block_len, dtype=jnp.int32)[None, :]
    )
    lag_value = jnp.maximum(lag_index, 0).astype(jnp.float32)
    pair_pow = jnp.exp(-decay_rates[:, :, None, None] * lag_value[None, None])
    toeplitz = jnp.where(
        lag_index[None] >= 0, jnp.sum(mode_coefs[:, :, None, None] * pair_pow, axis=1), 0.0
    )
    z_blocks = grouped_z.reshape(block_count, block_len, group_count, members)
    e_blocks = grouped_e.reshape(block_count, block_len, group_count, members)

    z_wide = z_blocks.astype(jnp.float32)
    block_ids = jnp.arange(block_count, dtype=jnp.float32)
    block_steps = (block_ids[:, None] - 1.0 - block_ids[None, :])[:, :, None, None, None]
    span_weight = jnp.where(
        block_steps >= 0,
        jnp.exp(-decay_rates.T[None, None, :, :, None] * (block_len * jnp.maximum(block_steps, 0.0))),
        0.0,
    )
    inside_fwd = jnp.einsum("gts,bsgm->btgm", toeplitz, z_wide, precision=threepass)
    fresh_fwd = jnp.einsum("kgns,bsgm->kbngm", block_ends, z_wide, precision=threepass)
    start_states = jnp.sum(span_weight * fresh_fwd[0][None], axis=1)
    start_lagged = jnp.sum(
        span_weight * (fresh_fwd[1][None] - block_len * block_steps * fresh_fwd[0][None]), axis=1
    )
    moments = jnp.einsum("kgnt,btgm->kbngm", block_moments, e_blocks, precision=precise)
    first_acc = jnp.sum(moments[0] * start_states, axis=(0, 3))
    lag_acc = jnp.sum(moments[0] * start_lagged - moments[1] * start_states, axis=(0, 3))
    gram_acc = jnp.einsum("btgm,bsgm->gts", e_blocks, z_wide, precision=precise)
    gram_low = jnp.where(lag_index[None] >= 0, gram_acc, 0.0)
    gram_pair = jnp.stack([gram_low, gram_low * lag_value[None]])
    rise_pow = jnp.exp(rate_axis * lag_axis)
    gram_rise = jnp.einsum("kgts,gns->kgnt", gram_pair, rise_pow, precision=precise)
    first_in = jnp.sum(block_pow * gram_rise[0], axis=2)
    lag_in = jnp.sum(block_pow * gram_rise[1], axis=2)
    first_local = first_acc.T + first_in
    lag_local = lag_acc.T - lag_in
    inside_bwd = jnp.einsum("gts,btgm->bsgm", toeplitz, e_blocks, precision=precise)
    fresh_bwd = jnp.einsum("gnt,btgm->bngm", block_pow, e_blocks, precision=precise)
    later_states = jnp.sum(jnp.swapaxes(span_weight, 0, 1) * fresh_bwd[None], axis=1)
    rates_ng = decay_rates.T[None, :, :, None]
    from_first = jnp.exp(-rates_ng * (block_len * block_ids[:, None, None, None]))
    from_last = jnp.exp(-rates_ng * (block_len * (block_count - 1.0 - block_ids[:, None, None, None])))
    end_state = jnp.sum(from_last * fresh_fwd[0], axis=0)
    end_lagged = jnp.sum(
        from_last
        * (fresh_fwd[1] - block_len * (block_count - 1.0 - block_ids[:, None, None, None]) * fresh_fwd[0]),
        axis=0,
    )
    start_state = jnp.sum(from_first * fresh_bwd, axis=0)
    second_moment = jnp.sum(
        from_first * (moments[1] + block_len * block_ids[:, None, None, None] * moments[0]), axis=0
    )
    partial_rows = jnp.stack([first_local, lag_local]).reshape(-1, channels)
    state_rows = jnp.stack([end_state, end_lagged, start_state, second_moment]).reshape(
        4 * order_count, channels
    )
    payload_rows = -(-(state_rows.shape[0] + partial_rows.shape[0]) // 8) * 8
    local_states = jnp.zeros((payload_rows, channels), jnp.float32)
    local_states = local_states.at[: state_rows.shape[0]].set(state_rows)
    local_states = local_states.at[state_rows.shape[0] : state_rows.shape[0] + partial_rows.shape[0]].set(
        partial_rows
    )
    rate_cols = jnp.repeat(decay_rates.T, members, axis=1)
    gathered = gather_along(local_states, "ctx", 0)
    everyone = gathered[:, : state_rows.shape[0]].reshape(ctx_count, 4, order_count, channels)
    device_ids = jnp.arange(ctx_count, dtype=jnp.int32)
    ahead_steps = (ctx_index - 1 - device_ids).astype(jnp.float32)[:, None, None]
    behind_steps = (device_ids - ctx_index - 1).astype(jnp.float32)[:, None, None]
    ahead_weight = jnp.where(
        ahead_steps >= 0, jnp.exp(-rate_cols[None] * (tokens * jnp.maximum(ahead_steps, 0.0))), 0.0
    )
    behind_weight = jnp.where(
        behind_steps >= 0,
        jnp.exp(-rate_cols[None] * (tokens * jnp.maximum(behind_steps, 0.0))),
        0.0,
    )
    prev_state = jnp.sum(ahead_weight * everyone[:, 0], axis=0)
    next_state = jnp.sum(behind_weight * everyone[:, 2], axis=0)
    all_ids = device_ids.astype(jnp.float32)
    pair_steps = (all_ids[:, None] - 1.0 - all_ids[None, :])[:, :, None, None]
    pair_weight = jnp.where(
        pair_steps >= 0, jnp.exp(-rate_cols[None, None] * (tokens * jnp.maximum(pair_steps, 0.0))), 0.0
    )
    all_prev = jnp.sum(pair_weight * everyone[None, :, 0], axis=1)
    all_lagged = jnp.sum(
        pair_weight * (everyone[None, :, 1] - tokens * pair_steps * everyone[None, :, 0]), axis=1
    )
    all_first = jnp.exp(-rate_cols)[None] * everyone[:, 2]
    cross_first = jnp.sum(all_first * all_prev, axis=0)
    cross_lag = jnp.sum(all_first * all_lagged - everyone[:, 3] * all_prev, axis=0)
    cross_first = cross_first.reshape(order_count, group_count, members).sum(axis=2).T
    cross_lag = cross_lag.reshape(order_count, group_count, members).sum(axis=2).T
    gathered_parts = gathered[:, state_rows.shape[0] : state_rows.shape[0] + partial_rows.shape[0]].reshape(
        ctx_count, 2, group_count, order_count
    )
    local_totals = jnp.sum(gathered_parts, axis=0)
    first_total = local_totals[0] + cross_first
    lag_total = local_totals[1] + cross_lag

    prev_grouped = prev_state.reshape(order_count, group_count, members)
    next_grouped = next_state.reshape(order_count, group_count, members)
    start_total = start_states + from_first * prev_grouped[None]
    later_total = later_states + from_last * next_grouped[None]
    carried_fwd = jnp.einsum("gnt,bngm->btgm", coef_after, start_total, precision=precise)
    inner_sum = (inside_fwd + carried_fwd).reshape(tokens, group_count, members)
    carried_bwd = jnp.einsum("gns,bngm->bsgm", coef_tail, later_total, precision=precise)
    product_grad = (inside_bwd + carried_bwd).reshape(tokens, group_count, members)
    gain_part = jnp.sqrt(2.0 * decay_rates) * first_total
    rate_part = mode_coefs * (0.5 * first_total + decay_rates * lag_total)
    inner_flat = inner_sum.reshape(tokens, channels)
    mixer_output = (query_part * inner_flat).astype(jnp.bfloat16)
    grad_flat = product_grad.reshape(tokens, channels)
    feature_adj = jnp.stack([cotangent * inner_flat, grad_flat * value_part, grad_flat * key_part])
    filter_local = jnp.stack([gain_part, rate_part])
    entry_count = 2 * group_count * order_count * lax.axis_size("fsdp")
    summed = filter_local
    square_tile = jnp.full((8, 128), jnp.sum(summed * summed), jnp.float32)
    rim_send = feature_adj[:, :rim_rows, :].reshape(3 * rim_rows, channels)
    square_tiles, rim_got = finish_exchange(square_tile, rim_send)
    squares = jnp.sum(square_tiles[:, 0, 0])
    later_rows = jnp.where(ctx_index == ctx_count - 1, 0.0, rim_got).reshape(3, rim_rows, channels)
    appended = jnp.concatenate([feature_adj, later_rows], axis=1)
    feature_grads = short_conv(short_taps, appended, tokens, rim_rows, False).astype(jnp.bfloat16)
    factor = jnp.minimum(1.0, lax.rsqrt(squares / entry_count + 1e-06))
    clipped = summed * factor
    return (mixer_output, feature_grads, clipped[0], clipped[1])


def solution(mesh):
    return jax.shard_map(
        per_device,
        mesh=mesh,
        in_specs=(
            P(None, "ctx", "fsdp"),
            P(None, None, "fsdp"),
            P("fsdp", None),
            P("fsdp", None),
            P("ctx", "fsdp"),
        ),
        out_specs=(P("ctx", "fsdp"), P(None, "ctx", "fsdp"), P("fsdp", None), P("fsdp", None)),
        check_vma=False,
    )
```

```python
import jax
import jax.numpy as jnp
from jax import lax
from jax.experimental import pallas as pl
from jax.experimental.pallas import tpu as pltpu
from jax.sharding import PartitionSpec as P
import functools

MESH = pl.DeviceIdType.MESH

precise = lax.Precision.HIGHEST
threepass = lax.Precision.HIGH


def gather_kernel(axis, count, x_ref, o_ref, held, send_sem, recv_sem):
    me = lax.axis_index(axis)

    def device(peer):
        if axis == "ctx":
            return (lax.axis_index("fsdp"), peer)
        return (peer, lax.axis_index("ctx"))

    barrier = pltpu.get_barrier_semaphore()
    for step in range(1, count):
        pl.semaphore_signal(
            barrier, inc=1, device_id=device(lax.rem(me + step, count)), device_id_type=MESH
        )
    pl.semaphore_wait(barrier, count - 1)
    copies = []
    for step in range(1, count):
        copy = pltpu.make_async_remote_copy(
            src_ref=x_ref,
            dst_ref=held.at[me],
            send_sem=send_sem.at[step - 1],
            recv_sem=recv_sem.at[step - 1],
            device_id=device(lax.rem(me + step, count)),
            device_id_type=MESH,
        )
        copy.start()
        copies.append(copy)
    for copy in copies:
        copy.wait()
    held[me] = x_ref[...]
    o_ref[...] = held[...]


def gather_along(value, axis, collective_id):
    count = lax.axis_size(axis)
    return pl.pallas_call(
        functools.partial(gather_kernel, axis, count),
        out_shape=jax.ShapeDtypeStruct((count,) + value.shape, value.dtype),
        in_specs=[pl.BlockSpec(memory_space=pltpu.VMEM)],
        out_specs=pl.BlockSpec(memory_space=pltpu.VMEM),
        scratch_shapes=[
            pltpu.VMEM((count,) + value.shape, value.dtype),
            pltpu.SemaphoreType.DMA((count - 1,)),
            pltpu.SemaphoreType.DMA((count - 1,)),
        ],
        compiler_params=pltpu.CompilerParams(collective_id=collective_id, has_side_effects=True),
    )(value)


def finish_kernel(
    fsdp_count, ctx_count, tile_ref, rim_ref, tiles_out, rim_out, tiles_held, rim_held,
    send_sem, recv_sem, rim_send_sem, rim_recv_sem,
):
    f_me = lax.axis_index("fsdp")
    c_me = lax.axis_index("ctx")
    left = lax.rem(c_me + ctx_count - 1, ctx_count)
    right = lax.rem(c_me + 1, ctx_count)
    barrier = pltpu.get_barrier_semaphore()
    for step in range(1, fsdp_count):
        peer = (lax.rem(f_me + step, fsdp_count), c_me)
        pl.semaphore_signal(barrier, inc=1, device_id=peer, device_id_type=MESH)
    for side in (left, right):
        pl.semaphore_signal(barrier, inc=1, device_id=(f_me, side), device_id_type=MESH)
    pl.semaphore_wait(barrier, fsdp_count + 1)
    rim_copy = pltpu.make_async_remote_copy(
        src_ref=rim_ref,
        dst_ref=rim_held,
        send_sem=rim_send_sem,
        recv_sem=rim_recv_sem,
        device_id=(f_me, left),
        device_id_type=MESH,
    )
    rim_copy.start()
    copies = []
    for step in range(1, fsdp_count):
        copy = pltpu.make_async_remote_copy(
            src_ref=tile_ref,
            dst_ref=tiles_held.at[f_me],
            send_sem=send_sem.at[step - 1],
            recv_sem=recv_sem.at[step - 1],
            device_id=(lax.rem(f_me + step, fsdp_count), c_me),
            device_id_type=MESH,
        )
        copy.start()
        copies.append(copy)
    for copy in copies:
        copy.wait()
    rim_copy.wait()
    tiles_held[f_me] = tile_ref[...]
    tiles_out[...] = tiles_held[...]
    rim_out[...] = rim_held[...]


def finish_exchange(tile, rim):
    fsdp_count = lax.axis_size("fsdp")
    ctx_count = lax.axis_size("ctx")
    return pl.pallas_call(
        functools.partial(finish_kernel, fsdp_count, ctx_count),
        out_shape=(
            jax.ShapeDtypeStruct((fsdp_count,) + tile.shape, tile.dtype),
            jax.ShapeDtypeStruct(rim.shape, rim.dtype),
        ),
        in_specs=[pl.BlockSpec(memory_space=pltpu.VMEM)] * 2,
        out_specs=(pl.BlockSpec(memory_space=pltpu.VMEM), pl.BlockSpec(memory_space=pltpu.VMEM)),
        scratch_shapes=[
            pltpu.VMEM((fsdp_count,) + tile.shape, tile.dtype),
            pltpu.VMEM(rim.shape, rim.dtype),
            pltpu.SemaphoreType.DMA((fsdp_count - 1,)),
            pltpu.SemaphoreType.DMA((fsdp_count - 1,)),
            pltpu.SemaphoreType.DMA(()),
            pltpu.SemaphoreType.DMA(()),
        ],
        compiler_params=pltpu.CompilerParams(collective_id=1, has_side_effects=True),
    )(tile, rim)


def passed_along(value, axis, steps):
    count = lax.axis_size(axis)
    leading, last = (max(0, -steps), min(count, count - steps))
    return lax.ppermute(value, axis, [(source, source + steps) for source in range(leading, last)])


def short_conv(taps_table, row_data, tokens, rim_rows, forward):
    summed = jnp.zeros((3, tokens, row_data.shape[2]), jnp.float32)
    for offset in range(taps_table.shape[1]):
        start_row = rim_rows - offset if forward else offset
        summed = (
            summed + taps_table[:, offset, None, :] * row_data[:, start_row : start_row + tokens, :]
        )
    return summed


def per_device(features, short_taps, decay_rates, mode_gains, cotangent):
    tokens = features.shape[1]
    channels = features.shape[2]
    group_count = decay_rates.shape[0]
    order_count = decay_rates.shape[1]
    members = channels // group_count
    rim_rows = short_taps.shape[1] - 1
    block_len = 128
    block_count = tokens // block_len
    ctx_count = lax.axis_size("ctx")
    ctx_index = lax.axis_index("ctx")
    earlier_rows = passed_along(features[:, tokens - rim_rows :, :], "ctx", 1)
    extended = jnp.concatenate([earlier_rows, features], axis=1)
    shaped = short_conv(short_taps, extended, tokens, rim_rows, True)
    query_part, key_part, value_part = (shaped[0], shaped[1], shaped[2])
    product = (key_part * value_part).astype(jnp.bfloat16)
    adjoint = cotangent * query_part
    grouped_z = product.reshape(tokens, group_count, members)
    grouped_e = adjoint.reshape(tokens, group_count, members)
    mode_coefs = mode_gains * jnp.sqrt(2.0 * decay_rates)
    rate_axis = decay_rates[:, :, None]
    lag_axis = jnp.arange(block_len, dtype=jnp.float32)[None, None, :]
    block_pow = jnp.exp(-rate_axis * lag_axis)
    block_after = block_pow * jnp.exp(-rate_axis)
    block_moments = jnp.stack([block_after, (lag_axis + 1.0) * block_after])
    coef_after = mode_coefs[:, :, None] * block_after
    tail_axis = block_len - 1.0 - lag_axis
    tail_pow = jnp.exp(-rate_axis * tail_axis)
    block_ends = jnp.stack([tail_pow, -tail_axis * tail_pow])
    coef_tail = mode_coefs[:, :, None] * jnp.exp(-rate_axis * (tail_axis + 1.0))
    lag_index = (
        jnp.arange(block_len, dtype=jnp.int32)[:, None]
        - jnp.arange(block_len, dtype=jnp.int32)[None, :]
    )
    lag_value = jnp.maximum(lag_index, 0).astype(jnp.float32)
    pair_pow = jnp.exp(-decay_rates[:, :, None, None] * lag_value[None, None])
    toeplitz = jnp.where(
        lag_index[None] >= 0, jnp.sum(mode_coefs[:, :, None, None] * pair_pow, axis=1), 0.0
    )
    z_blocks = grouped_z.reshape(block_count, block_len, group_count, members)
    e_blocks = grouped_e.reshape(block_count, block_len, group_count, members)

    z_wide = z_blocks.astype(jnp.float32)
    block_ids = jnp.arange(block_count, dtype=jnp.float32)
    rate_cols = jnp.repeat(decay_rates.T, members, axis=1)
    block_steps = (block_ids[:, None] - 1.0 - block_ids[None, :])[:, :, None, None]
    span_weight = jnp.where(
        block_steps >= 0,
        jnp.exp(-rate_cols[None, None] * (block_len * jnp.maximum(block_steps, 0.0))),
        0.0,
    )
    inside_fwd = jnp.einsum("gts,bsgm->btgm", toeplitz, z_wide, precision=threepass)
    fresh_fwd = jnp.einsum("kgns,bsgm->kbngm", block_ends, z_wide, precision=threepass).reshape(
        2, block_count, order_count, channels
    )
    start_flat = jnp.sum(span_weight * fresh_fwd[0][None], axis=1)
    lagged_flat = jnp.sum(
        span_weight * (fresh_fwd[1][None] - block_len * block_steps * fresh_fwd[0][None]), axis=1
    )
    moments = jnp.einsum("kgnt,btgm->kbngm", block_moments, e_blocks, precision=precise).reshape(
        2, block_count, order_count, channels
    )
    first_acc = jnp.sum(moments[0] * start_flat, axis=0)
    lag_acc = jnp.sum(moments[0] * lagged_flat - moments[1] * start_flat, axis=0)
    first_acc = first_acc.reshape(order_count, group_count, members).sum(axis=2)
    lag_acc = lag_acc.reshape(order_count, group_count, members).sum(axis=2)
    gram_acc = jnp.einsum("btgm,bsgm->gts", e_blocks, z_wide, precision=precise)
    gram_low = jnp.where(lag_index[None] >= 0, gram_acc, 0.0)
    gram_pair = jnp.stack([gram_low, gram_low * lag_value[None]])
    rise_pow = jnp.exp(rate_axis * lag_axis)
    gram_rise = jnp.einsum("kgts,gns->kgnt", gram_pair, rise_pow, precision=precise)
    first_in = jnp.sum(block_pow * gram_rise[0], axis=2)
    lag_in = jnp.sum(block_pow * gram_rise[1], axis=2)
    first_local = first_acc.T + first_in
    lag_local = lag_acc.T - lag_in
    inside_bwd = jnp.einsum("gts,btgm->bsgm", toeplitz, e_blocks, precision=precise)
    fresh_bwd = jnp.einsum("gnt,btgm->bngm", block_pow, e_blocks, precision=precise).reshape(
        block_count, order_count, channels
    )
    later_flat = jnp.sum(jnp.swapaxes(span_weight, 0, 1) * fresh_bwd[None], axis=1)
    first_ids = block_ids[:, None, None]
    last_ids = block_count - 1.0 - block_ids[:, None, None]
    from_first = jnp.exp(-rate_cols[None] * (block_len * first_ids))
    from_last = jnp.exp(-rate_cols[None] * (block_len * last_ids))
    end_state = jnp.sum(from_last * fresh_fwd[0], axis=0)
    end_lagged = jnp.sum(from_last * (fresh_fwd[1] - block_len * last_ids * fresh_fwd[0]), axis=0)
    start_state = jnp.sum(from_first * fresh_bwd, axis=0)
    second_moment = jnp.sum(from_first * (moments[1] + block_len * first_ids * moments[0]), axis=0)
    partial_rows = jnp.stack([first_local, lag_local]).reshape(-1, channels)
    state_rows = jnp.stack([end_state, end_lagged, start_state, second_moment]).reshape(
        4 * order_count, channels
    )
    payload_rows = -(-(state_rows.shape[0] + partial_rows.shape[0]) // 8) * 8
    local_states = jnp.zeros((payload_rows, channels), jnp.float32)
    local_states = local_states.at[: state_rows.shape[0]].set(state_rows)
    local_states = local_states.at[state_rows.shape[0] : state_rows.shape[0] + partial_rows.shape[0]].set(
        partial_rows
    )
    gathered = gather_along(local_states, "ctx", 0)
    everyone = gathered[:, : state_rows.shape[0]].reshape(ctx_count, 4, order_count, channels)
    device_ids = jnp.arange(ctx_count, dtype=jnp.int32)
    ahead_steps = (ctx_index - 1 - device_ids).astype(jnp.float32)[:, None, None]
    behind_steps = (device_ids - ctx_index - 1).astype(jnp.float32)[:, None, None]
    ahead_weight = jnp.where(
        ahead_steps >= 0, jnp.exp(-rate_cols[None] * (tokens * jnp.maximum(ahead_steps, 0.0))), 0.0
    )
    behind_weight = jnp.where(
        behind_steps >= 0,
        jnp.exp(-rate_cols[None] * (tokens * jnp.maximum(behind_steps, 0.0))),
        0.0,
    )
    prev_state = jnp.sum(ahead_weight * everyone[:, 0], axis=0)
    next_state = jnp.sum(behind_weight * everyone[:, 2], axis=0)
    all_ids = device_ids.astype(jnp.float32)
    pair_steps = (all_ids[:, None] - 1.0 - all_ids[None, :])[:, :, None, None]
    pair_weight = jnp.where(
        pair_steps >= 0, jnp.exp(-rate_cols[None, None] * (tokens * jnp.maximum(pair_steps, 0.0))), 0.0
    )
    all_prev = jnp.sum(pair_weight * everyone[None, :, 0], axis=1)
    all_lagged = jnp.sum(
        pair_weight * (everyone[None, :, 1] - tokens * pair_steps * everyone[None, :, 0]), axis=1
    )
    all_first = jnp.exp(-rate_cols)[None] * everyone[:, 2]
    cross_first = jnp.sum(all_first * all_prev, axis=0)
    cross_lag = jnp.sum(all_first * all_lagged - everyone[:, 3] * all_prev, axis=0)
    cross_first = cross_first.reshape(order_count, group_count, members).sum(axis=2).T
    cross_lag = cross_lag.reshape(order_count, group_count, members).sum(axis=2).T
    gathered_parts = gathered[:, state_rows.shape[0] : state_rows.shape[0] + partial_rows.shape[0]].reshape(
        ctx_count, 2, group_count, order_count
    )
    local_totals = jnp.sum(gathered_parts, axis=0)
    first_total = local_totals[0] + cross_first
    lag_total = local_totals[1] + cross_lag

    grouped_shape = (block_count, order_count, group_count, members)
    start_total = (start_flat + from_first * prev_state[None]).reshape(grouped_shape)
    later_total = (later_flat + from_last * next_state[None]).reshape(grouped_shape)
    carried_fwd = jnp.einsum("gnt,bngm->btgm", coef_after, start_total, precision=precise)
    inner_sum = (inside_fwd + carried_fwd).reshape(tokens, group_count, members)
    carried_bwd = jnp.einsum("gns,bngm->bsgm", coef_tail, later_total, precision=precise)
    product_grad = (inside_bwd + carried_bwd).reshape(tokens, group_count, members)
    gain_part = jnp.sqrt(2.0 * decay_rates) * first_total
    rate_part = mode_coefs * (0.5 * first_total + decay_rates * lag_total)
    inner_flat = inner_sum.reshape(tokens, channels)
    mixer_output = (query_part * inner_flat).astype(jnp.bfloat16)
    grad_flat = product_grad.reshape(tokens, channels)
    feature_adj = jnp.stack([cotangent * inner_flat, grad_flat * value_part, grad_flat * key_part])
    filter_local = jnp.stack([gain_part, rate_part])
    entry_count = 2 * group_count * order_count * lax.axis_size("fsdp")
    summed = filter_local
    square_tile = jnp.full((8, 128), jnp.sum(summed * summed), jnp.float32)
    rim_send = feature_adj[:, :rim_rows, :].reshape(3 * rim_rows, channels)
    square_tiles, rim_got = finish_exchange(square_tile, rim_send)
    squares = jnp.sum(square_tiles[:, 0, 0])
    later_rows = jnp.where(ctx_index == ctx_count - 1, 0.0, rim_got).reshape(3, rim_rows, channels)
    appended = jnp.concatenate([feature_adj, later_rows], axis=1)
    feature_grads = short_conv(short_taps, appended, tokens, rim_rows, False).astype(jnp.bfloat16)
    factor = jnp.minimum(1.0, lax.rsqrt(squares / entry_count + 1e-06))
    clipped = summed * factor
    return (mixer_output, feature_grads, clipped[0], clipped[1])


def solution(mesh):
    return jax.shard_map(
        per_device,
        mesh=mesh,
        in_specs=(
            P(None, "ctx", "fsdp"),
            P(None, None, "fsdp"),
            P("fsdp", None),
            P("fsdp", None),
            P("ctx", "fsdp"),
        ),
        out_specs=(P("ctx", "fsdp"), P(None, "ctx", "fsdp"), P("fsdp", None), P("fsdp", None)),
        check_vma=False,
    )
```

```python
import jax
import jax.numpy as jnp
from jax import lax
from jax.experimental import pallas as pl
from jax.experimental.pallas import tpu as pltpu
from jax.sharding import PartitionSpec as P
import functools

MESH = pl.DeviceIdType.MESH

precise = lax.Precision.HIGHEST
threepass = lax.Precision.HIGH


def gather_kernel(axis, count, x_ref, o_ref, held, send_sem, recv_sem):
    me = lax.axis_index(axis)

    def device(peer):
        if axis == "ctx":
            return (lax.axis_index("fsdp"), peer)
        return (peer, lax.axis_index("ctx"))

    barrier = pltpu.get_barrier_semaphore()
    for step in range(1, count):
        pl.semaphore_signal(
            barrier, inc=1, device_id=device(lax.rem(me + step, count)), device_id_type=MESH
        )
    pl.semaphore_wait(barrier, count - 1)
    copies = []
    for step in range(1, count):
        copy = pltpu.make_async_remote_copy(
            src_ref=x_ref,
            dst_ref=held.at[me],
            send_sem=send_sem.at[step - 1],
            recv_sem=recv_sem.at[step - 1],
            device_id=device(lax.rem(me + step, count)),
            device_id_type=MESH,
        )
        copy.start()
        copies.append(copy)
    for copy in copies:
        copy.wait()
    held[me] = x_ref[...]
    o_ref[...] = held[...]


def gather_along(value, axis, collective_id):
    count = lax.axis_size(axis)
    return pl.pallas_call(
        functools.partial(gather_kernel, axis, count),
        out_shape=jax.ShapeDtypeStruct((count,) + value.shape, value.dtype),
        in_specs=[pl.BlockSpec(memory_space=pltpu.VMEM)],
        out_specs=pl.BlockSpec(memory_space=pltpu.VMEM),
        scratch_shapes=[
            pltpu.VMEM((count,) + value.shape, value.dtype),
            pltpu.SemaphoreType.DMA((count - 1,)),
            pltpu.SemaphoreType.DMA((count - 1,)),
        ],
        compiler_params=pltpu.CompilerParams(collective_id=collective_id, has_side_effects=True),
    )(value)


def finish_kernel(
    fsdp_count, ctx_count, tile_ref, rim_ref, tiles_out, rim_out, tiles_held, rim_held,
    send_sem, recv_sem, rim_send_sem, rim_recv_sem,
):
    f_me = lax.axis_index("fsdp")
    c_me = lax.axis_index("ctx")
    left = lax.rem(c_me + ctx_count - 1, ctx_count)
    right = lax.rem(c_me + 1, ctx_count)
    barrier = pltpu.get_barrier_semaphore()
    for step in range(1, fsdp_count):
        peer = (lax.rem(f_me + step, fsdp_count), c_me)
        pl.semaphore_signal(barrier, inc=1, device_id=peer, device_id_type=MESH)
    for side in (left, right):
        pl.semaphore_signal(barrier, inc=1, device_id=(f_me, side), device_id_type=MESH)
    pl.semaphore_wait(barrier, fsdp_count + 1)
    rim_copy = pltpu.make_async_remote_copy(
        src_ref=rim_ref,
        dst_ref=rim_held,
        send_sem=rim_send_sem,
        recv_sem=rim_recv_sem,
        device_id=(f_me, left),
        device_id_type=MESH,
    )
    rim_copy.start()
    copies = []
    for step in range(1, fsdp_count):
        copy = pltpu.make_async_remote_copy(
            src_ref=tile_ref,
            dst_ref=tiles_held.at[f_me],
            send_sem=send_sem.at[step - 1],
            recv_sem=recv_sem.at[step - 1],
            device_id=(lax.rem(f_me + step, fsdp_count), c_me),
            device_id_type=MESH,
        )
        copy.start()
        copies.append(copy)
    for copy in copies:
        copy.wait()
    rim_copy.wait()
    tiles_held[f_me] = tile_ref[...]
    tiles_out[...] = tiles_held[...]
    rim_out[...] = rim_held[...]


def finish_exchange(tile, rim):
    fsdp_count = lax.axis_size("fsdp")
    ctx_count = lax.axis_size("ctx")
    return pl.pallas_call(
        functools.partial(finish_kernel, fsdp_count, ctx_count),
        out_shape=(
            jax.ShapeDtypeStruct((fsdp_count,) + tile.shape, tile.dtype),
            jax.ShapeDtypeStruct(rim.shape, rim.dtype),
        ),
        in_specs=[pl.BlockSpec(memory_space=pltpu.VMEM)] * 2,
        out_specs=(pl.BlockSpec(memory_space=pltpu.VMEM), pl.BlockSpec(memory_space=pltpu.VMEM)),
        scratch_shapes=[
            pltpu.VMEM((fsdp_count,) + tile.shape, tile.dtype),
            pltpu.VMEM(rim.shape, rim.dtype),
            pltpu.SemaphoreType.DMA((fsdp_count - 1,)),
            pltpu.SemaphoreType.DMA((fsdp_count - 1,)),
            pltpu.SemaphoreType.DMA(()),
            pltpu.SemaphoreType.DMA(()),
        ],
        compiler_params=pltpu.CompilerParams(collective_id=1, has_side_effects=True),
    )(tile, rim)


def passed_along(value, axis, steps):
    count = lax.axis_size(axis)
    leading, last = (max(0, -steps), min(count, count - steps))
    return lax.ppermute(value, axis, [(source, source + steps) for source in range(leading, last)])


def short_conv(taps_table, row_data, tokens, rim_rows, forward):
    summed = jnp.zeros((3, tokens, row_data.shape[2]), jnp.float32)
    for offset in range(taps_table.shape[1]):
        start_row = rim_rows - offset if forward else offset
        summed = (
            summed + taps_table[:, offset, None, :] * row_data[:, start_row : start_row + tokens, :]
        )
    return summed


def per_device(features, short_taps, decay_rates, mode_gains, cotangent):
    tokens = features.shape[1]
    channels = features.shape[2]
    group_count = decay_rates.shape[0]
    order_count = decay_rates.shape[1]
    members = channels // group_count
    rim_rows = short_taps.shape[1] - 1
    block_len = 128
    block_count = tokens // block_len
    ctx_count = lax.axis_size("ctx")
    ctx_index = lax.axis_index("ctx")
    earlier_rows = passed_along(features[:, tokens - rim_rows :, :], "ctx", 1)
    extended = jnp.concatenate([earlier_rows, features], axis=1)
    shaped = short_conv(short_taps, extended, tokens, rim_rows, True)
    query_part, key_part, value_part = (shaped[0], shaped[1], shaped[2])
    product = (key_part * value_part).astype(jnp.bfloat16)
    adjoint = cotangent * query_part
    grouped_z = product.reshape(tokens, group_count, members)
    grouped_e = adjoint.reshape(tokens, group_count, members)
    mode_coefs = mode_gains * jnp.sqrt(2.0 * decay_rates)
    rate_axis = decay_rates[:, :, None]
    lag_axis = jnp.arange(block_len, dtype=jnp.float32)[None, None, :]
    block_pow = jnp.exp(-rate_axis * lag_axis)
    block_after = block_pow * jnp.exp(-rate_axis)
    block_moments = jnp.stack([block_after, (lag_axis + 1.0) * block_after])
    coef_after = mode_coefs[:, :, None] * block_after
    tail_axis = block_len - 1.0 - lag_axis
    tail_pow = jnp.exp(-rate_axis * tail_axis)
    block_ends = jnp.stack([tail_pow, -tail_axis * tail_pow])
    coef_tail = mode_coefs[:, :, None] * jnp.exp(-rate_axis * (tail_axis + 1.0))
    lag_index = (
        jnp.arange(block_len, dtype=jnp.int32)[:, None]
        - jnp.arange(block_len, dtype=jnp.int32)[None, :]
    )
    lag_value = jnp.maximum(lag_index, 0).astype(jnp.float32)
    pair_pow = jnp.exp(-decay_rates[:, :, None, None] * lag_value[None, None])
    toeplitz = jnp.where(
        lag_index[None] >= 0, jnp.sum(mode_coefs[:, :, None, None] * pair_pow, axis=1), 0.0
    )
    z_blocks = grouped_z.reshape(block_count, block_len, group_count, members)
    e_blocks = grouped_e.reshape(block_count, block_len, group_count, members)

    z_wide = z_blocks.astype(jnp.float32)
    block_ids = jnp.arange(block_count, dtype=jnp.float32)
    rate_cols = jnp.repeat(decay_rates.T, members, axis=1)
    block_steps = (block_ids[:, None] - 1.0 - block_ids[None, :])[:, :, None, None]
    span_weight = jnp.where(
        block_steps >= 0,
        jnp.exp(-rate_cols[None, None] * (block_len * jnp.maximum(block_steps, 0.0))),
        0.0,
    )
    span_weight, span_back = lax.optimization_barrier(
        (span_weight, jnp.swapaxes(span_weight, 0, 1))
    )
    inside_fwd = jnp.einsum("gts,bsgm->btgm", toeplitz, z_wide, precision=threepass)
    fresh_fwd = jnp.einsum("kgns,bsgm->kbngm", block_ends, z_wide, precision=threepass).reshape(
        2, block_count, order_count, channels
    )
    start_flat = jnp.sum(span_weight * fresh_fwd[0][None], axis=1)
    lagged_flat = jnp.sum(
        span_weight * (fresh_fwd[1][None] - block_len * block_steps * fresh_fwd[0][None]), axis=1
    )
    moments = jnp.einsum("kgnt,btgm->kbngm", block_moments, e_blocks, precision=precise).reshape(
        2, block_count, order_count, channels
    )
    first_acc = jnp.sum(moments[0] * start_flat, axis=0)
    lag_acc = jnp.sum(moments[0] * lagged_flat - moments[1] * start_flat, axis=0)
    first_acc = first_acc.reshape(order_count, group_count, members).sum(axis=2)
    lag_acc = lag_acc.reshape(order_count, group_count, members).sum(axis=2)
    gram_acc = jnp.einsum("btgm,bsgm->gts", e_blocks, z_wide, precision=precise)
    gram_low = jnp.where(lag_index[None] >= 0, gram_acc, 0.0)
    gram_pair = jnp.stack([gram_low, gram_low * lag_value[None]])
    rise_pow = jnp.exp(rate_axis * lag_axis)
    gram_rise = jnp.einsum("kgts,gns->kgnt", gram_pair, rise_pow, precision=precise)
    first_in = jnp.sum(block_pow * gram_rise[0], axis=2)
    lag_in = jnp.sum(block_pow * gram_rise[1], axis=2)
    first_local = first_acc.T + first_in
    lag_local = lag_acc.T - lag_in
    inside_bwd = jnp.einsum("gts,btgm->bsgm", toeplitz, e_blocks, precision=precise)
    fresh_bwd = jnp.einsum("gnt,btgm->bngm", block_pow, e_blocks, precision=precise).reshape(
        block_count, order_count, channels
    )
    later_flat = jnp.sum(span_back * fresh_bwd[None], axis=1)
    first_ids = block_ids[:, None, None]
    last_ids = block_count - 1.0 - block_ids[:, None, None]
    from_first, from_last = lax.optimization_barrier(
        (
            jnp.exp(-rate_cols[None] * (block_len * first_ids)),
            jnp.exp(-rate_cols[None] * (block_len * last_ids)),
        )
    )
    end_state = jnp.sum(from_last * fresh_fwd[0], axis=0)
    end_lagged = jnp.sum(from_last * (fresh_fwd[1] - block_len * last_ids * fresh_fwd[0]), axis=0)
    start_state = jnp.sum(from_first * fresh_bwd, axis=0)
    second_moment = jnp.sum(from_first * (moments[1] + block_len * first_ids * moments[0]), axis=0)
    partial_rows = jnp.stack([first_local, lag_local]).reshape(-1, channels)
    state_rows = jnp.stack([end_state, end_lagged, start_state, second_moment]).reshape(
        4 * order_count, channels
    )
    payload_rows = -(-(state_rows.shape[0] + partial_rows.shape[0]) // 8) * 8
    local_states = jnp.zeros((payload_rows, channels), jnp.float32)
    local_states = local_states.at[: state_rows.shape[0]].set(state_rows)
    local_states = local_states.at[state_rows.shape[0] : state_rows.shape[0] + partial_rows.shape[0]].set(
        partial_rows
    )
    gathered = gather_along(local_states, "ctx", 0)
    everyone = gathered[:, : state_rows.shape[0]].reshape(ctx_count, 4, order_count, channels)
    device_ids = jnp.arange(ctx_count, dtype=jnp.int32)
    ahead_steps = (ctx_index - 1 - device_ids).astype(jnp.float32)[:, None, None]
    behind_steps = (device_ids - ctx_index - 1).astype(jnp.float32)[:, None, None]
    ahead_weight = jnp.where(
        ahead_steps >= 0, jnp.exp(-rate_cols[None] * (tokens * jnp.maximum(ahead_steps, 0.0))), 0.0
    )
    behind_weight = jnp.where(
        behind_steps >= 0,
        jnp.exp(-rate_cols[None] * (tokens * jnp.maximum(behind_steps, 0.0))),
        0.0,
    )
    prev_state = jnp.sum(ahead_weight * everyone[:, 0], axis=0)
    next_state = jnp.sum(behind_weight * everyone[:, 2], axis=0)
    all_ids = device_ids.astype(jnp.float32)
    pair_steps = (all_ids[:, None] - 1.0 - all_ids[None, :])[:, :, None, None]
    pair_weight = jnp.where(
        pair_steps >= 0, jnp.exp(-rate_cols[None, None] * (tokens * jnp.maximum(pair_steps, 0.0))), 0.0
    )
    all_prev = jnp.sum(pair_weight * everyone[None, :, 0], axis=1)
    all_lagged = jnp.sum(
        pair_weight * (everyone[None, :, 1] - tokens * pair_steps * everyone[None, :, 0]), axis=1
    )
    all_first = jnp.exp(-rate_cols)[None] * everyone[:, 2]
    cross_first = jnp.sum(all_first * all_prev, axis=0)
    cross_lag = jnp.sum(all_first * all_lagged - everyone[:, 3] * all_prev, axis=0)
    cross_first = cross_first.reshape(order_count, group_count, members).sum(axis=2).T
    cross_lag = cross_lag.reshape(order_count, group_count, members).sum(axis=2).T
    gathered_parts = gathered[:, state_rows.shape[0] : state_rows.shape[0] + partial_rows.shape[0]].reshape(
        ctx_count, 2, group_count, order_count
    )
    local_totals = jnp.sum(gathered_parts, axis=0)
    first_total = local_totals[0] + cross_first
    lag_total = local_totals[1] + cross_lag

    grouped_shape = (block_count, order_count, group_count, members)
    start_total = (start_flat + from_first * prev_state[None]).reshape(grouped_shape)
    later_total = (later_flat + from_last * next_state[None]).reshape(grouped_shape)
    carried_fwd = jnp.einsum("gnt,bngm->btgm", coef_after, start_total, precision=precise)
    inner_sum = (inside_fwd + carried_fwd).reshape(tokens, group_count, members)
    carried_bwd = jnp.einsum("gns,bngm->bsgm", coef_tail, later_total, precision=precise)
    product_grad = (inside_bwd + carried_bwd).reshape(tokens, group_count, members)
    gain_part = jnp.sqrt(2.0 * decay_rates) * first_total
    rate_part = mode_coefs * (0.5 * first_total + decay_rates * lag_total)
    inner_flat = inner_sum.reshape(tokens, channels)
    mixer_output = (query_part * inner_flat).astype(jnp.bfloat16)
    grad_flat = product_grad.reshape(tokens, channels)
    feature_adj = jnp.stack([cotangent * inner_flat, grad_flat * value_part, grad_flat * key_part])
    filter_local = jnp.stack([gain_part, rate_part])
    entry_count = 2 * group_count * order_count * lax.axis_size("fsdp")
    summed = filter_local
    square_tile = jnp.full((8, 128), jnp.sum(summed * summed), jnp.float32)
    rim_send = feature_adj[:, :rim_rows, :].reshape(3 * rim_rows, channels)
    square_tiles, rim_got = finish_exchange(square_tile, rim_send)
    squares = jnp.sum(square_tiles[:, 0, 0])
    later_rows = jnp.where(ctx_index == ctx_count - 1, 0.0, rim_got).reshape(3, rim_rows, channels)
    appended = jnp.concatenate([feature_adj, later_rows], axis=1)
    feature_grads = short_conv(short_taps, appended, tokens, rim_rows, False).astype(jnp.bfloat16)
    factor = jnp.minimum(1.0, lax.rsqrt(squares / entry_count + 1e-06))
    clipped = summed * factor
    return (mixer_output, feature_grads, clipped[0], clipped[1])


def solution(mesh):
    return jax.shard_map(
        per_device,
        mesh=mesh,
        in_specs=(
            P(None, "ctx", "fsdp"),
            P(None, None, "fsdp"),
            P("fsdp", None),
            P("fsdp", None),
            P("ctx", "fsdp"),
        ),
        out_specs=(P("ctx", "fsdp"), P(None, "ctx", "fsdp"), P("fsdp", None), P("fsdp", None)),
        check_vma=False,
    )
```

```python
import jax
import jax.numpy as jnp
from jax import lax
from jax.experimental import pallas as pl
from jax.experimental.pallas import tpu as pltpu
from jax.sharding import PartitionSpec as P
import functools

MESH = pl.DeviceIdType.MESH

precise = lax.Precision.HIGHEST
threepass = lax.Precision.HIGH


def gather_kernel(axis, count, x_ref, o_ref, held, send_sem, recv_sem):
    me = lax.axis_index(axis)

    def device(peer):
        if axis == "ctx":
            return (lax.axis_index("fsdp"), peer)
        return (peer, lax.axis_index("ctx"))

    barrier = pltpu.get_barrier_semaphore()
    for step in range(1, count):
        pl.semaphore_signal(
            barrier, inc=1, device_id=device(lax.rem(me + step, count)), device_id_type=MESH
        )
    pl.semaphore_wait(barrier, count - 1)
    copies = []
    for step in range(1, count):
        copy = pltpu.make_async_remote_copy(
            src_ref=x_ref,
            dst_ref=held.at[me],
            send_sem=send_sem.at[step - 1],
            recv_sem=recv_sem.at[step - 1],
            device_id=device(lax.rem(me + step, count)),
            device_id_type=MESH,
        )
        copy.start()
        copies.append(copy)
    for copy in copies:
        copy.wait()
    held[me] = x_ref[...]
    o_ref[...] = held[...]


def gather_along(value, axis, collective_id):
    count = lax.axis_size(axis)
    return pl.pallas_call(
        functools.partial(gather_kernel, axis, count),
        out_shape=jax.ShapeDtypeStruct((count,) + value.shape, value.dtype),
        in_specs=[pl.BlockSpec(memory_space=pltpu.VMEM)],
        out_specs=pl.BlockSpec(memory_space=pltpu.VMEM),
        scratch_shapes=[
            pltpu.VMEM((count,) + value.shape, value.dtype),
            pltpu.SemaphoreType.DMA((count - 1,)),
            pltpu.SemaphoreType.DMA((count - 1,)),
        ],
        compiler_params=pltpu.CompilerParams(collective_id=collective_id, has_side_effects=True),
    )(value)


def finish_kernel(
    fsdp_count, ctx_count, tile_ref, rim_ref, tiles_out, rim_out, tiles_held, rim_held,
    send_sem, recv_sem, rim_send_sem, rim_recv_sem,
):
    f_me = lax.axis_index("fsdp")
    c_me = lax.axis_index("ctx")
    left = lax.rem(c_me + ctx_count - 1, ctx_count)
    right = lax.rem(c_me + 1, ctx_count)
    barrier = pltpu.get_barrier_semaphore()
    for step in range(1, fsdp_count):
        peer = (lax.rem(f_me + step, fsdp_count), c_me)
        pl.semaphore_signal(barrier, inc=1, device_id=peer, device_id_type=MESH)
    for side in (left, right):
        pl.semaphore_signal(barrier, inc=1, device_id=(f_me, side), device_id_type=MESH)
    pl.semaphore_wait(barrier, fsdp_count + 1)
    rim_copy = pltpu.make_async_remote_copy(
        src_ref=rim_ref,
        dst_ref=rim_held,
        send_sem=rim_send_sem,
        recv_sem=rim_recv_sem,
        device_id=(f_me, left),
        device_id_type=MESH,
    )
    rim_copy.start()
    copies = []
    for step in range(1, fsdp_count):
        copy = pltpu.make_async_remote_copy(
            src_ref=tile_ref,
            dst_ref=tiles_held.at[f_me],
            send_sem=send_sem.at[step - 1],
            recv_sem=recv_sem.at[step - 1],
            device_id=(lax.rem(f_me + step, fsdp_count), c_me),
            device_id_type=MESH,
        )
        copy.start()
        copies.append(copy)
    for copy in copies:
        copy.wait()
    rim_copy.wait()
    tiles_held[f_me] = tile_ref[...]
    tiles_out[...] = tiles_held[...]
    rim_out[...] = rim_held[...]


def finish_exchange(tile, rim):
    fsdp_count = lax.axis_size("fsdp")
    ctx_count = lax.axis_size("ctx")
    return pl.pallas_call(
        functools.partial(finish_kernel, fsdp_count, ctx_count),
        out_shape=(
            jax.ShapeDtypeStruct((fsdp_count,) + tile.shape, tile.dtype),
            jax.ShapeDtypeStruct(rim.shape, rim.dtype),
        ),
        in_specs=[pl.BlockSpec(memory_space=pltpu.VMEM)] * 2,
        out_specs=(pl.BlockSpec(memory_space=pltpu.VMEM), pl.BlockSpec(memory_space=pltpu.VMEM)),
        scratch_shapes=[
            pltpu.VMEM((fsdp_count,) + tile.shape, tile.dtype),
            pltpu.VMEM(rim.shape, rim.dtype),
            pltpu.SemaphoreType.DMA((fsdp_count - 1,)),
            pltpu.SemaphoreType.DMA((fsdp_count - 1,)),
            pltpu.SemaphoreType.DMA(()),
            pltpu.SemaphoreType.DMA(()),
        ],
        compiler_params=pltpu.CompilerParams(collective_id=1, has_side_effects=True),
    )(tile, rim)


def passed_along(value, axis, steps):
    count = lax.axis_size(axis)
    leading, last = (max(0, -steps), min(count, count - steps))
    return lax.ppermute(value, axis, [(source, source + steps) for source in range(leading, last)])


def short_conv(taps_table, row_data, tokens, rim_rows, forward):
    summed = jnp.zeros((3, tokens, row_data.shape[2]), jnp.float32)
    for offset in range(taps_table.shape[1]):
        start_row = rim_rows - offset if forward else offset
        summed = (
            summed + taps_table[:, offset, None, :] * row_data[:, start_row : start_row + tokens, :]
        )
    return summed


def per_device(features, short_taps, decay_rates, mode_gains, cotangent):
    tokens = features.shape[1]
    channels = features.shape[2]
    group_count = decay_rates.shape[0]
    order_count = decay_rates.shape[1]
    members = channels // group_count
    rim_rows = short_taps.shape[1] - 1
    block_len = 128
    block_count = tokens // block_len
    ctx_count = lax.axis_size("ctx")
    ctx_index = lax.axis_index("ctx")
    earlier_rows = passed_along(features[:, tokens - rim_rows :, :], "ctx", 1)
    extended = jnp.concatenate([earlier_rows, features], axis=1)
    shaped = short_conv(short_taps, extended, tokens, rim_rows, True)
    query_part, key_part, value_part = (shaped[0], shaped[1], shaped[2])
    product = (key_part * value_part).astype(jnp.bfloat16)
    adjoint = cotangent * query_part
    grouped_z = product.reshape(tokens, group_count, members)
    grouped_e = adjoint.reshape(tokens, group_count, members)
    mode_coefs = mode_gains * jnp.sqrt(2.0 * decay_rates)
    rate_axis = decay_rates[:, :, None]
    lag_axis = jnp.arange(block_len, dtype=jnp.float32)[None, None, :]
    block_pow = jnp.exp(-rate_axis * lag_axis)
    block_after = block_pow * jnp.exp(-rate_axis)
    block_moments = jnp.stack([block_after, (lag_axis + 1.0) * block_after])
    coef_after = mode_coefs[:, :, None] * block_after
    tail_axis = block_len - 1.0 - lag_axis
    tail_pow = jnp.exp(-rate_axis * tail_axis)
    block_ends = jnp.stack([tail_pow, -tail_axis * tail_pow])
    coef_tail = mode_coefs[:, :, None] * jnp.exp(-rate_axis * (tail_axis + 1.0))
    lag_index = (
        jnp.arange(block_len, dtype=jnp.int32)[:, None]
        - jnp.arange(block_len, dtype=jnp.int32)[None, :]
    )
    lag_value = jnp.maximum(lag_index, 0).astype(jnp.float32)
    rise_pow = jnp.exp(rate_axis * lag_axis)
    toeplitz = jnp.where(
        lag_index[None] >= 0,
        jnp.einsum("gnt,gns->gts", mode_coefs[:, :, None] * block_pow, rise_pow, precision=precise),
        0.0,
    )
    z_blocks = grouped_z.reshape(block_count, block_len, group_count, members)
    e_blocks = grouped_e.reshape(block_count, block_len, group_count, members)

    z_wide = z_blocks.astype(jnp.float32)
    block_ids = jnp.arange(block_count, dtype=jnp.float32)
    block_steps = (block_ids[:, None] - 1.0 - block_ids[None, :])[:, :, None, None, None]
    span_weight = jnp.where(
        block_steps >= 0,
        jnp.exp(-decay_rates.T[None, None, :, :, None] * (block_len * jnp.maximum(block_steps, 0.0))),
        0.0,
    )
    inside_fwd = jnp.einsum("gts,bsgm->btgm", toeplitz, z_wide, precision=threepass)
    fresh_fwd = jnp.einsum("kgns,bsgm->kbngm", block_ends, z_wide, precision=threepass)
    start_states = jnp.sum(span_weight * fresh_fwd[0][None], axis=1)
    start_lagged = jnp.sum(
        span_weight * (fresh_fwd[1][None] - block_len * block_steps * fresh_fwd[0][None]), axis=1
    )
    moments = jnp.einsum("kgnt,btgm->kbngm", block_moments, e_blocks, precision=precise)
    first_acc = jnp.sum(moments[0] * start_states, axis=(0, 3))
    lag_acc = jnp.sum(moments[0] * start_lagged - moments[1] * start_states, axis=(0, 3))
    gram_acc = jnp.einsum("btgm,bsgm->gts", e_blocks, z_wide, precision=precise)
    gram_low = jnp.where(lag_index[None] >= 0, gram_acc, 0.0)
    gram_pair = jnp.stack([gram_low, gram_low * lag_value[None]])
    gram_rise = jnp.einsum("kgts,gns->kgnt", gram_pair, rise_pow, precision=precise)
    first_in = jnp.sum(block_pow * gram_rise[0], axis=2)
    lag_in = jnp.sum(block_pow * gram_rise[1], axis=2)
    first_local = first_acc.T + first_in
    lag_local = lag_acc.T - lag_in
    inside_bwd = jnp.einsum("gts,btgm->bsgm", toeplitz, e_blocks, precision=precise)
    fresh_bwd = jnp.einsum("gnt,btgm->bngm", block_pow, e_blocks, precision=precise)
    later_states = jnp.sum(jnp.swapaxes(span_weight, 0, 1) * fresh_bwd[None], axis=1)
    rates_ng = decay_rates.T[None, :, :, None]
    from_first = jnp.exp(-rates_ng * (block_len * block_ids[:, None, None, None]))
    from_last = jnp.exp(-rates_ng * (block_len * (block_count - 1.0 - block_ids[:, None, None, None])))
    end_state = jnp.sum(from_last * fresh_fwd[0], axis=0)
    end_lagged = jnp.sum(
        from_last
        * (fresh_fwd[1] - block_len * (block_count - 1.0 - block_ids[:, None, None, None]) * fresh_fwd[0]),
        axis=0,
    )
    start_state = jnp.sum(from_first * fresh_bwd, axis=0)
    second_moment = jnp.sum(
        from_first * (moments[1] + block_len * block_ids[:, None, None, None] * moments[0]), axis=0
    )
    partial_rows = jnp.stack([first_local, lag_local]).reshape(-1, channels)
    state_rows = jnp.stack([end_state, end_lagged, start_state, second_moment]).reshape(
        4 * order_count, channels
    )
    payload_rows = -(-(state_rows.shape[0] + partial_rows.shape[0]) // 8) * 8
    local_states = jnp.zeros((payload_rows, channels), jnp.float32)
    local_states = local_states.at[: state_rows.shape[0]].set(state_rows)
    local_states = local_states.at[state_rows.shape[0] : state_rows.shape[0] + partial_rows.shape[0]].set(
        partial_rows
    )
    rate_cols = jnp.repeat(decay_rates.T, members, axis=1)
    gathered = gather_along(local_states, "ctx", 0)
    everyone = gathered[:, : state_rows.shape[0]].reshape(ctx_count, 4, order_count, channels)
    device_ids = jnp.arange(ctx_count, dtype=jnp.int32)
    ahead_steps = (ctx_index - 1 - device_ids).astype(jnp.float32)[:, None, None]
    behind_steps = (device_ids - ctx_index - 1).astype(jnp.float32)[:, None, None]
    ahead_weight = jnp.where(
        ahead_steps >= 0, jnp.exp(-rate_cols[None] * (tokens * jnp.maximum(ahead_steps, 0.0))), 0.0
    )
    behind_weight = jnp.where(
        behind_steps >= 0,
        jnp.exp(-rate_cols[None] * (tokens * jnp.maximum(behind_steps, 0.0))),
        0.0,
    )
    prev_state = jnp.sum(ahead_weight * everyone[:, 0], axis=0)
    next_state = jnp.sum(behind_weight * everyone[:, 2], axis=0)
    all_ids = device_ids.astype(jnp.float32)
    pair_steps = (all_ids[:, None] - 1.0 - all_ids[None, :])[:, :, None, None]
    pair_weight = jnp.where(
        pair_steps >= 0, jnp.exp(-rate_cols[None, None] * (tokens * jnp.maximum(pair_steps, 0.0))), 0.0
    )
    all_prev = jnp.sum(pair_weight * everyone[None, :, 0], axis=1)
    all_lagged = jnp.sum(
        pair_weight * (everyone[None, :, 1] - tokens * pair_steps * everyone[None, :, 0]), axis=1
    )
    all_first = jnp.exp(-rate_cols)[None] * everyone[:, 2]
    cross_first = jnp.sum(all_first * all_prev, axis=0)
    cross_lag = jnp.sum(all_first * all_lagged - everyone[:, 3] * all_prev, axis=0)
    cross_first = cross_first.reshape(order_count, group_count, members).sum(axis=2).T
    cross_lag = cross_lag.reshape(order_count, group_count, members).sum(axis=2).T
    gathered_parts = gathered[:, state_rows.shape[0] : state_rows.shape[0] + partial_rows.shape[0]].reshape(
        ctx_count, 2, group_count, order_count
    )
    local_totals = jnp.sum(gathered_parts, axis=0)
    first_total = local_totals[0] + cross_first
    lag_total = local_totals[1] + cross_lag

    prev_grouped = prev_state.reshape(order_count, group_count, members)
    next_grouped = next_state.reshape(order_count, group_count, members)
    start_total = start_states + from_first * prev_grouped[None]
    later_total = later_states + from_last * next_grouped[None]
    carried_fwd = jnp.einsum("gnt,bngm->btgm", coef_after, start_total, precision=precise)
    inner_sum = (inside_fwd + carried_fwd).reshape(tokens, group_count, members)
    carried_bwd = jnp.einsum("gns,bngm->bsgm", coef_tail, later_total, precision=precise)
    product_grad = (inside_bwd + carried_bwd).reshape(tokens, group_count, members)
    gain_part = jnp.sqrt(2.0 * decay_rates) * first_total
    rate_part = mode_coefs * (0.5 * first_total + decay_rates * lag_total)
    inner_flat = inner_sum.reshape(tokens, channels)
    mixer_output = (query_part * inner_flat).astype(jnp.bfloat16)
    grad_flat = product_grad.reshape(tokens, channels)
    feature_adj = jnp.stack([cotangent * inner_flat, grad_flat * value_part, grad_flat * key_part])
    filter_local = jnp.stack([gain_part, rate_part])
    entry_count = 2 * group_count * order_count * lax.axis_size("fsdp")
    summed = filter_local
    square_tile = jnp.full((8, 128), jnp.sum(summed * summed), jnp.float32)
    rim_send = feature_adj[:, :rim_rows, :].reshape(3 * rim_rows, channels)
    square_tiles, rim_got = finish_exchange(square_tile, rim_send)
    squares = jnp.sum(square_tiles[:, 0, 0])
    later_rows = jnp.where(ctx_index == ctx_count - 1, 0.0, rim_got).reshape(3, rim_rows, channels)
    appended = jnp.concatenate([feature_adj, later_rows], axis=1)
    feature_grads = short_conv(short_taps, appended, tokens, rim_rows, False).astype(jnp.bfloat16)
    factor = jnp.minimum(1.0, lax.rsqrt(squares / entry_count + 1e-06))
    clipped = summed * factor
    return (mixer_output, feature_grads, clipped[0], clipped[1])


def solution(mesh):
    return jax.shard_map(
        per_device,
        mesh=mesh,
        in_specs=(
            P(None, "ctx", "fsdp"),
            P(None, None, "fsdp"),
            P("fsdp", None),
            P("fsdp", None),
            P("ctx", "fsdp"),
        ),
        out_specs=(P("ctx", "fsdp"), P(None, "ctx", "fsdp"), P("fsdp", None), P("fsdp", None)),
        check_vma=False,
    )
```

```python
import jax
import jax.numpy as jnp
from jax import lax
from jax.experimental import pallas as pl
from jax.experimental.pallas import tpu as pltpu
from jax.sharding import PartitionSpec as P
import functools

MESH = pl.DeviceIdType.MESH

precise = lax.Precision.HIGHEST
threepass = lax.Precision.HIGH


def gather_kernel(axis, count, x_ref, o_ref, held, send_sem, recv_sem):
    me = lax.axis_index(axis)

    def device(peer):
        if axis == "ctx":
            return (lax.axis_index("fsdp"), peer)
        return (peer, lax.axis_index("ctx"))

    barrier = pltpu.get_barrier_semaphore()
    for step in range(1, count):
        pl.semaphore_signal(
            barrier, inc=1, device_id=device(lax.rem(me + step, count)), device_id_type=MESH
        )
    pl.semaphore_wait(barrier, count - 1)
    copies = []
    for step in range(1, count):
        copy = pltpu.make_async_remote_copy(
            src_ref=x_ref,
            dst_ref=held.at[me],
            send_sem=send_sem.at[step - 1],
            recv_sem=recv_sem.at[step - 1],
            device_id=device(lax.rem(me + step, count)),
            device_id_type=MESH,
        )
        copy.start()
        copies.append(copy)
    for copy in copies:
        copy.wait()
    held[me] = x_ref[...]
    o_ref[...] = held[...]


def gather_along(value, axis, collective_id):
    count = lax.axis_size(axis)
    return pl.pallas_call(
        functools.partial(gather_kernel, axis, count),
        out_shape=jax.ShapeDtypeStruct((count,) + value.shape, value.dtype),
        in_specs=[pl.BlockSpec(memory_space=pltpu.VMEM)],
        out_specs=pl.BlockSpec(memory_space=pltpu.VMEM),
        scratch_shapes=[
            pltpu.VMEM((count,) + value.shape, value.dtype),
            pltpu.SemaphoreType.DMA((count - 1,)),
            pltpu.SemaphoreType.DMA((count - 1,)),
        ],
        compiler_params=pltpu.CompilerParams(collective_id=collective_id, has_side_effects=True),
    )(value)


def finish_kernel(
    fsdp_count, ctx_count, tile_ref, rim_ref, cot_ref, inner_ref, grad_ref, value_ref, key_ref,
    taps_ref, tiles_out, grads_out, tiles_held, rim_held, adj_buf,
    send_sem, recv_sem, rim_send_sem, rim_recv_sem,
):
    f_me = lax.axis_index("fsdp")
    c_me = lax.axis_index("ctx")
    left = lax.rem(c_me + ctx_count - 1, ctx_count)
    right = lax.rem(c_me + 1, ctx_count)
    barrier = pltpu.get_barrier_semaphore()
    for step in range(1, fsdp_count):
        peer = (lax.rem(f_me + step, fsdp_count), c_me)
        pl.semaphore_signal(barrier, inc=1, device_id=peer, device_id_type=MESH)
    for side in (left, right):
        pl.semaphore_signal(barrier, inc=1, device_id=(f_me, side), device_id_type=MESH)
    pl.semaphore_wait(barrier, fsdp_count + 1)
    rim_copy = pltpu.make_async_remote_copy(
        src_ref=rim_ref,
        dst_ref=rim_held,
        send_sem=rim_send_sem,
        recv_sem=rim_recv_sem,
        device_id=(f_me, left),
        device_id_type=MESH,
    )
    rim_copy.start()
    copies = []
    for step in range(1, fsdp_count):
        copy = pltpu.make_async_remote_copy(
            src_ref=tile_ref,
            dst_ref=tiles_held.at[f_me],
            send_sem=send_sem.at[step - 1],
            recv_sem=recv_sem.at[step - 1],
            device_id=(lax.rem(f_me + step, fsdp_count), c_me),
            device_id_type=MESH,
        )
        copy.start()
        copies.append(copy)
    tokens = cot_ref.shape[0]
    rim_rows = rim_ref.shape[0] // 3
    shifts = taps_ref.shape[1]
    adj_buf[0, :tokens] = cot_ref[...].astype(jnp.float32) * inner_ref[...]
    adj_buf[1, :tokens] = grad_ref[...] * value_ref[...]
    adj_buf[2, :tokens] = grad_ref[...] * key_ref[...]
    early = tokens - 16

    def conv_rows(start, count):
        for part in range(3):
            total = jnp.zeros((count, adj_buf.shape[2]), jnp.float32)
            for offset in range(shifts):
                total = total + taps_ref[part, offset][None, :] * adj_buf[
                    part, start + offset : start + offset + count
                ]
            grads_out[part, start : start + count] = total.astype(grads_out.dtype)

    conv_rows(0, early)
    for copy in copies:
        copy.wait()
    rim_copy.wait()
    keep = jnp.where(c_me == ctx_count - 1, 0.0, 1.0)
    for part in range(3):
        adj_buf[part, tokens : tokens + rim_rows] = (
            rim_held[part * rim_rows : (part + 1) * rim_rows] * keep
        )
    conv_rows(early, tokens - early)
    tiles_held[f_me] = tile_ref[...]
    tiles_out[...] = tiles_held[...]


def finish_exchange(tile, rim, cot, inner, grad, value, key, taps):
    fsdp_count = lax.axis_size("fsdp")
    ctx_count = lax.axis_size("ctx")
    tokens, channels = cot.shape
    rim_rows = rim.shape[0] // 3
    pad_rows = -(-(tokens + rim_rows) // 8) * 8
    return pl.pallas_call(
        functools.partial(finish_kernel, fsdp_count, ctx_count),
        out_shape=(
            jax.ShapeDtypeStruct((fsdp_count,) + tile.shape, tile.dtype),
            jax.ShapeDtypeStruct((3, tokens, channels), jnp.bfloat16),
        ),
        in_specs=[pl.BlockSpec(memory_space=pltpu.VMEM)] * 8,
        out_specs=(pl.BlockSpec(memory_space=pltpu.VMEM), pl.BlockSpec(memory_space=pltpu.VMEM)),
        scratch_shapes=[
            pltpu.VMEM((fsdp_count,) + tile.shape, tile.dtype),
            pltpu.VMEM(rim.shape, rim.dtype),
            pltpu.VMEM((3, pad_rows, channels), jnp.float32),
            pltpu.SemaphoreType.DMA((fsdp_count - 1,)),
            pltpu.SemaphoreType.DMA((fsdp_count - 1,)),
            pltpu.SemaphoreType.DMA(()),
            pltpu.SemaphoreType.DMA(()),
        ],
        compiler_params=pltpu.CompilerParams(collective_id=1, has_side_effects=True),
    )(tile, rim, cot, inner, grad, value, key, taps)


def passed_along(value, axis, steps):
    count = lax.axis_size(axis)
    leading, last = (max(0, -steps), min(count, count - steps))
    return lax.ppermute(value, axis, [(source, source + steps) for source in range(leading, last)])


def short_conv(taps_table, row_data, tokens, rim_rows, forward):
    summed = jnp.zeros((3, tokens, row_data.shape[2]), jnp.float32)
    for offset in range(taps_table.shape[1]):
        start_row = rim_rows - offset if forward else offset
        summed = (
            summed + taps_table[:, offset, None, :] * row_data[:, start_row : start_row + tokens, :]
        )
    return summed


def per_device(features, short_taps, decay_rates, mode_gains, cotangent):
    tokens = features.shape[1]
    channels = features.shape[2]
    group_count = decay_rates.shape[0]
    order_count = decay_rates.shape[1]
    members = channels // group_count
    rim_rows = short_taps.shape[1] - 1
    block_len = 128
    block_count = tokens // block_len
    ctx_count = lax.axis_size("ctx")
    ctx_index = lax.axis_index("ctx")
    earlier_rows = passed_along(features[:, tokens - rim_rows :, :], "ctx", 1)
    extended = jnp.concatenate([earlier_rows, features], axis=1)
    shaped = short_conv(short_taps, extended, tokens, rim_rows, True)
    query_part, key_part, value_part = (shaped[0], shaped[1], shaped[2])
    product = (key_part * value_part).astype(jnp.bfloat16)
    adjoint = cotangent * query_part
    grouped_z = product.reshape(tokens, group_count, members)
    grouped_e = adjoint.reshape(tokens, group_count, members)
    mode_coefs = mode_gains * jnp.sqrt(2.0 * decay_rates)
    rate_axis = decay_rates[:, :, None]
    lag_axis = jnp.arange(block_len, dtype=jnp.float32)[None, None, :]
    block_pow = jnp.exp(-rate_axis * lag_axis)
    block_after = block_pow * jnp.exp(-rate_axis)
    block_moments = jnp.stack([block_after, (lag_axis + 1.0) * block_after])
    coef_after = mode_coefs[:, :, None] * block_after
    tail_axis = block_len - 1.0 - lag_axis
    tail_pow = jnp.exp(-rate_axis * tail_axis)
    block_ends = jnp.stack([tail_pow, -tail_axis * tail_pow])
    coef_tail = mode_coefs[:, :, None] * jnp.exp(-rate_axis * (tail_axis + 1.0))
    lag_index = (
        jnp.arange(block_len, dtype=jnp.int32)[:, None]
        - jnp.arange(block_len, dtype=jnp.int32)[None, :]
    )
    lag_value = jnp.maximum(lag_index, 0).astype(jnp.float32)
    pair_pow = jnp.exp(-decay_rates[:, :, None, None] * lag_value[None, None])
    toeplitz = jnp.where(
        lag_index[None] >= 0, jnp.sum(mode_coefs[:, :, None, None] * pair_pow, axis=1), 0.0
    )
    z_blocks = grouped_z.reshape(block_count, block_len, group_count, members)
    e_blocks = grouped_e.reshape(block_count, block_len, group_count, members)

    z_wide = z_blocks.astype(jnp.float32)
    block_ids = jnp.arange(block_count, dtype=jnp.float32)
    block_steps = (block_ids[:, None] - 1.0 - block_ids[None, :])[:, :, None, None, None]
    span_weight = jnp.where(
        block_steps >= 0,
        jnp.exp(-decay_rates.T[None, None, :, :, None] * (block_len * jnp.maximum(block_steps, 0.0))),
        0.0,
    )
    inside_fwd = jnp.einsum("gts,bsgm->btgm", toeplitz, z_wide, precision=threepass)
    fresh_fwd = jnp.einsum("kgns,bsgm->kbngm", block_ends, z_wide, precision=threepass)
    start_states = jnp.sum(span_weight * fresh_fwd[0][None], axis=1)
    start_lagged = jnp.sum(
        span_weight * (fresh_fwd[1][None] - block_len * block_steps * fresh_fwd[0][None]), axis=1
    )
    moments = jnp.einsum("kgnt,btgm->kbngm", block_moments, e_blocks, precision=precise)
    first_acc = jnp.sum(moments[0] * start_states, axis=(0, 3))
    lag_acc = jnp.sum(moments[0] * start_lagged - moments[1] * start_states, axis=(0, 3))
    gram_acc = jnp.einsum("btgm,bsgm->gts", e_blocks, z_wide, precision=precise)
    gram_low = jnp.where(lag_index[None] >= 0, gram_acc, 0.0)
    gram_pair = jnp.stack([gram_low, gram_low * lag_value[None]])
    rise_pow = jnp.exp(rate_axis * lag_axis)
    gram_rise = jnp.einsum("kgts,gns->kgnt", gram_pair, rise_pow, precision=precise)
    first_in = jnp.sum(block_pow * gram_rise[0], axis=2)
    lag_in = jnp.sum(block_pow * gram_rise[1], axis=2)
    first_local = first_acc.T + first_in
    lag_local = lag_acc.T - lag_in
    inside_bwd = jnp.einsum("gts,btgm->bsgm", toeplitz, e_blocks, precision=precise)
    fresh_bwd = jnp.einsum("gnt,btgm->bngm", block_pow, e_blocks, precision=precise)
    later_states = jnp.sum(jnp.swapaxes(span_weight, 0, 1) * fresh_bwd[None], axis=1)
    rates_ng = decay_rates.T[None, :, :, None]
    from_first = jnp.exp(-rates_ng * (block_len * block_ids[:, None, None, None]))
    from_last = jnp.exp(-rates_ng * (block_len * (block_count - 1.0 - block_ids[:, None, None, None])))
    end_state = jnp.sum(from_last * fresh_fwd[0], axis=0)
    end_lagged = jnp.sum(
        from_last
        * (fresh_fwd[1] - block_len * (block_count - 1.0 - block_ids[:, None, None, None]) * fresh_fwd[0]),
        axis=0,
    )
    start_state = jnp.sum(from_first * fresh_bwd, axis=0)
    second_moment = jnp.sum(
        from_first * (moments[1] + block_len * block_ids[:, None, None, None] * moments[0]), axis=0
    )
    partial_rows = jnp.stack([first_local, lag_local]).reshape(-1, channels)
    state_rows = jnp.stack([end_state, end_lagged, start_state, second_moment]).reshape(
        4 * order_count, channels
    )
    payload_rows = -(-(state_rows.shape[0] + partial_rows.shape[0]) // 8) * 8
    local_states = jnp.zeros((payload_rows, channels), jnp.float32)
    local_states = local_states.at[: state_rows.shape[0]].set(state_rows)
    local_states = local_states.at[state_rows.shape[0] : state_rows.shape[0] + partial_rows.shape[0]].set(
        partial_rows
    )
    rate_cols = jnp.repeat(decay_rates.T, members, axis=1)
    gathered = gather_along(local_states, "ctx", 0)
    everyone = gathered[:, : state_rows.shape[0]].reshape(ctx_count, 4, order_count, channels)
    device_ids = jnp.arange(ctx_count, dtype=jnp.int32)
    ahead_steps = (ctx_index - 1 - device_ids).astype(jnp.float32)[:, None, None]
    behind_steps = (device_ids - ctx_index - 1).astype(jnp.float32)[:, None, None]
    ahead_weight = jnp.where(
        ahead_steps >= 0, jnp.exp(-rate_cols[None] * (tokens * jnp.maximum(ahead_steps, 0.0))), 0.0
    )
    behind_weight = jnp.where(
        behind_steps >= 0,
        jnp.exp(-rate_cols[None] * (tokens * jnp.maximum(behind_steps, 0.0))),
        0.0,
    )
    prev_state = jnp.sum(ahead_weight * everyone[:, 0], axis=0)
    next_state = jnp.sum(behind_weight * everyone[:, 2], axis=0)
    all_ids = device_ids.astype(jnp.float32)
    pair_steps = (all_ids[:, None] - 1.0 - all_ids[None, :])[:, :, None, None]
    pair_weight = jnp.where(
        pair_steps >= 0, jnp.exp(-rate_cols[None, None] * (tokens * jnp.maximum(pair_steps, 0.0))), 0.0
    )
    all_prev = jnp.sum(pair_weight * everyone[None, :, 0], axis=1)
    all_lagged = jnp.sum(
        pair_weight * (everyone[None, :, 1] - tokens * pair_steps * everyone[None, :, 0]), axis=1
    )
    all_first = jnp.exp(-rate_cols)[None] * everyone[:, 2]
    cross_first = jnp.sum(all_first * all_prev, axis=0)
    cross_lag = jnp.sum(all_first * all_lagged - everyone[:, 3] * all_prev, axis=0)
    cross_first = cross_first.reshape(order_count, group_count, members).sum(axis=2).T
    cross_lag = cross_lag.reshape(order_count, group_count, members).sum(axis=2).T
    gathered_parts = gathered[:, state_rows.shape[0] : state_rows.shape[0] + partial_rows.shape[0]].reshape(
        ctx_count, 2, group_count, order_count
    )
    local_totals = jnp.sum(gathered_parts, axis=0)
    first_total = local_totals[0] + cross_first
    lag_total = local_totals[1] + cross_lag

    prev_grouped = prev_state.reshape(order_count, group_count, members)
    next_grouped = next_state.reshape(order_count, group_count, members)
    start_total = start_states + from_first * prev_grouped[None]
    later_total = later_states + from_last * next_grouped[None]
    carried_fwd = jnp.einsum("gnt,bngm->btgm", coef_after, start_total, precision=precise)
    inner_sum = (inside_fwd + carried_fwd).reshape(tokens, group_count, members)
    carried_bwd = jnp.einsum("gns,bngm->bsgm", coef_tail, later_total, precision=precise)
    product_grad = (inside_bwd + carried_bwd).reshape(tokens, group_count, members)
    gain_part = jnp.sqrt(2.0 * decay_rates) * first_total
    rate_part = mode_coefs * (0.5 * first_total + decay_rates * lag_total)
    inner_flat = inner_sum.reshape(tokens, channels)
    mixer_output = (query_part * inner_flat).astype(jnp.bfloat16)
    grad_flat = product_grad.reshape(tokens, channels)
    rim_adj = jnp.stack(
        [
            cotangent[:rim_rows] * inner_flat[:rim_rows],
            grad_flat[:rim_rows] * value_part[:rim_rows],
            grad_flat[:rim_rows] * key_part[:rim_rows],
        ]
    )
    filter_local = jnp.stack([gain_part, rate_part])
    entry_count = 2 * group_count * order_count * lax.axis_size("fsdp")
    summed = filter_local
    square_tile = jnp.full((8, 128), jnp.sum(summed * summed), jnp.float32)
    rim_send = rim_adj.reshape(3 * rim_rows, channels)
    square_tiles, feature_grads = finish_exchange(
        square_tile, rim_send, cotangent, inner_flat, grad_flat, value_part, key_part, short_taps
    )
    squares = jnp.sum(square_tiles[:, 0, 0])
    factor = jnp.minimum(1.0, lax.rsqrt(squares / entry_count + 1e-06))
    clipped = summed * factor
    return (mixer_output, feature_grads, clipped[0], clipped[1])


def solution(mesh):
    return jax.shard_map(
        per_device,
        mesh=mesh,
        in_specs=(
            P(None, "ctx", "fsdp"),
            P(None, None, "fsdp"),
            P("fsdp", None),
            P("fsdp", None),
            P("ctx", "fsdp"),
        ),
        out_specs=(P("ctx", "fsdp"), P(None, "ctx", "fsdp"), P("fsdp", None), P("fsdp", None)),
        check_vma=False,
    )
```

```python
import jax
import jax.numpy as jnp
from jax import lax
from jax.experimental import pallas as pl
from jax.experimental.pallas import tpu as pltpu
from jax.sharding import PartitionSpec as P
import functools

MESH = pl.DeviceIdType.MESH

precise = lax.Precision.HIGHEST
threepass = lax.Precision.HIGH


def gather_kernel(axis, count, x_ref, o_ref, held, send_sem, recv_sem):
    me = lax.axis_index(axis)

    def device(peer):
        if axis == "ctx":
            return (lax.axis_index("fsdp"), peer)
        return (peer, lax.axis_index("ctx"))

    barrier = pltpu.get_barrier_semaphore()
    for step in range(1, count):
        pl.semaphore_signal(
            barrier, inc=1, device_id=device(lax.rem(me + step, count)), device_id_type=MESH
        )
    pl.semaphore_wait(barrier, count - 1)
    copies = []
    for step in range(1, count):
        copy = pltpu.make_async_remote_copy(
            src_ref=x_ref,
            dst_ref=held.at[me],
            send_sem=send_sem.at[step - 1],
            recv_sem=recv_sem.at[step - 1],
            device_id=device(lax.rem(me + step, count)),
            device_id_type=MESH,
        )
        copy.start()
        copies.append(copy)
    for copy in copies:
        copy.wait()
    held[me] = x_ref[...]
    o_ref[...] = held[...]


def gather_along(value, axis, collective_id):
    count = lax.axis_size(axis)
    return pl.pallas_call(
        functools.partial(gather_kernel, axis, count),
        out_shape=jax.ShapeDtypeStruct((count,) + value.shape, value.dtype),
        in_specs=[pl.BlockSpec(memory_space=pltpu.VMEM)],
        out_specs=pl.BlockSpec(memory_space=pltpu.VMEM),
        scratch_shapes=[
            pltpu.VMEM((count,) + value.shape, value.dtype),
            pltpu.SemaphoreType.DMA((count - 1,)),
            pltpu.SemaphoreType.DMA((count - 1,)),
        ],
        compiler_params=pltpu.CompilerParams(collective_id=collective_id, has_side_effects=True),
    )(value)


def finish_kernel(
    fsdp_count, ctx_count, tile_ref, rim_ref, cot_ref, inner_ref, grad_ref, value_ref, key_ref,
    taps_ref, query_ref, tiles_out, grads_out, mixed_out, tiles_held, rim_held, adj_buf,
    send_sem, recv_sem, rim_send_sem, rim_recv_sem,
):
    f_me = lax.axis_index("fsdp")
    c_me = lax.axis_index("ctx")
    left = lax.rem(c_me + ctx_count - 1, ctx_count)
    right = lax.rem(c_me + 1, ctx_count)
    barrier = pltpu.get_barrier_semaphore()
    for step in range(1, fsdp_count):
        peer = (lax.rem(f_me + step, fsdp_count), c_me)
        pl.semaphore_signal(barrier, inc=1, device_id=peer, device_id_type=MESH)
    for side in (left, right):
        pl.semaphore_signal(barrier, inc=1, device_id=(f_me, side), device_id_type=MESH)
    pl.semaphore_wait(barrier, fsdp_count + 1)
    rim_copy = pltpu.make_async_remote_copy(
        src_ref=rim_ref,
        dst_ref=rim_held,
        send_sem=rim_send_sem,
        recv_sem=rim_recv_sem,
        device_id=(f_me, left),
        device_id_type=MESH,
    )
    rim_copy.start()
    copies = []
    for step in range(1, fsdp_count):
        copy = pltpu.make_async_remote_copy(
            src_ref=tile_ref,
            dst_ref=tiles_held.at[f_me],
            send_sem=send_sem.at[step - 1],
            recv_sem=recv_sem.at[step - 1],
            device_id=(lax.rem(f_me + step, fsdp_count), c_me),
            device_id_type=MESH,
        )
        copy.start()
        copies.append(copy)
    tokens = cot_ref.shape[0]
    rim_rows = rim_ref.shape[0] // 3
    shifts = taps_ref.shape[1]
    mixed_out[...] = (query_ref[...] * inner_ref[...]).astype(mixed_out.dtype)
    adj_buf[0, :tokens] = cot_ref[...].astype(jnp.float32) * inner_ref[...]
    adj_buf[1, :tokens] = grad_ref[...] * value_ref[...]
    adj_buf[2, :tokens] = grad_ref[...] * key_ref[...]
    early = tokens - 16

    def conv_rows(start, count):
        for part in range(3):
            total = jnp.zeros((count, adj_buf.shape[2]), jnp.float32)
            for offset in range(shifts):
                total = total + taps_ref[part, offset][None, :] * adj_buf[
                    part, start + offset : start + offset + count
                ]
            grads_out[part, start : start + count] = total.astype(grads_out.dtype)

    conv_rows(0, early)
    for copy in copies:
        copy.wait()
    rim_copy.wait()
    keep = jnp.where(c_me == ctx_count - 1, 0.0, 1.0)
    for part in range(3):
        adj_buf[part, tokens : tokens + rim_rows] = (
            rim_held[part * rim_rows : (part + 1) * rim_rows] * keep
        )
    conv_rows(early, tokens - early)
    tiles_held[f_me] = tile_ref[...]
    total = tiles_held[0]
    for slot in range(1, fsdp_count):
        total = total + tiles_held[slot]
    tiles_out[...] = total


def finish_exchange(tile, rim, cot, inner, grad, value, key, taps, query):
    fsdp_count = lax.axis_size("fsdp")
    ctx_count = lax.axis_size("ctx")
    tokens, channels = cot.shape
    rim_rows = rim.shape[0] // 3
    pad_rows = -(-(tokens + rim_rows) // 8) * 8
    return pl.pallas_call(
        functools.partial(finish_kernel, fsdp_count, ctx_count),
        out_shape=(
            jax.ShapeDtypeStruct(tile.shape, tile.dtype),
            jax.ShapeDtypeStruct((3, tokens, channels), jnp.bfloat16),
            jax.ShapeDtypeStruct((tokens, channels), jnp.bfloat16),
        ),
        in_specs=[pl.BlockSpec(memory_space=pltpu.VMEM)] * 9,
        out_specs=(pl.BlockSpec(memory_space=pltpu.VMEM),) * 3,
        scratch_shapes=[
            pltpu.VMEM((fsdp_count,) + tile.shape, tile.dtype),
            pltpu.VMEM(rim.shape, rim.dtype),
            pltpu.VMEM((3, pad_rows, channels), jnp.float32),
            pltpu.SemaphoreType.DMA((fsdp_count - 1,)),
            pltpu.SemaphoreType.DMA((fsdp_count - 1,)),
            pltpu.SemaphoreType.DMA(()),
            pltpu.SemaphoreType.DMA(()),
        ],
        compiler_params=pltpu.CompilerParams(collective_id=1, has_side_effects=True),
    )(tile, rim, cot, inner, grad, value, key, taps, query)


def passed_along(value, axis, steps):
    count = lax.axis_size(axis)
    leading, last = (max(0, -steps), min(count, count - steps))
    return lax.ppermute(value, axis, [(source, source + steps) for source in range(leading, last)])


def short_conv(taps_table, row_data, tokens, rim_rows, forward):
    summed = jnp.zeros((3, tokens, row_data.shape[2]), jnp.float32)
    for offset in range(taps_table.shape[1]):
        start_row = rim_rows - offset if forward else offset
        summed = (
            summed + taps_table[:, offset, None, :] * row_data[:, start_row : start_row + tokens, :]
        )
    return summed


def per_device(features, short_taps, decay_rates, mode_gains, cotangent):
    tokens = features.shape[1]
    channels = features.shape[2]
    group_count = decay_rates.shape[0]
    order_count = decay_rates.shape[1]
    members = channels // group_count
    rim_rows = short_taps.shape[1] - 1
    block_len = 128
    block_count = tokens // block_len
    ctx_count = lax.axis_size("ctx")
    ctx_index = lax.axis_index("ctx")
    earlier_rows = passed_along(features[:, tokens - rim_rows :, :], "ctx", 1)
    extended = jnp.concatenate([earlier_rows, features], axis=1)
    shaped = short_conv(short_taps, extended, tokens, rim_rows, True)
    query_part, key_part, value_part = (shaped[0], shaped[1], shaped[2])
    product = (key_part * value_part).astype(jnp.bfloat16)
    adjoint = cotangent * query_part
    grouped_z = product.reshape(tokens, group_count, members)
    grouped_e = adjoint.reshape(tokens, group_count, members)
    mode_coefs = mode_gains * jnp.sqrt(2.0 * decay_rates)
    rate_axis = decay_rates[:, :, None]
    lag_axis = jnp.arange(block_len, dtype=jnp.float32)[None, None, :]
    block_pow = jnp.exp(-rate_axis * lag_axis)
    block_after = block_pow * jnp.exp(-rate_axis)
    block_moments = jnp.stack([block_after, (lag_axis + 1.0) * block_after])
    coef_after = mode_coefs[:, :, None] * block_after
    tail_axis = block_len - 1.0 - lag_axis
    tail_pow = jnp.exp(-rate_axis * tail_axis)
    block_ends = jnp.stack([tail_pow, -tail_axis * tail_pow])
    coef_tail = mode_coefs[:, :, None] * jnp.exp(-rate_axis * (tail_axis + 1.0))
    lag_index = (
        jnp.arange(block_len, dtype=jnp.int32)[:, None]
        - jnp.arange(block_len, dtype=jnp.int32)[None, :]
    )
    lag_value = jnp.maximum(lag_index, 0).astype(jnp.float32)
    pair_pow = jnp.exp(-decay_rates[:, :, None, None] * lag_value[None, None])
    toeplitz = jnp.where(
        lag_index[None] >= 0, jnp.sum(mode_coefs[:, :, None, None] * pair_pow, axis=1), 0.0
    )
    z_blocks = grouped_z.reshape(block_count, block_len, group_count, members)
    e_blocks = grouped_e.reshape(block_count, block_len, group_count, members)

    z_wide = z_blocks.astype(jnp.float32)
    block_ids = jnp.arange(block_count, dtype=jnp.float32)
    block_steps = (block_ids[:, None] - 1.0 - block_ids[None, :])[:, :, None, None, None]
    span_weight = jnp.where(
        block_steps >= 0,
        jnp.exp(-decay_rates.T[None, None, :, :, None] * (block_len * jnp.maximum(block_steps, 0.0))),
        0.0,
    )
    inside_fwd = jnp.einsum("gts,bsgm->btgm", toeplitz, z_wide, precision=threepass)
    fresh_fwd = jnp.einsum("kgns,bsgm->kbngm", block_ends, z_wide, precision=threepass)
    start_states = jnp.sum(span_weight * fresh_fwd[0][None], axis=1)
    start_lagged = jnp.sum(
        span_weight * (fresh_fwd[1][None] - block_len * block_steps * fresh_fwd[0][None]), axis=1
    )
    moments = jnp.einsum("kgnt,btgm->kbngm", block_moments, e_blocks, precision=precise)
    first_acc = jnp.sum(moments[0] * start_states, axis=(0, 3))
    lag_acc = jnp.sum(moments[0] * start_lagged - moments[1] * start_states, axis=(0, 3))
    gram_acc = jnp.einsum("btgm,bsgm->gts", e_blocks, z_wide, precision=precise)
    gram_low = jnp.where(lag_index[None] >= 0, gram_acc, 0.0)
    gram_pair = jnp.stack([gram_low, gram_low * lag_value[None]])
    rise_pow = jnp.exp(rate_axis * lag_axis)
    gram_rise = jnp.einsum("kgts,gns->kgnt", gram_pair, rise_pow, precision=precise)
    first_in = jnp.sum(block_pow * gram_rise[0], axis=2)
    lag_in = jnp.sum(block_pow * gram_rise[1], axis=2)
    first_local = first_acc.T + first_in
    lag_local = lag_acc.T - lag_in
    inside_bwd = jnp.einsum("gts,btgm->bsgm", toeplitz, e_blocks, precision=precise)
    fresh_bwd = jnp.einsum("gnt,btgm->bngm", block_pow, e_blocks, precision=precise)
    later_states = jnp.sum(jnp.swapaxes(span_weight, 0, 1) * fresh_bwd[None], axis=1)
    rates_ng = decay_rates.T[None, :, :, None]
    from_first = jnp.exp(-rates_ng * (block_len * block_ids[:, None, None, None]))
    from_last = jnp.exp(-rates_ng * (block_len * (block_count - 1.0 - block_ids[:, None, None, None])))
    end_state = jnp.sum(from_last * fresh_fwd[0], axis=0)
    end_lagged = jnp.sum(
        from_last
        * (fresh_fwd[1] - block_len * (block_count - 1.0 - block_ids[:, None, None, None]) * fresh_fwd[0]),
        axis=0,
    )
    start_state = jnp.sum(from_first * fresh_bwd, axis=0)
    second_moment = jnp.sum(
        from_first * (moments[1] + block_len * block_ids[:, None, None, None] * moments[0]), axis=0
    )
    partial_rows = jnp.stack([first_local, lag_local]).reshape(-1, channels)
    state_rows = jnp.stack([end_state, end_lagged, start_state, second_moment]).reshape(
        4 * order_count, channels
    )
    payload_rows = -(-(state_rows.shape[0] + partial_rows.shape[0]) // 8) * 8
    local_states = jnp.zeros((payload_rows, channels), jnp.float32)
    local_states = local_states.at[: state_rows.shape[0]].set(state_rows)
    local_states = local_states.at[state_rows.shape[0] : state_rows.shape[0] + partial_rows.shape[0]].set(
        partial_rows
    )
    rate_cols = jnp.repeat(decay_rates.T, members, axis=1)
    gathered = gather_along(local_states, "ctx", 0)
    everyone = gathered[:, : state_rows.shape[0]].reshape(ctx_count, 4, order_count, channels)
    device_ids = jnp.arange(ctx_count, dtype=jnp.int32)
    ahead_steps = (ctx_index - 1 - device_ids).astype(jnp.float32)[:, None, None]
    behind_steps = (device_ids - ctx_index - 1).astype(jnp.float32)[:, None, None]
    ahead_weight = jnp.where(
        ahead_steps >= 0, jnp.exp(-rate_cols[None] * (tokens * jnp.maximum(ahead_steps, 0.0))), 0.0
    )
    behind_weight = jnp.where(
        behind_steps >= 0,
        jnp.exp(-rate_cols[None] * (tokens * jnp.maximum(behind_steps, 0.0))),
        0.0,
    )
    prev_state = jnp.sum(ahead_weight * everyone[:, 0], axis=0)
    next_state = jnp.sum(behind_weight * everyone[:, 2], axis=0)
    all_ids = device_ids.astype(jnp.float32)
    pair_steps = (all_ids[:, None] - 1.0 - all_ids[None, :])[:, :, None, None]
    pair_weight = jnp.where(
        pair_steps >= 0, jnp.exp(-rate_cols[None, None] * (tokens * jnp.maximum(pair_steps, 0.0))), 0.0
    )
    all_prev = jnp.sum(pair_weight * everyone[None, :, 0], axis=1)
    all_lagged = jnp.sum(
        pair_weight * (everyone[None, :, 1] - tokens * pair_steps * everyone[None, :, 0]), axis=1
    )
    all_first = jnp.exp(-rate_cols)[None] * everyone[:, 2]
    cross_first = jnp.sum(all_first * all_prev, axis=0)
    cross_lag = jnp.sum(all_first * all_lagged - everyone[:, 3] * all_prev, axis=0)
    cross_first = cross_first.reshape(order_count, group_count, members).sum(axis=2).T
    cross_lag = cross_lag.reshape(order_count, group_count, members).sum(axis=2).T
    gathered_parts = gathered[:, state_rows.shape[0] : state_rows.shape[0] + partial_rows.shape[0]].reshape(
        ctx_count, 2, group_count, order_count
    )
    local_totals = jnp.sum(gathered_parts, axis=0)
    first_total = local_totals[0] + cross_first
    lag_total = local_totals[1] + cross_lag

    prev_grouped = prev_state.reshape(order_count, group_count, members)
    next_grouped = next_state.reshape(order_count, group_count, members)
    start_total = start_states + from_first * prev_grouped[None]
    later_total = later_states + from_last * next_grouped[None]
    carried_fwd = jnp.einsum("gnt,bngm->btgm", coef_after, start_total, precision=precise)
    inner_sum = (inside_fwd + carried_fwd).reshape(tokens, group_count, members)
    carried_bwd = jnp.einsum("gns,bngm->bsgm", coef_tail, later_total, precision=precise)
    product_grad = (inside_bwd + carried_bwd).reshape(tokens, group_count, members)
    gain_part = jnp.sqrt(2.0 * decay_rates) * first_total
    rate_part = mode_coefs * (0.5 * first_total + decay_rates * lag_total)
    inner_flat = inner_sum.reshape(tokens, channels)
    grad_flat = product_grad.reshape(tokens, channels)
    rim_adj = jnp.stack(
        [
            cotangent[:rim_rows] * inner_flat[:rim_rows],
            grad_flat[:rim_rows] * value_part[:rim_rows],
            grad_flat[:rim_rows] * key_part[:rim_rows],
        ]
    )
    filter_local = jnp.stack([gain_part, rate_part])
    entry_count = 2 * group_count * order_count * lax.axis_size("fsdp")
    summed = filter_local
    square_tile = jnp.full((8, 128), jnp.sum(summed * summed), jnp.float32)
    rim_send = rim_adj.reshape(3 * rim_rows, channels)
    square_total, feature_grads, mixer_output = finish_exchange(
        square_tile, rim_send, cotangent, inner_flat, grad_flat, value_part, key_part, short_taps,
        query_part,
    )
    squares = square_total[0, 0]
    factor = jnp.minimum(1.0, lax.rsqrt(squares / entry_count + 1e-06))
    clipped = summed * factor
    return (mixer_output, feature_grads, clipped[0], clipped[1])


def solution(mesh):
    return jax.shard_map(
        per_device,
        mesh=mesh,
        in_specs=(
            P(None, "ctx", "fsdp"),
            P(None, None, "fsdp"),
            P("fsdp", None),
            P("fsdp", None),
            P("ctx", "fsdp"),
        ),
        out_specs=(P("ctx", "fsdp"), P(None, "ctx", "fsdp"), P("fsdp", None), P("fsdp", None)),
        check_vma=False,
    )
```

```python
import jax
import jax.numpy as jnp
from jax import lax
from jax.experimental import pallas as pl
from jax.experimental.pallas import tpu as pltpu
from jax.sharding import PartitionSpec as P
import functools

MESH = pl.DeviceIdType.MESH

precise = lax.Precision.HIGHEST
threepass = lax.Precision.HIGH


def gather_kernel(axis, count, x_ref, rate_ref, coef_ref, o_ref, toe_ref, held, send_sem, recv_sem):
    me = lax.axis_index(axis)

    def device(peer):
        if axis == "ctx":
            return (lax.axis_index("fsdp"), peer)
        return (peer, lax.axis_index("ctx"))

    barrier = pltpu.get_barrier_semaphore()
    for step in range(1, count):
        pl.semaphore_signal(
            barrier, inc=1, device_id=device(lax.rem(me + step, count)), device_id_type=MESH
        )
    pl.semaphore_wait(barrier, count - 1)
    copies = []
    for step in range(1, count):
        copy = pltpu.make_async_remote_copy(
            src_ref=x_ref,
            dst_ref=held.at[me],
            send_sem=send_sem.at[step - 1],
            recv_sem=recv_sem.at[step - 1],
            device_id=device(lax.rem(me + step, count)),
            device_id_type=MESH,
        )
        copy.start()
        copies.append(copy)
    span = toe_ref.shape[1]
    lag = lax.broadcasted_iota(jnp.int32, (span, span), 0) - lax.broadcasted_iota(
        jnp.int32, (span, span), 1
    )
    lag_value = jnp.maximum(lag, 0).astype(jnp.float32)

    def one_group(group, carry):
        total = jnp.zeros((span, span), jnp.float32)
        for mode in range(rate_ref.shape[1]):
            total = total + coef_ref[group, mode] * jnp.exp(-rate_ref[group, mode] * lag_value)
        toe_ref[group] = jnp.where(lag >= 0, total, 0.0)
        return carry

    lax.fori_loop(0, toe_ref.shape[0], one_group, 0)
    for copy in copies:
        copy.wait()
    held[me] = x_ref[...]
    o_ref[...] = held[...]


def gather_along(value, axis, collective_id, rates, coefs, span):
    count = lax.axis_size(axis)
    return pl.pallas_call(
        functools.partial(gather_kernel, axis, count),
        out_shape=(
            jax.ShapeDtypeStruct((count,) + value.shape, value.dtype),
            jax.ShapeDtypeStruct((rates.shape[0], span, span), jnp.float32),
        ),
        in_specs=[
            pl.BlockSpec(memory_space=pltpu.VMEM),
            pl.BlockSpec(memory_space=pltpu.SMEM),
            pl.BlockSpec(memory_space=pltpu.SMEM),
        ],
        out_specs=(pl.BlockSpec(memory_space=pltpu.VMEM), pl.BlockSpec(memory_space=pltpu.VMEM)),
        scratch_shapes=[
            pltpu.VMEM((count,) + value.shape, value.dtype),
            pltpu.SemaphoreType.DMA((count - 1,)),
            pltpu.SemaphoreType.DMA((count - 1,)),
        ],
        compiler_params=pltpu.CompilerParams(collective_id=collective_id, has_side_effects=True),
    )(value, rates, coefs)


def finish_kernel(
    fsdp_count, ctx_count, tile_ref, rim_ref, cot_ref, inner_ref, grad_ref, value_ref, key_ref,
    taps_ref, tiles_out, grads_out, tiles_held, rim_held, adj_buf,
    send_sem, recv_sem, rim_send_sem, rim_recv_sem,
):
    f_me = lax.axis_index("fsdp")
    c_me = lax.axis_index("ctx")
    left = lax.rem(c_me + ctx_count - 1, ctx_count)
    right = lax.rem(c_me + 1, ctx_count)
    barrier = pltpu.get_barrier_semaphore()
    for step in range(1, fsdp_count):
        peer = (lax.rem(f_me + step, fsdp_count), c_me)
        pl.semaphore_signal(barrier, inc=1, device_id=peer, device_id_type=MESH)
    for side in (left, right):
        pl.semaphore_signal(barrier, inc=1, device_id=(f_me, side), device_id_type=MESH)
    pl.semaphore_wait(barrier, fsdp_count + 1)
    rim_copy = pltpu.make_async_remote_copy(
        src_ref=rim_ref,
        dst_ref=rim_held,
        send_sem=rim_send_sem,
        recv_sem=rim_recv_sem,
        device_id=(f_me, left),
        device_id_type=MESH,
    )
    rim_copy.start()
    copies = []
    for step in range(1, fsdp_count):
        copy = pltpu.make_async_remote_copy(
            src_ref=tile_ref,
            dst_ref=tiles_held.at[f_me],
            send_sem=send_sem.at[step - 1],
            recv_sem=recv_sem.at[step - 1],
            device_id=(lax.rem(f_me + step, fsdp_count), c_me),
            device_id_type=MESH,
        )
        copy.start()
        copies.append(copy)
    tokens = cot_ref.shape[0]
    rim_rows = rim_ref.shape[0] // 3
    shifts = taps_ref.shape[1]
    adj_buf[0, :tokens] = cot_ref[...].astype(jnp.float32) * inner_ref[...]
    adj_buf[1, :tokens] = grad_ref[...] * value_ref[...]
    adj_buf[2, :tokens] = grad_ref[...] * key_ref[...]
    early = tokens - 16

    def conv_rows(start, count):
        for part in range(3):
            total = jnp.zeros((count, adj_buf.shape[2]), jnp.float32)
            for offset in range(shifts):
                total = total + taps_ref[part, offset][None, :] * adj_buf[
                    part, start + offset : start + offset + count
                ]
            grads_out[part, start : start + count] = total.astype(grads_out.dtype)

    conv_rows(0, early)
    for copy in copies:
        copy.wait()
    rim_copy.wait()
    keep = jnp.where(c_me == ctx_count - 1, 0.0, 1.0)
    for part in range(3):
        adj_buf[part, tokens : tokens + rim_rows] = (
            rim_held[part * rim_rows : (part + 1) * rim_rows] * keep
        )
    conv_rows(early, tokens - early)
    tiles_held[f_me] = tile_ref[...]
    tiles_out[...] = tiles_held[...]


def finish_exchange(tile, rim, cot, inner, grad, value, key, taps):
    fsdp_count = lax.axis_size("fsdp")
    ctx_count = lax.axis_size("ctx")
    tokens, channels = cot.shape
    rim_rows = rim.shape[0] // 3
    pad_rows = -(-(tokens + rim_rows) // 8) * 8
    return pl.pallas_call(
        functools.partial(finish_kernel, fsdp_count, ctx_count),
        out_shape=(
            jax.ShapeDtypeStruct((fsdp_count,) + tile.shape, tile.dtype),
            jax.ShapeDtypeStruct((3, tokens, channels), jnp.bfloat16),
        ),
        in_specs=[pl.BlockSpec(memory_space=pltpu.VMEM)] * 8,
        out_specs=(pl.BlockSpec(memory_space=pltpu.VMEM), pl.BlockSpec(memory_space=pltpu.VMEM)),
        scratch_shapes=[
            pltpu.VMEM((fsdp_count,) + tile.shape, tile.dtype),
            pltpu.VMEM(rim.shape, rim.dtype),
            pltpu.VMEM((3, pad_rows, channels), jnp.float32),
            pltpu.SemaphoreType.DMA((fsdp_count - 1,)),
            pltpu.SemaphoreType.DMA((fsdp_count - 1,)),
            pltpu.SemaphoreType.DMA(()),
            pltpu.SemaphoreType.DMA(()),
        ],
        compiler_params=pltpu.CompilerParams(collective_id=1, has_side_effects=True),
    )(tile, rim, cot, inner, grad, value, key, taps)


def passed_along(value, axis, steps):
    count = lax.axis_size(axis)
    leading, last = (max(0, -steps), min(count, count - steps))
    return lax.ppermute(value, axis, [(source, source + steps) for source in range(leading, last)])


def short_conv(taps_table, row_data, tokens, rim_rows, forward):
    summed = jnp.zeros((3, tokens, row_data.shape[2]), jnp.float32)
    for offset in range(taps_table.shape[1]):
        start_row = rim_rows - offset if forward else offset
        summed = (
            summed + taps_table[:, offset, None, :] * row_data[:, start_row : start_row + tokens, :]
        )
    return summed


def per_device(features, short_taps, decay_rates, mode_gains, cotangent):
    tokens = features.shape[1]
    channels = features.shape[2]
    group_count = decay_rates.shape[0]
    order_count = decay_rates.shape[1]
    members = channels // group_count
    rim_rows = short_taps.shape[1] - 1
    block_len = 128
    block_count = tokens // block_len
    ctx_count = lax.axis_size("ctx")
    ctx_index = lax.axis_index("ctx")
    earlier_rows = passed_along(features[:, tokens - rim_rows :, :], "ctx", 1)
    extended = jnp.concatenate([earlier_rows, features], axis=1)
    shaped = short_conv(short_taps, extended, tokens, rim_rows, True)
    query_part, key_part, value_part = (shaped[0], shaped[1], shaped[2])
    product = (key_part * value_part).astype(jnp.bfloat16)
    adjoint = cotangent * query_part
    grouped_z = product.reshape(tokens, group_count, members)
    grouped_e = adjoint.reshape(tokens, group_count, members)
    mode_coefs = mode_gains * jnp.sqrt(2.0 * decay_rates)
    rate_axis = decay_rates[:, :, None]
    lag_axis = jnp.arange(block_len, dtype=jnp.float32)[None, None, :]
    block_pow = jnp.exp(-rate_axis * lag_axis)
    block_after = block_pow * jnp.exp(-rate_axis)
    block_moments = jnp.stack([block_after, (lag_axis + 1.0) * block_after])
    coef_after = mode_coefs[:, :, None] * block_after
    tail_axis = block_len - 1.0 - lag_axis
    tail_pow = jnp.exp(-rate_axis * tail_axis)
    block_ends = jnp.stack([tail_pow, -tail_axis * tail_pow])
    coef_tail = mode_coefs[:, :, None] * jnp.exp(-rate_axis * (tail_axis + 1.0))
    lag_index = (
        jnp.arange(block_len, dtype=jnp.int32)[:, None]
        - jnp.arange(block_len, dtype=jnp.int32)[None, :]
    )
    lag_value = jnp.maximum(lag_index, 0).astype(jnp.float32)
    z_blocks = grouped_z.reshape(block_count, block_len, group_count, members)
    e_blocks = grouped_e.reshape(block_count, block_len, group_count, members)

    z_wide = z_blocks.astype(jnp.float32)
    block_ids = jnp.arange(block_count, dtype=jnp.float32)
    block_steps = (block_ids[:, None] - 1.0 - block_ids[None, :])[:, :, None, None, None]
    span_weight = jnp.where(
        block_steps >= 0,
        jnp.exp(-decay_rates.T[None, None, :, :, None] * (block_len * jnp.maximum(block_steps, 0.0))),
        0.0,
    )
    fresh_fwd = jnp.einsum("kgns,bsgm->kbngm", block_ends, z_wide, precision=threepass)
    start_states = jnp.sum(span_weight * fresh_fwd[0][None], axis=1)
    start_lagged = jnp.sum(
        span_weight * (fresh_fwd[1][None] - block_len * block_steps * fresh_fwd[0][None]), axis=1
    )
    moments = jnp.einsum("kgnt,btgm->kbngm", block_moments, e_blocks, precision=precise)
    first_acc = jnp.sum(moments[0] * start_states, axis=(0, 3))
    lag_acc = jnp.sum(moments[0] * start_lagged - moments[1] * start_states, axis=(0, 3))
    gram_acc = jnp.einsum("btgm,bsgm->gts", e_blocks, z_wide, precision=precise)
    gram_low = jnp.where(lag_index[None] >= 0, gram_acc, 0.0)
    gram_pair = jnp.stack([gram_low, gram_low * lag_value[None]])
    rise_pow = jnp.exp(rate_axis * lag_axis)
    gram_rise = jnp.einsum("kgts,gns->kgnt", gram_pair, rise_pow, precision=precise)
    first_in = jnp.sum(block_pow * gram_rise[0], axis=2)
    lag_in = jnp.sum(block_pow * gram_rise[1], axis=2)
    first_local = first_acc.T + first_in
    lag_local = lag_acc.T - lag_in
    fresh_bwd = jnp.einsum("gnt,btgm->bngm", block_pow, e_blocks, precision=precise)
    later_states = jnp.sum(jnp.swapaxes(span_weight, 0, 1) * fresh_bwd[None], axis=1)
    rates_ng = decay_rates.T[None, :, :, None]
    from_first = jnp.exp(-rates_ng * (block_len * block_ids[:, None, None, None]))
    from_last = jnp.exp(-rates_ng * (block_len * (block_count - 1.0 - block_ids[:, None, None, None])))
    end_state = jnp.sum(from_last * fresh_fwd[0], axis=0)
    end_lagged = jnp.sum(
        from_last
        * (fresh_fwd[1] - block_len * (block_count - 1.0 - block_ids[:, None, None, None]) * fresh_fwd[0]),
        axis=0,
    )
    start_state = jnp.sum(from_first * fresh_bwd, axis=0)
    second_moment = jnp.sum(
        from_first * (moments[1] + block_len * block_ids[:, None, None, None] * moments[0]), axis=0
    )
    partial_rows = jnp.stack([first_local, lag_local]).reshape(-1, channels)
    state_rows = jnp.stack([end_state, end_lagged, start_state, second_moment]).reshape(
        4 * order_count, channels
    )
    payload_rows = -(-(state_rows.shape[0] + partial_rows.shape[0]) // 8) * 8
    local_states = jnp.zeros((payload_rows, channels), jnp.float32)
    local_states = local_states.at[: state_rows.shape[0]].set(state_rows)
    local_states = local_states.at[state_rows.shape[0] : state_rows.shape[0] + partial_rows.shape[0]].set(
        partial_rows
    )
    rate_cols = jnp.repeat(decay_rates.T, members, axis=1)
    gathered, toeplitz = gather_along(local_states, "ctx", 0, decay_rates, mode_coefs, block_len)
    inside_fwd = jnp.einsum("gts,bsgm->btgm", toeplitz, z_wide, precision=threepass)
    inside_bwd = jnp.einsum("gts,btgm->bsgm", toeplitz, e_blocks, precision=precise)
    everyone = gathered[:, : state_rows.shape[0]].reshape(ctx_count, 4, order_count, channels)
    device_ids = jnp.arange(ctx_count, dtype=jnp.int32)
    ahead_steps = (ctx_index - 1 - device_ids).astype(jnp.float32)[:, None, None]
    behind_steps = (device_ids - ctx_index - 1).astype(jnp.float32)[:, None, None]
    ahead_weight = jnp.where(
        ahead_steps >= 0, jnp.exp(-rate_cols[None] * (tokens * jnp.maximum(ahead_steps, 0.0))), 0.0
    )
    behind_weight = jnp.where(
        behind_steps >= 0,
        jnp.exp(-rate_cols[None] * (tokens * jnp.maximum(behind_steps, 0.0))),
        0.0,
    )
    prev_state = jnp.sum(ahead_weight * everyone[:, 0], axis=0)
    next_state = jnp.sum(behind_weight * everyone[:, 2], axis=0)
    all_ids = device_ids.astype(jnp.float32)
    pair_steps = (all_ids[:, None] - 1.0 - all_ids[None, :])[:, :, None, None]
    pair_weight = jnp.where(
        pair_steps >= 0, jnp.exp(-rate_cols[None, None] * (tokens * jnp.maximum(pair_steps, 0.0))), 0.0
    )
    all_prev = jnp.sum(pair_weight * everyone[None, :, 0], axis=1)
    all_lagged = jnp.sum(
        pair_weight * (everyone[None, :, 1] - tokens * pair_steps * everyone[None, :, 0]), axis=1
    )
    all_first = jnp.exp(-rate_cols)[None] * everyone[:, 2]
    cross_first = jnp.sum(all_first * all_prev, axis=0)
    cross_lag = jnp.sum(all_first * all_lagged - everyone[:, 3] * all_prev, axis=0)
    cross_first = cross_first.reshape(order_count, group_count, members).sum(axis=2).T
    cross_lag = cross_lag.reshape(order_count, group_count, members).sum(axis=2).T
    gathered_parts = gathered[:, state_rows.shape[0] : state_rows.shape[0] + partial_rows.shape[0]].reshape(
        ctx_count, 2, group_count, order_count
    )
    local_totals = jnp.sum(gathered_parts, axis=0)
    first_total = local_totals[0] + cross_first
    lag_total = local_totals[1] + cross_lag

    prev_grouped = prev_state.reshape(order_count, group_count, members)
    next_grouped = next_state.reshape(order_count, group_count, members)
    start_total = start_states + from_first * prev_grouped[None]
    later_total = later_states + from_last * next_grouped[None]
    carried_fwd = jnp.einsum("gnt,bngm->btgm", coef_after, start_total, precision=precise)
    inner_sum = (inside_fwd + carried_fwd).reshape(tokens, group_count, members)
    carried_bwd = jnp.einsum("gns,bngm->bsgm", coef_tail, later_total, precision=precise)
    product_grad = (inside_bwd + carried_bwd).reshape(tokens, group_count, members)
    gain_part = jnp.sqrt(2.0 * decay_rates) * first_total
    rate_part = mode_coefs * (0.5 * first_total + decay_rates * lag_total)
    inner_flat = inner_sum.reshape(tokens, channels)
    mixer_output = (query_part * inner_flat).astype(jnp.bfloat16)
    grad_flat = product_grad.reshape(tokens, channels)
    rim_adj = jnp.stack(
        [
            cotangent[:rim_rows] * inner_flat[:rim_rows],
            grad_flat[:rim_rows] * value_part[:rim_rows],
            grad_flat[:rim_rows] * key_part[:rim_rows],
        ]
    )
    filter_local = jnp.stack([gain_part, rate_part])
    entry_count = 2 * group_count * order_count * lax.axis_size("fsdp")
    summed = filter_local
    square_tile = jnp.full((8, 128), jnp.sum(summed * summed), jnp.float32)
    rim_send = rim_adj.reshape(3 * rim_rows, channels)
    square_tiles, feature_grads = finish_exchange(
        square_tile, rim_send, cotangent, inner_flat, grad_flat, value_part, key_part, short_taps
    )
    squares = jnp.sum(square_tiles[:, 0, 0])
    factor = jnp.minimum(1.0, lax.rsqrt(squares / entry_count + 1e-06))
    clipped = summed * factor
    return (mixer_output, feature_grads, clipped[0], clipped[1])


def solution(mesh):
    return jax.shard_map(
        per_device,
        mesh=mesh,
        in_specs=(
            P(None, "ctx", "fsdp"),
            P(None, None, "fsdp"),
            P("fsdp", None),
            P("fsdp", None),
            P("ctx", "fsdp"),
        ),
        out_specs=(P("ctx", "fsdp"), P(None, "ctx", "fsdp"), P("fsdp", None), P("fsdp", None)),
        check_vma=False,
    )
```

```python
import jax
import jax.numpy as jnp
from jax import lax
from jax.experimental import pallas as pl
from jax.experimental.pallas import tpu as pltpu
from jax.sharding import PartitionSpec as P
import functools

MESH = pl.DeviceIdType.MESH

precise = lax.Precision.HIGHEST
threepass = lax.Precision.HIGH


def gather_kernel(
    axis, count, x_ref, rate_ref, coef_ref, fresh_ref, cols_ref, o_ref, toe_ref, later_ref, held,
    send_sem, recv_sem,
):
    me = lax.axis_index(axis)

    def device(peer):
        if axis == "ctx":
            return (lax.axis_index("fsdp"), peer)
        return (peer, lax.axis_index("ctx"))

    barrier = pltpu.get_barrier_semaphore()
    for step in range(1, count):
        pl.semaphore_signal(
            barrier, inc=1, device_id=device(lax.rem(me + step, count)), device_id_type=MESH
        )
    pl.semaphore_wait(barrier, count - 1)
    copies = []
    for step in range(1, count):
        copy = pltpu.make_async_remote_copy(
            src_ref=x_ref,
            dst_ref=held.at[me],
            send_sem=send_sem.at[step - 1],
            recv_sem=recv_sem.at[step - 1],
            device_id=device(lax.rem(me + step, count)),
            device_id_type=MESH,
        )
        copy.start()
        copies.append(copy)
    span = toe_ref.shape[1]
    lag = lax.broadcasted_iota(jnp.int32, (span, span), 0) - lax.broadcasted_iota(
        jnp.int32, (span, span), 1
    )
    lag_value = jnp.maximum(lag, 0).astype(jnp.float32)

    def one_group(group, carry):
        total = jnp.zeros((span, span), jnp.float32)
        for mode in range(rate_ref.shape[1]):
            total = total + coef_ref[group, mode] * jnp.exp(-rate_ref[group, mode] * lag_value)
        toe_ref[group] = jnp.where(lag >= 0, total, 0.0)
        return carry

    lax.fori_loop(0, toe_ref.shape[0], one_group, 0)
    block_count = fresh_ref.shape[0]
    step_pow = [jnp.exp(-cols_ref[...] * (span * float(k))) for k in range(block_count - 1)]
    for block in range(block_count):
        total = jnp.zeros(fresh_ref.shape[1:], jnp.float32)
        for later in range(block + 1, block_count):
            total = total + step_pow[later - block - 1] * fresh_ref[later]
        later_ref[block] = total
    for copy in copies:
        copy.wait()
    held[me] = x_ref[...]
    o_ref[...] = held[...]


def gather_along(value, axis, collective_id, rates, coefs, span, fresh, cols):
    count = lax.axis_size(axis)
    return pl.pallas_call(
        functools.partial(gather_kernel, axis, count),
        out_shape=(
            jax.ShapeDtypeStruct((count,) + value.shape, value.dtype),
            jax.ShapeDtypeStruct((rates.shape[0], span, span), jnp.float32),
            jax.ShapeDtypeStruct(fresh.shape, jnp.float32),
        ),
        in_specs=[
            pl.BlockSpec(memory_space=pltpu.VMEM),
            pl.BlockSpec(memory_space=pltpu.SMEM),
            pl.BlockSpec(memory_space=pltpu.SMEM),
            pl.BlockSpec(memory_space=pltpu.VMEM),
            pl.BlockSpec(memory_space=pltpu.VMEM),
        ],
        out_specs=(pl.BlockSpec(memory_space=pltpu.VMEM),) * 3,
        scratch_shapes=[
            pltpu.VMEM((count,) + value.shape, value.dtype),
            pltpu.SemaphoreType.DMA((count - 1,)),
            pltpu.SemaphoreType.DMA((count - 1,)),
        ],
        compiler_params=pltpu.CompilerParams(collective_id=collective_id, has_side_effects=True),
    )(value, rates, coefs, fresh, cols)


def finish_kernel(
    fsdp_count, ctx_count, tile_ref, rim_ref, cot_ref, inner_ref, grad_ref, value_ref, key_ref,
    taps_ref, tiles_out, grads_out, tiles_held, rim_held, adj_buf,
    send_sem, recv_sem, rim_send_sem, rim_recv_sem,
):
    f_me = lax.axis_index("fsdp")
    c_me = lax.axis_index("ctx")
    left = lax.rem(c_me + ctx_count - 1, ctx_count)
    right = lax.rem(c_me + 1, ctx_count)
    barrier = pltpu.get_barrier_semaphore()
    for step in range(1, fsdp_count):
        peer = (lax.rem(f_me + step, fsdp_count), c_me)
        pl.semaphore_signal(barrier, inc=1, device_id=peer, device_id_type=MESH)
    for side in (left, right):
        pl.semaphore_signal(barrier, inc=1, device_id=(f_me, side), device_id_type=MESH)
    pl.semaphore_wait(barrier, fsdp_count + 1)
    rim_copy = pltpu.make_async_remote_copy(
        src_ref=rim_ref,
        dst_ref=rim_held,
        send_sem=rim_send_sem,
        recv_sem=rim_recv_sem,
        device_id=(f_me, left),
        device_id_type=MESH,
    )
    rim_copy.start()
    copies = []
    for step in range(1, fsdp_count):
        copy = pltpu.make_async_remote_copy(
            src_ref=tile_ref,
            dst_ref=tiles_held.at[f_me],
            send_sem=send_sem.at[step - 1],
            recv_sem=recv_sem.at[step - 1],
            device_id=(lax.rem(f_me + step, fsdp_count), c_me),
            device_id_type=MESH,
        )
        copy.start()
        copies.append(copy)
    tokens = cot_ref.shape[0]
    rim_rows = rim_ref.shape[0] // 3
    shifts = taps_ref.shape[1]
    adj_buf[0, :tokens] = cot_ref[...].astype(jnp.float32) * inner_ref[...]
    adj_buf[1, :tokens] = grad_ref[...] * value_ref[...]
    adj_buf[2, :tokens] = grad_ref[...] * key_ref[...]
    early = tokens - 16

    def conv_rows(start, count):
        for part in range(3):
            total = jnp.zeros((count, adj_buf.shape[2]), jnp.float32)
            for offset in range(shifts):
                total = total + taps_ref[part, offset][None, :] * adj_buf[
                    part, start + offset : start + offset + count
                ]
            grads_out[part, start : start + count] = total.astype(grads_out.dtype)

    conv_rows(0, early)
    for copy in copies:
        copy.wait()
    rim_copy.wait()
    keep = jnp.where(c_me == ctx_count - 1, 0.0, 1.0)
    for part in range(3):
        adj_buf[part, tokens : tokens + rim_rows] = (
            rim_held[part * rim_rows : (part + 1) * rim_rows] * keep
        )
    conv_rows(early, tokens - early)
    tiles_held[f_me] = tile_ref[...]
    tiles_out[...] = tiles_held[...]


def finish_exchange(tile, rim, cot, inner, grad, value, key, taps):
    fsdp_count = lax.axis_size("fsdp")
    ctx_count = lax.axis_size("ctx")
    tokens, channels = cot.shape
    rim_rows = rim.shape[0] // 3
    pad_rows = -(-(tokens + rim_rows) // 8) * 8
    return pl.pallas_call(
        functools.partial(finish_kernel, fsdp_count, ctx_count),
        out_shape=(
            jax.ShapeDtypeStruct((fsdp_count,) + tile.shape, tile.dtype),
            jax.ShapeDtypeStruct((3, tokens, channels), jnp.bfloat16),
        ),
        in_specs=[pl.BlockSpec(memory_space=pltpu.VMEM)] * 8,
        out_specs=(pl.BlockSpec(memory_space=pltpu.VMEM), pl.BlockSpec(memory_space=pltpu.VMEM)),
        scratch_shapes=[
            pltpu.VMEM((fsdp_count,) + tile.shape, tile.dtype),
            pltpu.VMEM(rim.shape, rim.dtype),
            pltpu.VMEM((3, pad_rows, channels), jnp.float32),
            pltpu.SemaphoreType.DMA((fsdp_count - 1,)),
            pltpu.SemaphoreType.DMA((fsdp_count - 1,)),
            pltpu.SemaphoreType.DMA(()),
            pltpu.SemaphoreType.DMA(()),
        ],
        compiler_params=pltpu.CompilerParams(collective_id=1, has_side_effects=True),
    )(tile, rim, cot, inner, grad, value, key, taps)


def passed_along(value, axis, steps):
    count = lax.axis_size(axis)
    leading, last = (max(0, -steps), min(count, count - steps))
    return lax.ppermute(value, axis, [(source, source + steps) for source in range(leading, last)])


def short_conv(taps_table, row_data, tokens, rim_rows, forward):
    summed = jnp.zeros((3, tokens, row_data.shape[2]), jnp.float32)
    for offset in range(taps_table.shape[1]):
        start_row = rim_rows - offset if forward else offset
        summed = (
            summed + taps_table[:, offset, None, :] * row_data[:, start_row : start_row + tokens, :]
        )
    return summed


def per_device(features, short_taps, decay_rates, mode_gains, cotangent):
    tokens = features.shape[1]
    channels = features.shape[2]
    group_count = decay_rates.shape[0]
    order_count = decay_rates.shape[1]
    members = channels // group_count
    rim_rows = short_taps.shape[1] - 1
    block_len = 128
    block_count = tokens // block_len
    ctx_count = lax.axis_size("ctx")
    ctx_index = lax.axis_index("ctx")
    earlier_rows = passed_along(features[:, tokens - rim_rows :, :], "ctx", 1)
    extended = jnp.concatenate([earlier_rows, features], axis=1)
    shaped = short_conv(short_taps, extended, tokens, rim_rows, True)
    query_part, key_part, value_part = (shaped[0], shaped[1], shaped[2])
    product = (key_part * value_part).astype(jnp.bfloat16)
    adjoint = cotangent * query_part
    grouped_z = product.reshape(tokens, group_count, members)
    grouped_e = adjoint.reshape(tokens, group_count, members)
    mode_coefs = mode_gains * jnp.sqrt(2.0 * decay_rates)
    rate_axis = decay_rates[:, :, None]
    lag_axis = jnp.arange(block_len, dtype=jnp.float32)[None, None, :]
    block_pow = jnp.exp(-rate_axis * lag_axis)
    block_after = block_pow * jnp.exp(-rate_axis)
    block_moments = jnp.stack([block_after, (lag_axis + 1.0) * block_after])
    coef_after = mode_coefs[:, :, None] * block_after
    tail_axis = block_len - 1.0 - lag_axis
    tail_pow = jnp.exp(-rate_axis * tail_axis)
    block_ends = jnp.stack([tail_pow, -tail_axis * tail_pow])
    coef_tail = mode_coefs[:, :, None] * jnp.exp(-rate_axis * (tail_axis + 1.0))
    lag_index = (
        jnp.arange(block_len, dtype=jnp.int32)[:, None]
        - jnp.arange(block_len, dtype=jnp.int32)[None, :]
    )
    lag_value = jnp.maximum(lag_index, 0).astype(jnp.float32)
    z_blocks = grouped_z.reshape(block_count, block_len, group_count, members)
    e_blocks = grouped_e.reshape(block_count, block_len, group_count, members)

    z_wide = z_blocks.astype(jnp.float32)
    block_ids = jnp.arange(block_count, dtype=jnp.float32)
    block_steps = (block_ids[:, None] - 1.0 - block_ids[None, :])[:, :, None, None, None]
    span_weight = jnp.where(
        block_steps >= 0,
        jnp.exp(-decay_rates.T[None, None, :, :, None] * (block_len * jnp.maximum(block_steps, 0.0))),
        0.0,
    )
    fresh_fwd = jnp.einsum("kgns,bsgm->kbngm", block_ends, z_wide, precision=threepass)
    start_states = jnp.sum(span_weight * fresh_fwd[0][None], axis=1)
    start_lagged = jnp.sum(
        span_weight * (fresh_fwd[1][None] - block_len * block_steps * fresh_fwd[0][None]), axis=1
    )
    moments = jnp.einsum("kgnt,btgm->kbngm", block_moments, e_blocks, precision=precise)
    first_acc = jnp.sum(moments[0] * start_states, axis=(0, 3))
    lag_acc = jnp.sum(moments[0] * start_lagged - moments[1] * start_states, axis=(0, 3))
    gram_acc = jnp.einsum("btgm,bsgm->gts", e_blocks, z_wide, precision=precise)
    gram_low = jnp.where(lag_index[None] >= 0, gram_acc, 0.0)
    gram_pair = jnp.stack([gram_low, gram_low * lag_value[None]])
    rise_pow = jnp.exp(rate_axis * lag_axis)
    gram_rise = jnp.einsum("kgts,gns->kgnt", gram_pair, rise_pow, precision=precise)
    first_in = jnp.sum(block_pow * gram_rise[0], axis=2)
    lag_in = jnp.sum(block_pow * gram_rise[1], axis=2)
    first_local = first_acc.T + first_in
    lag_local = lag_acc.T - lag_in
    fresh_bwd = jnp.einsum("gnt,btgm->bngm", block_pow, e_blocks, precision=precise)
    rates_ng = decay_rates.T[None, :, :, None]
    from_first = jnp.exp(-rates_ng * (block_len * block_ids[:, None, None, None]))
    from_last = jnp.exp(-rates_ng * (block_len * (block_count - 1.0 - block_ids[:, None, None, None])))
    end_state = jnp.sum(from_last * fresh_fwd[0], axis=0)
    end_lagged = jnp.sum(
        from_last
        * (fresh_fwd[1] - block_len * (block_count - 1.0 - block_ids[:, None, None, None]) * fresh_fwd[0]),
        axis=0,
    )
    start_state = jnp.sum(from_first * fresh_bwd, axis=0)
    second_moment = jnp.sum(
        from_first * (moments[1] + block_len * block_ids[:, None, None, None] * moments[0]), axis=0
    )
    partial_rows = jnp.stack([first_local, lag_local]).reshape(-1, channels)
    state_rows = jnp.stack([end_state, end_lagged, start_state, second_moment]).reshape(
        4 * order_count, channels
    )
    payload_rows = -(-(state_rows.shape[0] + partial_rows.shape[0]) // 8) * 8
    local_states = jnp.zeros((payload_rows, channels), jnp.float32)
    local_states = local_states.at[: state_rows.shape[0]].set(state_rows)
    local_states = local_states.at[state_rows.shape[0] : state_rows.shape[0] + partial_rows.shape[0]].set(
        partial_rows
    )
    rate_cols = jnp.repeat(decay_rates.T, members, axis=1)
    gathered, toeplitz, later_flat = gather_along(
        local_states, "ctx", 0, decay_rates, mode_coefs, block_len,
        fresh_bwd.reshape(block_count, order_count, channels), rate_cols,
    )
    later_states = later_flat.reshape(block_count, order_count, group_count, members)
    inside_fwd = jnp.einsum("gts,bsgm->btgm", toeplitz, z_wide, precision=threepass)
    inside_bwd = jnp.einsum("gts,btgm->bsgm", toeplitz, e_blocks, precision=precise)
    everyone = gathered[:, : state_rows.shape[0]].reshape(ctx_count, 4, order_count, channels)
    device_ids = jnp.arange(ctx_count, dtype=jnp.int32)
    ahead_steps = (ctx_index - 1 - device_ids).astype(jnp.float32)[:, None, None]
    behind_steps = (device_ids - ctx_index - 1).astype(jnp.float32)[:, None, None]
    ahead_weight = jnp.where(
        ahead_steps >= 0, jnp.exp(-rate_cols[None] * (tokens * jnp.maximum(ahead_steps, 0.0))), 0.0
    )
    behind_weight = jnp.where(
        behind_steps >= 0,
        jnp.exp(-rate_cols[None] * (tokens * jnp.maximum(behind_steps, 0.0))),
        0.0,
    )
    prev_state = jnp.sum(ahead_weight * everyone[:, 0], axis=0)
    next_state = jnp.sum(behind_weight * everyone[:, 2], axis=0)
    all_ids = device_ids.astype(jnp.float32)
    pair_steps = (all_ids[:, None] - 1.0 - all_ids[None, :])[:, :, None, None]
    pair_weight = jnp.where(
        pair_steps >= 0, jnp.exp(-rate_cols[None, None] * (tokens * jnp.maximum(pair_steps, 0.0))), 0.0
    )
    all_prev = jnp.sum(pair_weight * everyone[None, :, 0], axis=1)
    all_lagged = jnp.sum(
        pair_weight * (everyone[None, :, 1] - tokens * pair_steps * everyone[None, :, 0]), axis=1
    )
    all_first = jnp.exp(-rate_cols)[None] * everyone[:, 2]
    cross_first = jnp.sum(all_first * all_prev, axis=0)
    cross_lag = jnp.sum(all_first * all_lagged - everyone[:, 3] * all_prev, axis=0)
    cross_first = cross_first.reshape(order_count, group_count, members).sum(axis=2).T
    cross_lag = cross_lag.reshape(order_count, group_count, members).sum(axis=2).T
    gathered_parts = gathered[:, state_rows.shape[0] : state_rows.shape[0] + partial_rows.shape[0]].reshape(
        ctx_count, 2, group_count, order_count
    )
    local_totals = jnp.sum(gathered_parts, axis=0)
    first_total = local_totals[0] + cross_first
    lag_total = local_totals[1] + cross_lag

    prev_grouped = prev_state.reshape(order_count, group_count, members)
    next_grouped = next_state.reshape(order_count, group_count, members)
    start_total = start_states + from_first * prev_grouped[None]
    later_total = later_states + from_last * next_grouped[None]
    carried_fwd = jnp.einsum("gnt,bngm->btgm", coef_after, start_total, precision=precise)
    inner_sum = (inside_fwd + carried_fwd).reshape(tokens, group_count, members)
    carried_bwd = jnp.einsum("gns,bngm->bsgm", coef_tail, later_total, precision=precise)
    product_grad = (inside_bwd + carried_bwd).reshape(tokens, group_count, members)
    gain_part = jnp.sqrt(2.0 * decay_rates) * first_total
    rate_part = mode_coefs * (0.5 * first_total + decay_rates * lag_total)
    inner_flat = inner_sum.reshape(tokens, channels)
    mixer_output = (query_part * inner_flat).astype(jnp.bfloat16)
    grad_flat = product_grad.reshape(tokens, channels)
    rim_adj = jnp.stack(
        [
            cotangent[:rim_rows] * inner_flat[:rim_rows],
            grad_flat[:rim_rows] * value_part[:rim_rows],
            grad_flat[:rim_rows] * key_part[:rim_rows],
        ]
    )
    filter_local = jnp.stack([gain_part, rate_part])
    entry_count = 2 * group_count * order_count * lax.axis_size("fsdp")
    summed = filter_local
    square_tile = jnp.full((8, 128), jnp.sum(summed * summed), jnp.float32)
    rim_send = rim_adj.reshape(3 * rim_rows, channels)
    square_tiles, feature_grads = finish_exchange(
        square_tile, rim_send, cotangent, inner_flat, grad_flat, value_part, key_part, short_taps
    )
    squares = jnp.sum(square_tiles[:, 0, 0])
    factor = jnp.minimum(1.0, lax.rsqrt(squares / entry_count + 1e-06))
    clipped = summed * factor
    return (mixer_output, feature_grads, clipped[0], clipped[1])


def solution(mesh):
    return jax.shard_map(
        per_device,
        mesh=mesh,
        in_specs=(
            P(None, "ctx", "fsdp"),
            P(None, None, "fsdp"),
            P("fsdp", None),
            P("fsdp", None),
            P("ctx", "fsdp"),
        ),
        out_specs=(P("ctx", "fsdp"), P(None, "ctx", "fsdp"), P("fsdp", None), P("fsdp", None)),
        check_vma=False,
    )
```

```python
import jax
import jax.numpy as jnp
from jax import lax
from jax.experimental import pallas as pl
from jax.experimental.pallas import tpu as pltpu
from jax.sharding import PartitionSpec as P
import functools

MESH = pl.DeviceIdType.MESH

precise = lax.Precision.HIGHEST
threepass = lax.Precision.HIGH


def gather_kernel(axis, count, x_ref, rate_ref, coef_ref, o_ref, toe_ref, held, send_sem, recv_sem):
    me = lax.axis_index(axis)

    def device(peer):
        if axis == "ctx":
            return (lax.axis_index("fsdp"), peer)
        return (peer, lax.axis_index("ctx"))

    barrier = pltpu.get_barrier_semaphore()
    for step in range(1, count):
        pl.semaphore_signal(
            barrier, inc=1, device_id=device(lax.rem(me + step, count)), device_id_type=MESH
        )
    pl.semaphore_wait(barrier, count - 1)
    copies = []
    for step in range(1, count):
        copy = pltpu.make_async_remote_copy(
            src_ref=x_ref,
            dst_ref=held.at[me],
            send_sem=send_sem.at[step - 1],
            recv_sem=recv_sem.at[step - 1],
            device_id=device(lax.rem(me + step, count)),
            device_id_type=MESH,
        )
        copy.start()
        copies.append(copy)
    span = toe_ref.shape[1]
    lag = lax.broadcasted_iota(jnp.int32, (span, span), 0) - lax.broadcasted_iota(
        jnp.int32, (span, span), 1
    )
    lag_value = jnp.maximum(lag, 0).astype(jnp.float32)

    def one_group(group, carry):
        total = jnp.zeros((span, span), jnp.float32)
        for mode in range(rate_ref.shape[1]):
            total = total + coef_ref[group, mode] * jnp.exp(-rate_ref[group, mode] * lag_value)
        toe_ref[group] = jnp.where(lag >= 0, total, 0.0)
        return carry

    lax.fori_loop(0, toe_ref.shape[0], one_group, 0)
    for copy in copies:
        copy.wait()
    held[me] = x_ref[...]
    o_ref[...] = held[...]


def gather_along(value, axis, collective_id, rates, coefs, span):
    count = lax.axis_size(axis)
    return pl.pallas_call(
        functools.partial(gather_kernel, axis, count),
        out_shape=(
            jax.ShapeDtypeStruct((count,) + value.shape, value.dtype),
            jax.ShapeDtypeStruct((rates.shape[0], span, span), jnp.float32),
        ),
        in_specs=[
            pl.BlockSpec(memory_space=pltpu.VMEM),
            pl.BlockSpec(memory_space=pltpu.SMEM),
            pl.BlockSpec(memory_space=pltpu.SMEM),
        ],
        out_specs=(pl.BlockSpec(memory_space=pltpu.VMEM), pl.BlockSpec(memory_space=pltpu.VMEM)),
        scratch_shapes=[
            pltpu.VMEM((count,) + value.shape, value.dtype),
            pltpu.SemaphoreType.DMA((count - 1,)),
            pltpu.SemaphoreType.DMA((count - 1,)),
        ],
        compiler_params=pltpu.CompilerParams(collective_id=collective_id, has_side_effects=True),
    )(value, rates, coefs)


def finish_kernel(
    fsdp_count, ctx_count, tile_ref, rim_ref, cot_ref, inner_ref, grad_ref, value_ref, key_ref,
    taps_ref, tiles_out, grads_out, tiles_held, rim_held, adj_buf,
    send_sem, recv_sem, rim_send_sem, rim_recv_sem,
):
    f_me = lax.axis_index("fsdp")
    c_me = lax.axis_index("ctx")
    left = lax.rem(c_me + ctx_count - 1, ctx_count)
    right = lax.rem(c_me + 1, ctx_count)
    barrier = pltpu.get_barrier_semaphore()
    for step in range(1, fsdp_count):
        peer = (lax.rem(f_me + step, fsdp_count), c_me)
        pl.semaphore_signal(barrier, inc=1, device_id=peer, device_id_type=MESH)
    for side in (left, right):
        pl.semaphore_signal(barrier, inc=1, device_id=(f_me, side), device_id_type=MESH)
    pl.semaphore_wait(barrier, fsdp_count + 1)
    rim_copy = pltpu.make_async_remote_copy(
        src_ref=rim_ref,
        dst_ref=rim_held,
        send_sem=rim_send_sem,
        recv_sem=rim_recv_sem,
        device_id=(f_me, left),
        device_id_type=MESH,
    )
    rim_copy.start()
    copies = []
    for step in range(1, fsdp_count):
        copy = pltpu.make_async_remote_copy(
            src_ref=tile_ref,
            dst_ref=tiles_held.at[f_me],
            send_sem=send_sem.at[step - 1],
            recv_sem=recv_sem.at[step - 1],
            device_id=(lax.rem(f_me + step, fsdp_count), c_me),
            device_id_type=MESH,
        )
        copy.start()
        copies.append(copy)
    tokens = cot_ref.shape[0]
    rim_rows = rim_ref.shape[0] // 3
    shifts = taps_ref.shape[1]
    adj_buf[0, :tokens] = cot_ref[...].astype(jnp.float32) * inner_ref[...]
    adj_buf[1, :tokens] = grad_ref[...] * value_ref[...]
    adj_buf[2, :tokens] = grad_ref[...] * key_ref[...]
    early = tokens - 16

    def conv_rows(start, count):
        for part in range(3):
            total = jnp.zeros((count, adj_buf.shape[2]), jnp.float32)
            for offset in range(shifts):
                total = total + taps_ref[part, offset][None, :] * adj_buf[
                    part, start + offset : start + offset + count
                ]
            grads_out[part, start : start + count] = total.astype(grads_out.dtype)

    conv_rows(0, early)
    for copy in copies:
        copy.wait()
    rim_copy.wait()
    keep = jnp.where(c_me == ctx_count - 1, 0.0, 1.0)
    for part in range(3):
        adj_buf[part, tokens : tokens + rim_rows] = (
            rim_held[part * rim_rows : (part + 1) * rim_rows] * keep
        )
    conv_rows(early, tokens - early)
    tiles_held[f_me] = tile_ref[...]
    total = tiles_held[0]
    for slot in range(1, fsdp_count):
        total = total + tiles_held[slot]
    tiles_out[...] = total


def finish_exchange(tile, rim, cot, inner, grad, value, key, taps):
    fsdp_count = lax.axis_size("fsdp")
    ctx_count = lax.axis_size("ctx")
    tokens, channels = cot.shape
    rim_rows = rim.shape[0] // 3
    pad_rows = -(-(tokens + rim_rows) // 8) * 8
    return pl.pallas_call(
        functools.partial(finish_kernel, fsdp_count, ctx_count),
        out_shape=(
            jax.ShapeDtypeStruct(tile.shape, tile.dtype),
            jax.ShapeDtypeStruct((3, tokens, channels), jnp.bfloat16),
        ),
        in_specs=[pl.BlockSpec(memory_space=pltpu.VMEM)] * 8,
        out_specs=(pl.BlockSpec(memory_space=pltpu.VMEM), pl.BlockSpec(memory_space=pltpu.VMEM)),
        scratch_shapes=[
            pltpu.VMEM((fsdp_count,) + tile.shape, tile.dtype),
            pltpu.VMEM(rim.shape, rim.dtype),
            pltpu.VMEM((3, pad_rows, channels), jnp.float32),
            pltpu.SemaphoreType.DMA((fsdp_count - 1,)),
            pltpu.SemaphoreType.DMA((fsdp_count - 1,)),
            pltpu.SemaphoreType.DMA(()),
            pltpu.SemaphoreType.DMA(()),
        ],
        compiler_params=pltpu.CompilerParams(collective_id=1, has_side_effects=True),
    )(tile, rim, cot, inner, grad, value, key, taps)


def passed_along(value, axis, steps):
    count = lax.axis_size(axis)
    leading, last = (max(0, -steps), min(count, count - steps))
    return lax.ppermute(value, axis, [(source, source + steps) for source in range(leading, last)])


def short_conv(taps_table, row_data, tokens, rim_rows, forward):
    summed = jnp.zeros((3, tokens, row_data.shape[2]), jnp.float32)
    for offset in range(taps_table.shape[1]):
        start_row = rim_rows - offset if forward else offset
        summed = (
            summed + taps_table[:, offset, None, :] * row_data[:, start_row : start_row + tokens, :]
        )
    return summed


def per_device(features, short_taps, decay_rates, mode_gains, cotangent):
    tokens = features.shape[1]
    channels = features.shape[2]
    group_count = decay_rates.shape[0]
    order_count = decay_rates.shape[1]
    members = channels // group_count
    rim_rows = short_taps.shape[1] - 1
    block_len = 128
    block_count = tokens // block_len
    ctx_count = lax.axis_size("ctx")
    ctx_index = lax.axis_index("ctx")
    earlier_rows = passed_along(features[:, tokens - rim_rows :, :], "ctx", 1)
    extended = jnp.concatenate([earlier_rows, features], axis=1)
    shaped = short_conv(short_taps, extended, tokens, rim_rows, True)
    query_part, key_part, value_part = (shaped[0], shaped[1], shaped[2])
    product = (key_part * value_part).astype(jnp.bfloat16)
    adjoint = cotangent * query_part
    grouped_z = product.reshape(tokens, group_count, members)
    grouped_e = adjoint.reshape(tokens, group_count, members)
    mode_coefs = mode_gains * jnp.sqrt(2.0 * decay_rates)
    rate_axis = decay_rates[:, :, None]
    lag_axis = jnp.arange(block_len, dtype=jnp.float32)[None, None, :]
    block_pow = jnp.exp(-rate_axis * lag_axis)
    block_after = block_pow * jnp.exp(-rate_axis)
    block_moments = jnp.stack([block_after, (lag_axis + 1.0) * block_after])
    coef_after = mode_coefs[:, :, None] * block_after
    tail_axis = block_len - 1.0 - lag_axis
    tail_pow = jnp.exp(-rate_axis * tail_axis)
    block_ends = jnp.stack([tail_pow, -tail_axis * tail_pow])
    coef_tail = mode_coefs[:, :, None] * jnp.exp(-rate_axis * (tail_axis + 1.0))
    lag_index = (
        jnp.arange(block_len, dtype=jnp.int32)[:, None]
        - jnp.arange(block_len, dtype=jnp.int32)[None, :]
    )
    lag_value = jnp.maximum(lag_index, 0).astype(jnp.float32)
    z_blocks = grouped_z.reshape(block_count, block_len, group_count, members)
    e_blocks = grouped_e.reshape(block_count, block_len, group_count, members)

    z_wide = z_blocks.astype(jnp.float32)
    block_ids = jnp.arange(block_count, dtype=jnp.float32)
    block_steps = (block_ids[:, None] - 1.0 - block_ids[None, :])[:, :, None, None, None]
    span_weight = jnp.where(
        block_steps >= 0,
        jnp.exp(-decay_rates.T[None, None, :, :, None] * (block_len * jnp.maximum(block_steps, 0.0))),
        0.0,
    )
    fresh_fwd = jnp.einsum("kgns,bsgm->kbngm", block_ends, z_wide, precision=threepass)
    start_states = jnp.sum(span_weight * fresh_fwd[0][None], axis=1)
    start_lagged = jnp.sum(
        span_weight * (fresh_fwd[1][None] - block_len * block_steps * fresh_fwd[0][None]), axis=1
    )
    moments = jnp.einsum("kgnt,btgm->kbngm", block_moments, e_blocks, precision=precise)
    first_acc = jnp.sum(moments[0] * start_states, axis=(0, 3))
    lag_acc = jnp.sum(moments[0] * start_lagged - moments[1] * start_states, axis=(0, 3))
    gram_acc = jnp.einsum("btgm,bsgm->gts", e_blocks, z_wide, precision=precise)
    gram_low = jnp.where(lag_index[None] >= 0, gram_acc, 0.0)
    gram_pair = jnp.stack([gram_low, gram_low * lag_value[None]])
    rise_pow = jnp.exp(rate_axis * lag_axis)
    gram_rise = jnp.einsum("kgts,gns->kgnt", gram_pair, rise_pow, precision=precise)
    first_in = jnp.sum(block_pow * gram_rise[0], axis=2)
    lag_in = jnp.sum(block_pow * gram_rise[1], axis=2)
    first_local = first_acc.T + first_in
    lag_local = lag_acc.T - lag_in
    fresh_bwd = jnp.einsum("gnt,btgm->bngm", block_pow, e_blocks, precision=precise)
    later_states = jnp.sum(jnp.swapaxes(span_weight, 0, 1) * fresh_bwd[None], axis=1)
    rates_ng = decay_rates.T[None, :, :, None]
    from_first = jnp.exp(-rates_ng * (block_len * block_ids[:, None, None, None]))
    from_last = jnp.exp(-rates_ng * (block_len * (block_count - 1.0 - block_ids[:, None, None, None])))
    end_state = jnp.sum(from_last * fresh_fwd[0], axis=0)
    end_lagged = jnp.sum(
        from_last
        * (fresh_fwd[1] - block_len * (block_count - 1.0 - block_ids[:, None, None, None]) * fresh_fwd[0]),
        axis=0,
    )
    start_state = jnp.sum(from_first * fresh_bwd, axis=0)
    second_moment = jnp.sum(
        from_first * (moments[1] + block_len * block_ids[:, None, None, None] * moments[0]), axis=0
    )
    partial_rows = jnp.stack([first_local, lag_local]).reshape(-1, channels)
    state_rows = jnp.stack([end_state, end_lagged, start_state, second_moment]).reshape(
        4 * order_count, channels
    )
    payload_rows = -(-(state_rows.shape[0] + partial_rows.shape[0]) // 8) * 8
    local_states = jnp.zeros((payload_rows, channels), jnp.float32)
    local_states = local_states.at[: state_rows.shape[0]].set(state_rows)
    local_states = local_states.at[state_rows.shape[0] : state_rows.shape[0] + partial_rows.shape[0]].set(
        partial_rows
    )
    rate_cols = jnp.repeat(decay_rates.T, members, axis=1)
    gathered, toeplitz = gather_along(local_states, "ctx", 0, decay_rates, mode_coefs, block_len)
    inside_fwd = jnp.einsum("gts,bsgm->btgm", toeplitz, z_wide, precision=threepass)
    inside_bwd = jnp.einsum("gts,btgm->bsgm", toeplitz, e_blocks, precision=precise)
    everyone = gathered[:, : state_rows.shape[0]].reshape(ctx_count, 4, order_count, channels)
    device_ids = jnp.arange(ctx_count, dtype=jnp.int32)
    ahead_steps = (ctx_index - 1 - device_ids).astype(jnp.float32)[:, None, None]
    behind_steps = (device_ids - ctx_index - 1).astype(jnp.float32)[:, None, None]
    ahead_weight = jnp.where(
        ahead_steps >= 0, jnp.exp(-rate_cols[None] * (tokens * jnp.maximum(ahead_steps, 0.0))), 0.0
    )
    behind_weight = jnp.where(
        behind_steps >= 0,
        jnp.exp(-rate_cols[None] * (tokens * jnp.maximum(behind_steps, 0.0))),
        0.0,
    )
    prev_state = jnp.sum(ahead_weight * everyone[:, 0], axis=0)
    next_state = jnp.sum(behind_weight * everyone[:, 2], axis=0)
    all_ids = device_ids.astype(jnp.float32)
    pair_steps = (all_ids[:, None] - 1.0 - all_ids[None, :])[:, :, None, None]
    pair_weight = jnp.where(
        pair_steps >= 0, jnp.exp(-rate_cols[None, None] * (tokens * jnp.maximum(pair_steps, 0.0))), 0.0
    )
    all_prev = jnp.sum(pair_weight * everyone[None, :, 0], axis=1)
    all_lagged = jnp.sum(
        pair_weight * (everyone[None, :, 1] - tokens * pair_steps * everyone[None, :, 0]), axis=1
    )
    all_first = jnp.exp(-rate_cols)[None] * everyone[:, 2]
    cross_first = jnp.sum(all_first * all_prev, axis=0)
    cross_lag = jnp.sum(all_first * all_lagged - everyone[:, 3] * all_prev, axis=0)
    cross_first = cross_first.reshape(order_count, group_count, members).sum(axis=2).T
    cross_lag = cross_lag.reshape(order_count, group_count, members).sum(axis=2).T
    gathered_parts = gathered[:, state_rows.shape[0] : state_rows.shape[0] + partial_rows.shape[0]].reshape(
        ctx_count, 2, group_count, order_count
    )
    local_totals = jnp.sum(gathered_parts, axis=0)
    first_total = local_totals[0] + cross_first
    lag_total = local_totals[1] + cross_lag

    prev_grouped = prev_state.reshape(order_count, group_count, members)
    next_grouped = next_state.reshape(order_count, group_count, members)
    start_total = start_states + from_first * prev_grouped[None]
    later_total = later_states + from_last * next_grouped[None]
    carried_fwd = jnp.einsum("gnt,bngm->btgm", coef_after, start_total, precision=precise)
    inner_sum = (inside_fwd + carried_fwd).reshape(tokens, group_count, members)
    carried_bwd = jnp.einsum("gns,bngm->bsgm", coef_tail, later_total, precision=precise)
    product_grad = (inside_bwd + carried_bwd).reshape(tokens, group_count, members)
    gain_part = jnp.sqrt(2.0 * decay_rates) * first_total
    rate_part = mode_coefs * (0.5 * first_total + decay_rates * lag_total)
    inner_flat = inner_sum.reshape(tokens, channels)
    mixer_output = (query_part * inner_flat).astype(jnp.bfloat16)
    grad_flat = product_grad.reshape(tokens, channels)
    rim_adj = jnp.stack(
        [
            cotangent[:rim_rows] * inner_flat[:rim_rows],
            grad_flat[:rim_rows] * value_part[:rim_rows],
            grad_flat[:rim_rows] * key_part[:rim_rows],
        ]
    )
    filter_local = jnp.stack([gain_part, rate_part])
    entry_count = 2 * group_count * order_count * lax.axis_size("fsdp")
    summed = filter_local
    square_tile = jnp.full((8, 128), jnp.sum(summed * summed), jnp.float32)
    rim_send = rim_adj.reshape(3 * rim_rows, channels)
    square_tiles, feature_grads = finish_exchange(
        square_tile, rim_send, cotangent, inner_flat, grad_flat, value_part, key_part, short_taps
    )
    squares = square_tiles[0, 0]
    factor = jnp.minimum(1.0, lax.rsqrt(squares / entry_count + 1e-06))
    clipped = summed * factor
    return (mixer_output, feature_grads, clipped[0], clipped[1])


def solution(mesh):
    return jax.shard_map(
        per_device,
        mesh=mesh,
        in_specs=(
            P(None, "ctx", "fsdp"),
            P(None, None, "fsdp"),
            P("fsdp", None),
            P("fsdp", None),
            P("ctx", "fsdp"),
        ),
        out_specs=(P("ctx", "fsdp"), P(None, "ctx", "fsdp"), P("fsdp", None), P("fsdp", None)),
        check_vma=False,
    )
```

```python
import jax
import jax.numpy as jnp
from jax import lax
from jax.experimental import pallas as pl
from jax.experimental.pallas import tpu as pltpu
from jax.sharding import PartitionSpec as P
import functools

MESH = pl.DeviceIdType.MESH

precise = lax.Precision.HIGHEST
threepass = lax.Precision.HIGH


def gather_kernel(axis, count, x_ref, rate_ref, coef_ref, o_ref, toe_ref, held, send_sem, recv_sem):
    me = lax.axis_index(axis)

    def device(peer):
        if axis == "ctx":
            return (lax.axis_index("fsdp"), peer)
        return (peer, lax.axis_index("ctx"))

    barrier = pltpu.get_barrier_semaphore()
    for step in range(1, count):
        pl.semaphore_signal(
            barrier, inc=1, device_id=device(lax.rem(me + step, count)), device_id_type=MESH
        )
    pl.semaphore_wait(barrier, count - 1)
    copies = []
    for step in range(1, count):
        copy = pltpu.make_async_remote_copy(
            src_ref=x_ref,
            dst_ref=held.at[me],
            send_sem=send_sem.at[step - 1],
            recv_sem=recv_sem.at[step - 1],
            device_id=device(lax.rem(me + step, count)),
            device_id_type=MESH,
        )
        copy.start()
        copies.append(copy)
    span = toe_ref.shape[1]
    lag = lax.broadcasted_iota(jnp.int32, (span, span), 0) - lax.broadcasted_iota(
        jnp.int32, (span, span), 1
    )
    lag_value = jnp.maximum(lag, 0).astype(jnp.float32)

    def one_group(group, carry):
        total = jnp.zeros((span, span), jnp.float32)
        for mode in range(rate_ref.shape[1]):
            total = total + coef_ref[group, mode] * jnp.exp(-rate_ref[group, mode] * lag_value)
        toe_ref[group] = jnp.where(lag >= 0, total, 0.0)
        return carry

    lax.fori_loop(0, toe_ref.shape[0], one_group, 0)
    for copy in copies:
        copy.wait()
    held[me] = x_ref[...]
    o_ref[...] = held[...]


def gather_along(value, axis, collective_id, rates, coefs, span):
    count = lax.axis_size(axis)
    return pl.pallas_call(
        functools.partial(gather_kernel, axis, count),
        out_shape=(
            jax.ShapeDtypeStruct((count,) + value.shape, value.dtype),
            jax.ShapeDtypeStruct((rates.shape[0], span, span), jnp.float32),
        ),
        in_specs=[
            pl.BlockSpec(memory_space=pltpu.VMEM),
            pl.BlockSpec(memory_space=pltpu.SMEM),
            pl.BlockSpec(memory_space=pltpu.SMEM),
        ],
        out_specs=(pl.BlockSpec(memory_space=pltpu.VMEM), pl.BlockSpec(memory_space=pltpu.VMEM)),
        scratch_shapes=[
            pltpu.VMEM((count,) + value.shape, value.dtype),
            pltpu.SemaphoreType.DMA((count - 1,)),
            pltpu.SemaphoreType.DMA((count - 1,)),
        ],
        compiler_params=pltpu.CompilerParams(collective_id=collective_id, has_side_effects=True),
    )(value, rates, coefs)


def finish_kernel(
    fsdp_count, ctx_count, tile_ref, rim_ref, cot_ref, inner_ref, grad_ref, value_ref, key_ref,
    taps_ref, tiles_out, grads_out, tiles_held, rim_held, adj_buf,
    send_sem, recv_sem, rim_send_sem, rim_recv_sem,
):
    f_me = lax.axis_index("fsdp")
    c_me = lax.axis_index("ctx")
    left = lax.rem(c_me + ctx_count - 1, ctx_count)
    right = lax.rem(c_me + 1, ctx_count)
    barrier = pltpu.get_barrier_semaphore()
    for step in range(1, fsdp_count):
        peer = (lax.rem(f_me + step, fsdp_count), c_me)
        pl.semaphore_signal(barrier, inc=1, device_id=peer, device_id_type=MESH)
    for side in (left, right):
        pl.semaphore_signal(barrier, inc=1, device_id=(f_me, side), device_id_type=MESH)
    pl.semaphore_wait(barrier, fsdp_count + 1)
    rim_copy = pltpu.make_async_remote_copy(
        src_ref=rim_ref,
        dst_ref=rim_held,
        send_sem=rim_send_sem,
        recv_sem=rim_recv_sem,
        device_id=(f_me, left),
        device_id_type=MESH,
    )
    rim_copy.start()
    copies = []
    for step in range(1, fsdp_count):
        copy = pltpu.make_async_remote_copy(
            src_ref=tile_ref,
            dst_ref=tiles_held.at[f_me],
            send_sem=send_sem.at[step - 1],
            recv_sem=recv_sem.at[step - 1],
            device_id=(lax.rem(f_me + step, fsdp_count), c_me),
            device_id_type=MESH,
        )
        copy.start()
        copies.append(copy)
    tokens = cot_ref.shape[0]
    rim_rows = rim_ref.shape[0] // 3
    shifts = taps_ref.shape[1]
    adj_buf[0, :tokens] = cot_ref[...].astype(jnp.float32) * inner_ref[...]
    adj_buf[1, :tokens] = grad_ref[...] * value_ref[...]
    adj_buf[2, :tokens] = grad_ref[...] * key_ref[...]
    early = tokens - 16

    def conv_rows(start, count):
        for part in range(3):
            total = jnp.zeros((count, adj_buf.shape[2]), jnp.float32)
            for offset in range(shifts):
                total = total + taps_ref[part, offset][None, :] * adj_buf[
                    part, start + offset : start + offset + count
                ]
            grads_out[part, start : start + count] = total.astype(grads_out.dtype)

    conv_rows(0, early)
    for copy in copies:
        copy.wait()
    rim_copy.wait()
    keep = jnp.where(c_me == ctx_count - 1, 0.0, 1.0)
    for part in range(3):
        adj_buf[part, tokens : tokens + rim_rows] = (
            rim_held[part * rim_rows : (part + 1) * rim_rows] * keep
        )
    conv_rows(early, tokens - early)
    tiles_held[f_me] = tile_ref[...]
    total = tiles_held[0]
    for slot in range(1, fsdp_count):
        total = total + tiles_held[slot]
    tiles_out[...] = total


def finish_exchange(tile, rim, cot, inner, grad, value, key, taps):
    fsdp_count = lax.axis_size("fsdp")
    ctx_count = lax.axis_size("ctx")
    tokens, channels = cot.shape
    rim_rows = rim.shape[0] // 3
    pad_rows = -(-(tokens + rim_rows) // 8) * 8
    return pl.pallas_call(
        functools.partial(finish_kernel, fsdp_count, ctx_count),
        out_shape=(
            jax.ShapeDtypeStruct(tile.shape, tile.dtype),
            jax.ShapeDtypeStruct((3, tokens, channels), jnp.bfloat16),
        ),
        in_specs=[pl.BlockSpec(memory_space=pltpu.VMEM)] * 8,
        out_specs=(pl.BlockSpec(memory_space=pltpu.VMEM), pl.BlockSpec(memory_space=pltpu.VMEM)),
        scratch_shapes=[
            pltpu.VMEM((fsdp_count,) + tile.shape, tile.dtype),
            pltpu.VMEM(rim.shape, rim.dtype),
            pltpu.VMEM((3, pad_rows, channels), jnp.float32),
            pltpu.SemaphoreType.DMA((fsdp_count - 1,)),
            pltpu.SemaphoreType.DMA((fsdp_count - 1,)),
            pltpu.SemaphoreType.DMA(()),
            pltpu.SemaphoreType.DMA(()),
        ],
        compiler_params=pltpu.CompilerParams(collective_id=1, has_side_effects=True),
    )(tile, rim, cot, inner, grad, value, key, taps)


def passed_along(value, axis, steps):
    count = lax.axis_size(axis)
    leading, last = (max(0, -steps), min(count, count - steps))
    return lax.ppermute(value, axis, [(source, source + steps) for source in range(leading, last)])


def short_conv(taps_table, row_data, tokens, rim_rows, forward):
    summed = jnp.zeros((3, tokens, row_data.shape[2]), jnp.float32)
    for offset in range(taps_table.shape[1]):
        start_row = rim_rows - offset if forward else offset
        summed = (
            summed + taps_table[:, offset, None, :] * row_data[:, start_row : start_row + tokens, :]
        )
    return summed


def per_device(features, short_taps, decay_rates, mode_gains, cotangent):
    tokens = features.shape[1]
    channels = features.shape[2]
    group_count = decay_rates.shape[0]
    order_count = decay_rates.shape[1]
    members = channels // group_count
    rim_rows = short_taps.shape[1] - 1
    block_len = 128
    block_count = tokens // block_len
    ctx_count = lax.axis_size("ctx")
    ctx_index = lax.axis_index("ctx")
    earlier_rows = passed_along(features[:, tokens - rim_rows :, :], "ctx", 1)
    extended = jnp.concatenate([earlier_rows, features], axis=1)
    shaped = short_conv(short_taps, extended, tokens, rim_rows, True)
    query_part, key_part, value_part = (shaped[0], shaped[1], shaped[2])
    product = (key_part * value_part).astype(jnp.bfloat16)
    adjoint = cotangent * query_part
    grouped_z = product.reshape(tokens, group_count, members)
    grouped_e = adjoint.reshape(tokens, group_count, members)
    mode_coefs = mode_gains * jnp.sqrt(2.0 * decay_rates)
    rate_axis = decay_rates[:, :, None]
    lag_axis = jnp.arange(block_len, dtype=jnp.float32)[None, None, :]
    block_pow = jnp.exp(-rate_axis * lag_axis)
    block_after = block_pow * jnp.exp(-rate_axis)
    block_moments = jnp.stack([block_after, (lag_axis + 1.0) * block_after])
    coef_after = mode_coefs[:, :, None] * block_after
    tail_axis = block_len - 1.0 - lag_axis
    tail_pow = jnp.exp(-rate_axis * tail_axis)
    block_ends = jnp.stack([tail_pow, -tail_axis * tail_pow])
    coef_tail = mode_coefs[:, :, None] * jnp.exp(-rate_axis * (tail_axis + 1.0))
    lag_index = (
        jnp.arange(block_len, dtype=jnp.int32)[:, None]
        - jnp.arange(block_len, dtype=jnp.int32)[None, :]
    )
    lag_value = jnp.maximum(lag_index, 0).astype(jnp.float32)
    z_blocks = grouped_z.reshape(block_count, block_len, group_count, members)
    e_blocks = grouped_e.reshape(block_count, block_len, group_count, members)

    z_wide = z_blocks.astype(jnp.float32)
    block_ids = jnp.arange(block_count, dtype=jnp.float32)
    block_steps = (block_ids[:, None] - 1.0 - block_ids[None, :])[:, :, None, None, None]
    span_weight = jnp.where(
        block_steps >= 0,
        jnp.exp(-decay_rates.T[None, None, :, :, None] * (block_len * jnp.maximum(block_steps, 0.0))),
        0.0,
    )
    fresh_fwd = jnp.einsum("kgns,bsgm->kbngm", block_ends, z_wide, precision=threepass)
    start_states = jnp.sum(span_weight * fresh_fwd[0][None], axis=1)
    start_lagged = jnp.sum(
        span_weight * (fresh_fwd[1][None] - block_len * block_steps * fresh_fwd[0][None]), axis=1
    )
    moments = jnp.einsum("kgnt,btgm->kbngm", block_moments, e_blocks, precision=precise)
    first_acc = jnp.sum(moments[0] * start_states, axis=(0, 3))
    lag_acc = jnp.sum(moments[0] * start_lagged - moments[1] * start_states, axis=(0, 3))
    gram_acc = jnp.einsum("btgm,bsgm->gts", e_blocks, z_wide, precision=precise)
    gram_low = jnp.where(lag_index[None] >= 0, gram_acc, 0.0)
    gram_pair = jnp.stack([gram_low, gram_low * lag_value[None]])
    rise_pow = jnp.exp(rate_axis * lag_axis)
    gram_rise = jnp.einsum("kgts,gns->kgnt", gram_pair, rise_pow, precision=precise)
    first_in = jnp.sum(block_pow * gram_rise[0], axis=2)
    lag_in = jnp.sum(block_pow * gram_rise[1], axis=2)
    first_local = first_acc.T + first_in
    lag_local = lag_acc.T - lag_in
    fresh_bwd = jnp.einsum("gnt,btgm->bngm", block_pow, e_blocks, precision=precise)
    later_states = jnp.sum(jnp.swapaxes(span_weight, 0, 1) * fresh_bwd[None], axis=1)
    rates_ng = decay_rates.T[None, :, :, None]
    from_first = jnp.exp(-rates_ng * (block_len * block_ids[:, None, None, None]))
    from_last = jnp.exp(-rates_ng * (block_len * (block_count - 1.0 - block_ids[:, None, None, None])))
    end_state = jnp.sum(from_last * fresh_fwd[0], axis=0)
    end_lagged = jnp.sum(
        from_last
        * (fresh_fwd[1] - block_len * (block_count - 1.0 - block_ids[:, None, None, None]) * fresh_fwd[0]),
        axis=0,
    )
    start_state = jnp.sum(from_first * fresh_bwd, axis=0)
    second_moment = jnp.sum(
        from_first * (moments[1] + block_len * block_ids[:, None, None, None] * moments[0]), axis=0
    )
    partial_rows = jnp.stack([first_local, lag_local]).reshape(-1, channels)
    state_rows = jnp.stack([end_state, end_lagged, start_state, second_moment]).reshape(
        4 * order_count, channels
    )
    payload_rows = state_rows.shape[0] + partial_rows.shape[0]
    local_states = jnp.zeros((payload_rows, channels), jnp.float32)
    local_states = local_states.at[: state_rows.shape[0]].set(state_rows)
    local_states = local_states.at[state_rows.shape[0] : state_rows.shape[0] + partial_rows.shape[0]].set(
        partial_rows
    )
    rate_cols = jnp.repeat(decay_rates.T, members, axis=1)
    gathered, toeplitz = gather_along(local_states, "ctx", 0, decay_rates, mode_coefs, block_len)
    inside_fwd = jnp.einsum("gts,bsgm->btgm", toeplitz, z_wide, precision=threepass)
    inside_bwd = jnp.einsum("gts,btgm->bsgm", toeplitz, e_blocks, precision=precise)
    everyone = gathered[:, : state_rows.shape[0]].reshape(ctx_count, 4, order_count, channels)
    device_ids = jnp.arange(ctx_count, dtype=jnp.int32)
    ahead_steps = (ctx_index - 1 - device_ids).astype(jnp.float32)[:, None, None]
    behind_steps = (device_ids - ctx_index - 1).astype(jnp.float32)[:, None, None]
    ahead_weight = jnp.where(
        ahead_steps >= 0, jnp.exp(-rate_cols[None] * (tokens * jnp.maximum(ahead_steps, 0.0))), 0.0
    )
    behind_weight = jnp.where(
        behind_steps >= 0,
        jnp.exp(-rate_cols[None] * (tokens * jnp.maximum(behind_steps, 0.0))),
        0.0,
    )
    prev_state = jnp.sum(ahead_weight * everyone[:, 0], axis=0)
    next_state = jnp.sum(behind_weight * everyone[:, 2], axis=0)
    all_ids = device_ids.astype(jnp.float32)
    pair_steps = (all_ids[:, None] - 1.0 - all_ids[None, :])[:, :, None, None]
    pair_weight = jnp.where(
        pair_steps >= 0, jnp.exp(-rate_cols[None, None] * (tokens * jnp.maximum(pair_steps, 0.0))), 0.0
    )
    all_prev = jnp.sum(pair_weight * everyone[None, :, 0], axis=1)
    all_lagged = jnp.sum(
        pair_weight * (everyone[None, :, 1] - tokens * pair_steps * everyone[None, :, 0]), axis=1
    )
    all_first = jnp.exp(-rate_cols)[None] * everyone[:, 2]
    cross_first = jnp.sum(all_first * all_prev, axis=0)
    cross_lag = jnp.sum(all_first * all_lagged - everyone[:, 3] * all_prev, axis=0)
    cross_first = cross_first.reshape(order_count, group_count, members).sum(axis=2).T
    cross_lag = cross_lag.reshape(order_count, group_count, members).sum(axis=2).T
    gathered_parts = gathered[:, state_rows.shape[0] : state_rows.shape[0] + partial_rows.shape[0]].reshape(
        ctx_count, 2, group_count, order_count
    )
    local_totals = jnp.sum(gathered_parts, axis=0)
    first_total = local_totals[0] + cross_first
    lag_total = local_totals[1] + cross_lag

    prev_grouped = prev_state.reshape(order_count, group_count, members)
    next_grouped = next_state.reshape(order_count, group_count, members)
    start_total = start_states + from_first * prev_grouped[None]
    later_total = later_states + from_last * next_grouped[None]
    carried_fwd = jnp.einsum("gnt,bngm->btgm", coef_after, start_total, precision=precise)
    inner_sum = (inside_fwd + carried_fwd).reshape(tokens, group_count, members)
    carried_bwd = jnp.einsum("gns,bngm->bsgm", coef_tail, later_total, precision=precise)
    product_grad = (inside_bwd + carried_bwd).reshape(tokens, group_count, members)
    gain_part = jnp.sqrt(2.0 * decay_rates) * first_total
    rate_part = mode_coefs * (0.5 * first_total + decay_rates * lag_total)
    inner_flat = inner_sum.reshape(tokens, channels)
    mixer_output = (query_part * inner_flat).astype(jnp.bfloat16)
    grad_flat = product_grad.reshape(tokens, channels)
    rim_adj = jnp.stack(
        [
            cotangent[:rim_rows] * inner_flat[:rim_rows],
            grad_flat[:rim_rows] * value_part[:rim_rows],
            grad_flat[:rim_rows] * key_part[:rim_rows],
        ]
    )
    filter_local = jnp.stack([gain_part, rate_part])
    entry_count = 2 * group_count * order_count * lax.axis_size("fsdp")
    summed = filter_local
    square_tile = jnp.full((8, 128), jnp.sum(summed * summed), jnp.float32)
    rim_send = rim_adj.reshape(3 * rim_rows, channels)
    square_tiles, feature_grads = finish_exchange(
        square_tile, rim_send, cotangent, inner_flat, grad_flat, value_part, key_part, short_taps
    )
    squares = square_tiles[0, 0]
    factor = jnp.minimum(1.0, lax.rsqrt(squares / entry_count + 1e-06))
    clipped = summed * factor
    return (mixer_output, feature_grads, clipped[0], clipped[1])


def solution(mesh):
    return jax.shard_map(
        per_device,
        mesh=mesh,
        in_specs=(
            P(None, "ctx", "fsdp"),
            P(None, None, "fsdp"),
            P("fsdp", None),
            P("fsdp", None),
            P("ctx", "fsdp"),
        ),
        out_specs=(P("ctx", "fsdp"), P(None, "ctx", "fsdp"), P("fsdp", None), P("fsdp", None)),
        check_vma=False,
    )
```
